32 devices in a mesh: wide: 16 (over z, x, core), narrow: 2 (over y).
Axes of the slice: x: 2, y: 2, z: 4, core: 2. Of those that a mesh axis runs over, the one named last changes fastest.
Arguments:
- plots: bfloat16 [32, 1024, 768], P('wide', 'narrow'), may hold values from -6 to 6
- plot_grid: int32 [32, 2], P('wide'), may hold values from 2 to 512, as said below
- query_weight: bfloat16 [768, 768], P('wide'), may hold values from -0.109375 to 0.109375
- key_weight: bfloat16 [768, 768], P('wide'), may hold values from -0.109375 to 0.109375
- value_weight: bfloat16 [768, 768], P('wide'), may hold values from -0.21875 to 0.21875
- out_weight: bfloat16 [768, 768], P('wide'), may hold values from -0.625 to 0.625
- gate_weight: bfloat16 [768, 2048], P('wide'), may hold values from -0.21875 to 0.21875
- up_weight: bfloat16 [768, 2048], P('wide'), may hold values from -0.21875 to 0.21875
- down_weight: bfloat16 [2048, 768], P('wide'), may hold values from -0.125 to 0.125
- gain_attn: bfloat16 [768], P('wide'), may hold values from 0.5 to 1.5
- gain_mlp: bfloat16 [768], P('wide'), may hold values from 0.5 to 1.5
- cotangent: bfloat16 [32, 1024, 768], P('wide', 'narrow'), may hold values from -6 to 6
Outputs:
- block_out: bfloat16 [32, 1024, 768], P('wide', 'narrow')
- grad_plots: bfloat16 [32, 1024, 768], P('wide', 'narrow')
- grad_query: float32 [768, 768], P('wide')
- grad_key: float32 [768, 768], P('wide')
- grad_value: float32 [768, 768], P('wide')
- grad_out: float32 [768, 768], P('wide')
- grad_gate: float32 [768, 2048], P('wide')
- grad_up: float32 [768, 2048], P('wide')
- grad_down: float32 [2048, 768], P('wide')
- grad_gain_attn: float32 [768], P('wide')
- grad_gain_mlp: float32 [768], P('wide')
The draws below stay inside these ranges and needn't reach their ends.
Inputs may be any that keep to these rules, and one draw needn't show every extreme that they name: `plot_grid`: rows times columns of every plot is at most 1024 and equals it for some plot; rows are 2 to 32.
All inputs are finite; a program needn't handle non-finite values.
Results may differ from the reference program's by a relative error of at most 0.023.
Values may be sent and summed in bfloat16 or wider, within the bound.
A program may use at most 192 MiB of HBM per device.

```python
import jax
import jax.numpy as jnp
from jax import lax

D = 768
HEADS = 12
HEAD_DIM = 64
FF = 2048
SLOTS = 1024
PLOTS = 32


def draw_plot_grid(key, part):
    key_rows = jax.random.fold_in(key, 11)
    key_cols = jax.random.fold_in(key, 12)
    key_full = jax.random.fold_in(key, 13)
    grid_rows = jax.random.randint(key_rows, (PLOTS,), 2, 33)
    chosen = jax.random.randint(key_full, (), 0, PLOTS)
    grid_rows = jnp.where(jnp.arange(PLOTS) == chosen, 2, grid_rows)
    cols_most = SLOTS // grid_rows
    cols_least = jnp.maximum((cols_most + 1) // 2, 2)
    grid_cols = jax.random.randint(key_cols, (PLOTS,), cols_least, cols_most + 1)
    grid_cols = jnp.where(jnp.arange(PLOTS) == chosen, SLOTS // 2, grid_cols)
    return jnp.stack([grid_rows, grid_cols], axis=1).astype(jnp.int32)


def shard_levels(key, shape, shards, low, largest):
    def one(position, blocks):
        draws = jax.random.uniform(jax.random.fold_in(jax.random.fold_in(key, 6), position), (blocks,), jnp.float32, low / len(shards), largest / len(shards))
        return jnp.repeat(jnp.exp(draws), shape[position] // blocks).reshape((-1,) + (1,) * (len(shape) - position - 1))

    loudness = one(*shards[0])
    for cut in shards[1:]:
        loudness = loudness * one(*cut)
    return loudness


def scatter_about(own_key, dims, scale, most, cuts=(), held_as=jnp.bfloat16):
    values = jax.random.normal(own_key, dims, jnp.float32) * scale
    if len(cuts) > 0:
        values = shard_levels(own_key, dims, cuts, -0.22, 0.18) * values
    return jnp.clip(values, min=-most, max=most).astype(held_as)


def setup_inputs(seed: int = 0) -> dict:
    key_of = jax.random.split(jax.random.key(seed), 13)
    plots = scatter_about(key_of[0], (PLOTS, SLOTS, D), 1.0, 6.0, ((0, 16), (1, 2)))
    plot_grid = draw_plot_grid(jax.random.fold_in(key_of[12], 71), 0)
    query_weight = scatter_about(key_of[2], (D, D), (4 * D) ** -0.5, 0.109375, ((0, 16),))
    key_weight = scatter_about(key_of[3], (D, D), (4 * D) ** -0.5, 0.109375, ((0, 16),))
    value_weight = scatter_about(key_of[4], (D, D), D ** -0.5, 0.21875, ((0, 16),))
    out_weight = scatter_about(key_of[5], (D, D), (D // 8) ** -0.5, 0.625, ((0, 16),))
    gate_weight = scatter_about(key_of[6], (D, FF), D ** -0.5, 0.21875, ((0, 16),))
    up_weight = scatter_about(key_of[7], (D, FF), D ** -0.5, 0.21875, ((0, 16),))
    down_weight = scatter_about(key_of[8], (FF, D), FF ** -0.5, 0.125, ((0, 16),))
    gain_attn = jnp.clip(1.0 + 0.1 * jax.random.normal(key_of[9], (D,), jnp.float32), 0.5, 1.5).astype(jnp.bfloat16)
    gain_mlp = jnp.clip(1.0 + 0.1 * jax.random.normal(key_of[10], (D,), jnp.float32), 0.5, 1.5).astype(jnp.bfloat16)
    cotangent = scatter_about(key_of[11], (PLOTS, SLOTS, D), 1.0, 6.0, ((0, 16), (1, 2)))
    return dict(plots=plots, plot_grid=plot_grid, query_weight=query_weight, key_weight=key_weight, value_weight=value_weight, out_weight=out_weight, gate_weight=gate_weight, up_weight=up_weight, down_weight=down_weight, gain_attn=gain_attn, gain_mlp=gain_mlp, cotangent=cotangent)


@jax.custom_vjp
def low(v):
    return lax.optimization_barrier(v.astype(jnp.bfloat16)).astype(jnp.float32)

@jax.custom_vjp
def low_back(v):
    return v

def low_keep(v):
    return (low(v), None)

def low_pass(kept, grad):
    return (grad,)

def back_keep(v):
    return (v, None)

def back_low(kept, grad):
    return (low(grad),)
low.defvjp(low_keep, low_pass)
low_back.defvjp(back_keep, back_low)
highest = lax.Precision.HIGHEST
epsilon = 1e-06

def product(left, right):
    return jnp.matmul(left, right, precision=highest)

def rms_norm(values, gain):
    return values * lax.rsqrt(lax.optimization_barrier(jnp.mean(values * values, axis=-1, keepdims=True)) + epsilon) * gain

def attend_plot(operands):
    query, keys, values, count = operands
    length = query.shape[0]
    query_heads = query.reshape(length, HEADS, HEAD_DIM)
    key_heads = keys.reshape(length, HEADS, HEAD_DIM)
    value_heads = values.reshape(length, HEADS, HEAD_DIM)
    scores = jnp.einsum('qhe,khe->hqk', query_heads, key_heads, precision=highest)
    valid = jnp.arange(length) < count
    scores = low_back(jnp.where(valid[None, None, :], scores, -1e+30))
    row_max = lax.optimization_barrier(jnp.max(scores, axis=-1, keepdims=True))
    exponent = jnp.exp(scores - row_max)
    attention = low(exponent / lax.optimization_barrier(jnp.sum(exponent, axis=-1, keepdims=True)))
    mixed = jnp.einsum('hqk,khe->qhe', attention, value_heads, precision=highest)
    return mixed.reshape(length, HEADS * HEAD_DIM)

def reference(plots, plot_grid, query_weight, key_weight, value_weight, out_weight, gate_weight, up_weight, down_weight, gain_attn, gain_mlp, cotangent):
    counts = (plot_grid[:, 0] * plot_grid[:, 1]).astype(jnp.int32)

    def forward(inputs, weight_query, weight_key, weight_value, weight_out, weight_gate, weight_up, weight_down, gain_one, gain_two):
        normed = low(rms_norm(inputs, gain_one))
        query = low_back(low(product(normed, weight_query)))
        keys = low_back(low(product(normed, weight_key)))
        values = low_back(low(product(normed, weight_value)))
        mixed = lax.map(jax.checkpoint(attend_plot), (query, keys, values, counts))
        mixed = low_back(low(mixed))
        hidden_in = inputs + low_back(product(mixed, weight_out))
        normed_mlp = low(rms_norm(hidden_in, gain_two))
        gate_pre = low_back(product(normed_mlp, weight_gate))
        up_pre = low_back(product(normed_mlp, weight_up))
        activated = low(jax.nn.gelu(gate_pre, approximate=True) * up_pre)
        return hidden_in + low_back(product(activated, weight_down))
    floats = (plots.astype(jnp.float32), query_weight.astype(jnp.float32), key_weight.astype(jnp.float32), value_weight.astype(jnp.float32), out_weight.astype(jnp.float32), gate_weight.astype(jnp.float32), up_weight.astype(jnp.float32), down_weight.astype(jnp.float32), gain_attn.astype(jnp.float32), gain_mlp.astype(jnp.float32))
    output, pullback = jax.vjp(forward, *floats)
    grads = pullback(cotangent.astype(jnp.float32))
    return (output.astype(jnp.bfloat16), grads[0].astype(jnp.bfloat16), grads[1], grads[2], grads[3], grads[4], grads[5], grads[6], grads[7], grads[8], grads[9])
```

```python
import functools

import jax
import jax.numpy as jnp
from jax import lax
from jax.experimental import pallas as pl
from jax.experimental.pallas import tpu as pltpu
from jax.sharding import PartitionSpec as P

HEADS = 12
HEAD_DIM = 64


epsilon = 1e-06


def norm_rows(values, gain):
    return values * lax.rsqrt(jnp.mean(values * values, axis=-1, keepdims=True) + epsilon) * gain


def gated(gate_pre, up_pre):
    return jax.nn.gelu(gate_pre, approximate=True) * up_pre


def to_heads(tensor):
    return tensor.reshape(tensor.shape[0], tensor.shape[1], HEADS, HEAD_DIM).transpose(2, 0, 1, 3)


def from_heads(tensor):
    return tensor.transpose(1, 2, 0, 3).reshape(tensor.shape[1], tensor.shape[2], HEADS * HEAD_DIM)


def masked_scores(query_one, keys_one, valid):
    scores = jnp.einsum("pqe,pke->pqk", query_one, keys_one, preferred_element_type=jnp.float32)
    return jnp.where(valid[:, None, :], scores, -1e30)


def weight_grad(left, right):
    return jnp.einsum("psd,pse->de", left, right, preferred_element_type=jnp.float32)


def back_product(grad_rows, weight):
    return jnp.einsum("pse,de->psd", grad_rows, weight, preferred_element_type=jnp.float32)


def forward_pass(inputs, weights, valid):
    (
        query_weight,
        key_weight,
        value_weight,
        out_weight,
        gate_weight,
        up_weight,
        down_weight,
        gain_attn,
        gain_mlp,
    ) = weights
    normed = norm_rows(inputs, gain_attn.astype(jnp.float32)).astype(jnp.bfloat16)
    query = jnp.dot(normed, query_weight, preferred_element_type=jnp.float32).astype(jnp.bfloat16)
    keys_local = jnp.dot(normed, key_weight, preferred_element_type=jnp.float32).astype(
        jnp.bfloat16
    )
    values_local = jnp.dot(normed, value_weight, preferred_element_type=jnp.float32).astype(
        jnp.bfloat16
    )
    keys_all, values_all = (
        lax.all_gather(keys_local, "narrow", axis=1, tiled=True),
        lax.all_gather(values_local, "narrow", axis=1, tiled=True),
    )
    query_heads = to_heads(query)
    key_heads = to_heads(keys_all)
    value_heads = to_heads(values_all)

    def head_forward(operands):
        query_one, keys_one, values_one = operands
        scores = masked_scores(query_one, keys_one, valid)
        row_max = jnp.max(scores, axis=-1, keepdims=True)
        exponent = jnp.exp(scores - row_max)
        total = jnp.sum(exponent, axis=-1, keepdims=True)
        mixed = jnp.einsum(
            "pqk,pke->pqe",
            (exponent / total).astype(jnp.bfloat16),
            values_one,
            preferred_element_type=jnp.float32,
        )
        return (mixed.astype(jnp.bfloat16), (row_max + jnp.log(total))[..., 0])

    mixed_heads, log_total = lax.map(head_forward, (query_heads, key_heads, value_heads))
    attended = from_heads(mixed_heads)
    hidden_in = inputs + jnp.dot(attended, out_weight, preferred_element_type=jnp.float32)
    normed_mlp = norm_rows(hidden_in, gain_mlp.astype(jnp.float32)).astype(jnp.bfloat16)
    gate_pre = jnp.dot(normed_mlp, gate_weight, preferred_element_type=jnp.float32)
    up_pre = jnp.dot(normed_mlp, up_weight, preferred_element_type=jnp.float32)
    activated = gated(gate_pre, up_pre).astype(jnp.bfloat16)
    output = hidden_in + jnp.dot(activated, down_weight, preferred_element_type=jnp.float32)
    saved = (
        normed,
        query_heads,
        key_heads,
        value_heads,
        log_total,
        attended,
        hidden_in,
        normed_mlp,
        gate_pre,
        up_pre,
        activated,
    )
    return (output, saved)


def body_general(
    plots,
    plot_grid,
    query_weight,
    key_weight,
    value_weight,
    out_weight,
    gate_weight,
    up_weight,
    down_weight,
    gain_attn,
    gain_mlp,
    cotangent,
):
    shards = (
        query_weight,
        key_weight,
        value_weight,
        out_weight,
        gate_weight,
        up_weight,
        down_weight,
        gain_attn,
        gain_mlp,
    )
    inputs = plots.astype(jnp.float32)
    counts = plot_grid[:, 0] * plot_grid[:, 1]
    length = plots.shape[1] * lax.axis_size("narrow")
    valid = jnp.arange(length)[None, :] < counts[:, None]
    weights = (
        lax.all_gather(shards[0], "wide", axis=0, tiled=True),
        lax.all_gather(shards[1], "wide", axis=0, tiled=True),
        lax.all_gather(shards[2], "wide", axis=0, tiled=True),
        lax.all_gather(shards[3], "wide", axis=0, tiled=True),
        lax.all_gather(shards[4], "wide", axis=0, tiled=True),
        lax.all_gather(shards[5], "wide", axis=0, tiled=True),
        lax.all_gather(shards[6], "wide", axis=0, tiled=True),
        lax.all_gather(shards[7], "wide", axis=0, tiled=True),
        lax.all_gather(shards[8], "wide", axis=0, tiled=True),
    )
    output, saved = forward_pass(inputs, weights, valid)
    weights = (
        lax.all_gather(shards[0], "wide", axis=0, tiled=True),
        lax.all_gather(shards[1], "wide", axis=0, tiled=True),
        lax.all_gather(shards[2], "wide", axis=0, tiled=True),
        lax.all_gather(shards[3], "wide", axis=0, tiled=True),
        lax.all_gather(shards[4], "wide", axis=0, tiled=True),
        lax.all_gather(shards[5], "wide", axis=0, tiled=True),
        lax.all_gather(shards[6], "wide", axis=0, tiled=True),
        lax.all_gather(shards[7], "wide", axis=0, tiled=True),
        lax.all_gather(shards[8], "wide", axis=0, tiled=True),
    )
    rerun, saved = forward_pass(inputs, weights, valid)
    (
        normed,
        query_heads,
        key_heads,
        value_heads,
        log_total,
        attended,
        hidden_in,
        normed_mlp,
        gate_pre,
        up_pre,
        activated,
    ) = saved
    (
        full_query,
        full_key,
        full_value,
        full_out,
        full_gate,
        full_up,
        full_down,
        full_gain_attn,
        full_gain_mlp,
    ) = weights
    grad_output = cotangent.astype(jnp.float32)
    grad_branch = grad_output.astype(jnp.bfloat16)
    grad_down = weight_grad(activated, grad_branch)
    grad_act = back_product(grad_branch, full_down)
    gate_value, gate_pull = jax.vjp(gated, gate_pre, up_pre)
    grad_gate_pre, grad_up_pre = gate_pull(grad_act)
    grad_gate_low = grad_gate_pre.astype(jnp.bfloat16)
    grad_up_low = grad_up_pre.astype(jnp.bfloat16)
    grad_gate = weight_grad(normed_mlp, grad_gate_low)
    grad_up = weight_grad(normed_mlp, grad_up_low)
    grad_normed_mlp = back_product(grad_gate_low, full_gate) + back_product(grad_up_low, full_up)
    norm_value, norm_pull = jax.vjp(norm_rows, hidden_in, full_gain_mlp.astype(jnp.float32))
    grad_hidden_norm, grad_gain_mlp = norm_pull(grad_normed_mlp)
    grad_hidden = grad_output + grad_hidden_norm
    grad_hidden_low = grad_hidden.astype(jnp.bfloat16)
    grad_out = weight_grad(attended, grad_hidden_low)
    grad_attended = back_product(grad_hidden_low, full_out).astype(jnp.bfloat16)
    grad_heads = to_heads(grad_attended)

    def head_backward(operands):
        query_one, keys_one, values_one, log_one, grad_one = operands
        scores = masked_scores(query_one, keys_one, valid)
        attention = jnp.exp(scores - log_one[..., None])
        grad_soft = jnp.einsum(
            "pqe,pke->pqk", grad_one, values_one, preferred_element_type=jnp.float32
        )
        row_dot = jnp.sum(attention * grad_soft, axis=-1, keepdims=True)
        grad_scores = (attention * (grad_soft - row_dot)).astype(jnp.bfloat16)
        grad_query_one = jnp.einsum(
            "pqk,pke->pqe", grad_scores, keys_one, preferred_element_type=jnp.float32
        )
        grad_keys_one = jnp.einsum(
            "pqk,pqe->pke", grad_scores, query_one, preferred_element_type=jnp.float32
        )
        grad_values_one = jnp.einsum(
            "pqk,pqe->pke",
            attention.astype(jnp.bfloat16),
            grad_one,
            preferred_element_type=jnp.float32,
        )
        return (grad_query_one, grad_keys_one, grad_values_one)

    grad_query_heads, grad_key_heads, grad_value_heads = lax.map(
        head_backward, (query_heads, key_heads, value_heads, log_total, grad_heads)
    )
    grad_key_local, grad_value_local = (
        lax.psum_scatter(
            grad_key_heads.astype(jnp.bfloat16), "narrow", scatter_dimension=2, tiled=True
        ).astype(jnp.float32),
        lax.psum_scatter(
            grad_value_heads.astype(jnp.bfloat16), "narrow", scatter_dimension=2, tiled=True
        ).astype(jnp.float32),
    )
    grad_query_low = from_heads(grad_query_heads).astype(jnp.bfloat16)
    grad_key_low = from_heads(grad_key_local).astype(jnp.bfloat16)
    grad_value_low = from_heads(grad_value_local).astype(jnp.bfloat16)
    grad_query = weight_grad(normed, grad_query_low)
    grad_key = weight_grad(normed, grad_key_low)
    grad_value = weight_grad(normed, grad_value_low)
    grad_normed = (
        back_product(grad_query_low, full_query)
        + back_product(grad_key_low, full_key)
        + back_product(grad_value_low, full_value)
    )
    first_value, first_pull = jax.vjp(norm_rows, inputs, full_gain_attn.astype(jnp.float32))
    grad_input_norm, grad_gain_attn = first_pull(grad_normed)
    grad_plots = (grad_hidden + grad_input_norm).astype(jnp.bfloat16)
    owned = (
        lax.psum_scatter(
            grad_query.astype(jnp.bfloat16), "wide", scatter_dimension=0, tiled=True
        ).astype(jnp.float32),
        lax.psum_scatter(
            grad_key.astype(jnp.bfloat16), "wide", scatter_dimension=0, tiled=True
        ).astype(jnp.float32),
        lax.psum_scatter(
            grad_value.astype(jnp.bfloat16), "wide", scatter_dimension=0, tiled=True
        ).astype(jnp.float32),
        lax.psum_scatter(
            grad_out.astype(jnp.bfloat16), "wide", scatter_dimension=0, tiled=True
        ).astype(jnp.float32),
        lax.psum_scatter(
            grad_gate.astype(jnp.bfloat16), "wide", scatter_dimension=0, tiled=True
        ).astype(jnp.float32),
        lax.psum_scatter(
            grad_up.astype(jnp.bfloat16), "wide", scatter_dimension=0, tiled=True
        ).astype(jnp.float32),
        lax.psum_scatter(
            grad_down.astype(jnp.bfloat16), "wide", scatter_dimension=0, tiled=True
        ).astype(jnp.float32),
        lax.psum_scatter(
            grad_gain_attn.astype(jnp.bfloat16), "wide", scatter_dimension=0, tiled=True
        ).astype(jnp.float32),
        lax.psum_scatter(
            grad_gain_mlp.astype(jnp.bfloat16), "wide", scatter_dimension=0, tiled=True
        ).astype(jnp.float32),
    )
    summed = (
        lax.psum(owned[0].astype(jnp.bfloat16), "narrow").astype(jnp.float32),
        lax.psum(owned[1].astype(jnp.bfloat16), "narrow").astype(jnp.float32),
        lax.psum(owned[2].astype(jnp.bfloat16), "narrow").astype(jnp.float32),
        lax.psum(owned[3].astype(jnp.bfloat16), "narrow").astype(jnp.float32),
        lax.psum(owned[4].astype(jnp.bfloat16), "narrow").astype(jnp.float32),
        lax.psum(owned[5].astype(jnp.bfloat16), "narrow").astype(jnp.float32),
        lax.psum(owned[6].astype(jnp.bfloat16), "narrow").astype(jnp.float32),
        lax.psum(owned[7].astype(jnp.bfloat16), "narrow").astype(jnp.float32),
        lax.psum(owned[8].astype(jnp.bfloat16), "narrow").astype(jnp.float32),
    )
    return (
        output.astype(jnp.bfloat16),
        grad_plots,
        summed[0],
        summed[1],
        summed[2],
        summed[3],
        summed[4],
        summed[5],
        summed[6],
        summed[7],
        summed[8],
    )


F32, BF16 = jnp.float32, jnp.bfloat16
ROOT = 0.7978845608028654
CUBE = 0.044715
VMEM_BYTES = 60 << 20


def nn(left, right):
    return lax.dot_general(left, right, (((1,), (0,)), ((), ())), preferred_element_type=F32)


def nt(left, right):
    return lax.dot_general(left, right, (((1,), (1,)), ((), ())), preferred_element_type=F32)


def lanes_of(rows, width=128):
    return lax.broadcasted_iota(jnp.int32, (rows, width), 1)


def row_block(index, size):
    return pl.ds(pl.multiple_of(index * size, size), size)


def head_masks(pair, lane, flag):
    first = jnp.where(lane < 64, pair, jnp.where(lane == 64, flag, 0.0))
    second = jnp.where(lane >= 64, pair, jnp.where(lane == 0, flag, 0.0))
    return first.astype(BF16), second.astype(BF16)


def attend_forward(count_ref, x_ref, gain_ref, wq_ref, wk_ref, wv_ref, wo_ref,
                   q_ref, k_ref, v_ref, normed_ref, mixed_ref, lse_ref, hidden_ref,
                   qh, kh, vh, lse_cols):
    slots = x_ref.shape[0]
    tile = 256
    tiles = slots // tile
    pairs = HEADS // 2

    def project(t, carry):
        rows = row_block(t, tile)
        x = x_ref[rows, :].astype(F32)
        r = lax.rsqrt(jnp.mean(x * x, axis=-1, keepdims=True) + epsilon)
        normed = (x * r * gain_ref[...]).astype(BF16)
        normed_ref[rows, :] = normed
        q_ref[rows, :] = nn(normed, wq_ref[...]).astype(BF16)
        k_ref[rows, :] = nn(normed, wk_ref[...]).astype(BF16)
        v_ref[rows, :] = nn(normed, wv_ref[...]).astype(BF16)
        return carry

    lax.fori_loop(0, tiles, project, 0)
    count = count_ref[0]
    lane = lanes_of(slots)
    slot = lax.broadcasted_iota(jnp.int32, (slots, 128), 0)
    bias = jnp.where(slot < count, 0.0, -1e30)
    lse_cols[...] = jnp.zeros_like(lse_cols)
    for h in range(2):
        vh[h, :, 128:] = jnp.ones((slots, 128), BF16)

    def pair_step(p, carry):
        cols = row_block(p, 128)
        kh[0], kh[1] = head_masks(k_ref[:, cols].astype(F32), lane, bias)
        qp = q_ref[:, cols].astype(F32)
        qh[0] = jnp.where(lane == 64, 1.0, qp).astype(BF16)
        qh[1] = jnp.where(lane == 0, 1.0, qp).astype(BF16)
        vh[0, :, :128], vh[1, :, :128] = head_masks(v_ref[:, cols].astype(F32), lane, 0.0)

        def tile_step(t, carry):
            rows = row_block(t, tile)
            total = None
            cols_out = lse_cols[rows, :]
            for h in range(2):
                score = nt(qh[h, rows, :], kh[h])
                top = jnp.max(score, axis=1, keepdims=True)
                weight = jnp.exp(score - top).astype(BF16)
                acc = nn(weight, vh[h])
                part = acc[:, :128] / acc[:, 128:]
                total = part if total is None else total + part
                cols_out = jnp.where(lanes_of(tile) == 2 * p + h, top + jnp.log(acc[:, 128:]), cols_out)
            mixed_ref[rows, cols] = total.astype(BF16)
            lse_cols[rows, :] = cols_out
            return carry

        lax.fori_loop(0, tiles, tile_step, 0)
        return carry

    lax.fori_loop(0, pairs, pair_step, 0)

    def project_out(t, carry):
        rows = row_block(t, tile)
        hidden_ref[rows, :] = x_ref[rows, :].astype(F32) + nn(mixed_ref[rows, :], wo_ref[...])
        lse_ref[:, rows] = jnp.transpose(lse_cols[rows, :])
        return carry

    lax.fori_loop(0, tiles, project_out, 0)


def permuted_store(target, index, value, block):
    blocks = target.shape[0] // block
    deep = blocks // 4
    turned = jnp.transpose(value)
    for w in range(blocks):
        z, x, c = w // 4, (w // 2) % 2, w % 2
        place = (c * 2 + x) * deep + z
        target[place * block:(place + 1) * block, index] = turned[w * block:(w + 1) * block, :]


def mlp_both(hidden_ref, cot_ref, gain_ref, wg_ref, wu_ref, wd_ref,
             out_ref, dhid_ref, gdown_ref, ggate_ref, gup_ref, ggain_ref,
             nmt, actt, dg_s, du_s):
    slots, d = hidden_ref.shape
    ff = wg_ref.shape[1]
    tile = 128
    blocks = 16
    ggain_ref[...] = jnp.zeros_like(ggain_ref)

    def step(t, carry):
        rows = row_block(t, tile)
        hidden = hidden_ref[rows, :]
        r = lax.rsqrt(jnp.mean(hidden * hidden, axis=-1, keepdims=True) + epsilon)
        gain = gain_ref[...]
        normed = (hidden * r * gain).astype(BF16)
        permuted_store(nmt, rows, normed, d // blocks)
        gate_pre = nn(normed, wg_ref[...])
        up_pre = nn(normed, wu_ref[...])
        square = gate_pre * gate_pre
        inner = ROOT * gate_pre * (1.0 + CUBE * square)
        th = jnp.tanh(inner)
        half = 0.5 * (1.0 + th)
        gelu = gate_pre * half
        slope = half + 0.5 * gate_pre * (1.0 - th * th) * (ROOT * (1.0 + 3.0 * CUBE * square))
        act = (gelu * up_pre).astype(BF16)
        permuted_store(actt, rows, act, ff // blocks)
        out_ref[rows, :] = (hidden + nn(act, wd_ref[...])).astype(BF16)
        dy = cot_ref[rows, :]
        d_act = nt(dy, wd_ref[...])
        dg = (d_act * up_pre * slope).astype(BF16)
        du = (d_act * gelu).astype(BF16)
        dg_s[rows, :] = dg
        du_s[rows, :] = du
        dn = nt(dg, wg_ref[...]) + nt(du, wu_ref[...])
        scaled = dn * gain
        mean = jnp.mean(scaled * hidden, axis=-1, keepdims=True)
        dhid_ref[rows, :] = dy.astype(F32) + r * scaled - hidden * (r * r * r * mean)
        ggain_ref[...] += jnp.sum(dn * hidden * r, axis=0, keepdims=True)
        return carry

    lax.fori_loop(0, slots // tile, step, 0)

    def down_step(n, carry):
        cols = row_block(n, 128)
        gdown_ref[:, cols] = nn(actt[...], cot_ref[:, cols]).astype(BF16)
        return carry

    lax.fori_loop(0, d // 128, down_step, 0)

    def gate_step(n, carry):
        cols = row_block(n, 256)
        ggate_ref[:, cols] = nn(nmt[...], dg_s[:, cols]).astype(BF16)
        gup_ref[:, cols] = nn(nmt[...], du_s[:, cols]).astype(BF16)
        return carry

    lax.fori_loop(0, ff // 256, gate_step, 0)


def attend_backward(count_ref, x_ref, gain_ref, wq_ref, wk_ref, wv_ref, wo_ref,
                    q_ref, k_ref, v_ref, normed_ref, mixed_ref, lse_ref, dhid_ref,
                    gplots_ref, gq_ref, gk_ref, gv_ref, gout_ref, ggain_ref,
                    dhl, dmix, dsum, turned, qh, kh, vh, dh, kt, dq_s, dk_s, dv_s, dqt):
    slots, d = x_ref.shape
    tile = 256
    tiles = slots // tile
    pairs = HEADS // 2
    blocks = 16
    head_row = lax.broadcasted_iota(jnp.int32, (128, d), 0)
    head_col = lax.broadcasted_iota(jnp.int32, (128, d), 1)
    pick = jnp.where(head_col // HEAD_DIM == head_row, 1.0, 0.0).astype(BF16)

    def first(t, carry):
        rows = row_block(t, tile)
        low = dhid_ref[rows, :].astype(BF16)
        dhl[rows, :] = low
        grad = nt(low, wo_ref[...]).astype(BF16)
        dmix[rows, :] = grad
        mixed = mixed_ref[rows, :]
        prod = grad.astype(F32) * mixed.astype(F32)
        high = prod.astype(BF16)
        rest = (prod - high.astype(F32)).astype(BF16)
        dsum[:, rows] = nt(pick, high) + nt(pick, rest)
        permuted_store(turned, rows, mixed, d // blocks)
        return carry

    lax.fori_loop(0, tiles, first, 0)

    def weight_grads(target, right):
        def step(n, carry):
            cols = row_block(n, 256)
            target[:, cols] = nn(turned[...], right[:, cols]).astype(BF16)
            return carry

        lax.fori_loop(0, d // 256, step, 0)

    weight_grads(gout_ref, dhl)
    count = count_ref[0]
    lane = lanes_of(slots)
    slot = lax.broadcasted_iota(jnp.int32, (slots, 128), 0)
    bias = jnp.where(slot < count, 0.0, -1e30)

    def pair_step(p, carry):
        cols = row_block(p, 128)
        kp = k_ref[:, cols].astype(F32)
        kh[0], kh[1] = head_masks(kp, lane, bias)
        for h in range(2):
            own = (lane < 64) if h == 0 else (lane >= 64)
            kt[h] = jnp.transpose(jnp.where(own, kp, 0.0)).astype(BF16)
        qp = q_ref[:, cols].astype(F32)
        qh[0] = jnp.where(lane == 64, 1.0, qp).astype(BF16)
        qh[1] = jnp.where(lane == 0, 1.0, qp).astype(BF16)
        qh[2], qh[3] = head_masks(qp, lane, 0.0)
        vh[0], vh[1] = head_masks(v_ref[:, cols].astype(F32), lane, 0.0)
        grad_pair = dmix[:, cols]
        dh[0], dh[1] = head_masks(grad_pair.astype(F32), lane, 0.0)
        dqt[...] = jnp.zeros_like(dqt)

        def tile_step(t, carry):
            rows = row_block(t, tile)
            d_k = d_v = None
            for h in range(2):
                score = nt(kh[h, rows, :], qh[h])
                weight = jnp.exp(score - lse_ref[pl.ds(2 * p + h, 1), :])
                d_att = nt(vh[h, rows, :], dmix[:, cols])
                d_score = (weight * (d_att - dsum[pl.ds(2 * p + h, 1), :])).astype(BF16)
                part_v = nn(weight.astype(BF16), dh[h])
                part_k = nn(d_score, qh[2 + h])
                d_v = part_v if d_v is None else d_v + part_v
                d_k = part_k if d_k is None else d_k + part_k
                dqt[...] += nn(kt[h, :, rows], d_score)
            dk_s[rows, cols] = d_k.astype(BF16)
            dv_s[rows, cols] = d_v.astype(BF16)
            return carry

        lax.fori_loop(0, tiles, tile_step, 0)
        dq_s[:, cols] = jnp.transpose(dqt[...]).astype(BF16)
        return carry

    lax.fori_loop(0, pairs, pair_step, 0)
    ggain_ref[...] = jnp.zeros_like(ggain_ref)

    def last(t, carry):
        rows = row_block(t, tile)
        permuted_store(turned, rows, normed_ref[rows, :], d // blocks)
        x = x_ref[rows, :].astype(F32)
        r = lax.rsqrt(jnp.mean(x * x, axis=-1, keepdims=True) + epsilon)
        dn = nt(dq_s[rows, :], wq_ref[...]) + nt(dk_s[rows, :], wk_ref[...]) + nt(dv_s[rows, :], wv_ref[...])
        scaled = dn * gain_ref[...]
        mean = jnp.mean(scaled * x, axis=-1, keepdims=True)
        gplots_ref[rows, :] = (dhid_ref[rows, :] + r * scaled - x * (r * r * r * mean)).astype(BF16)
        ggain_ref[...] += jnp.sum(dn * x * r, axis=0, keepdims=True)
        return carry

    lax.fori_loop(0, tiles, last, 0)
    weight_grads(gq_ref, dq_s)
    weight_grads(gk_ref, dk_s)
    weight_grads(gv_ref, dv_s)


def call(kernel, outs, scratch, args, scalars=1):
    return pl.pallas_call(
        kernel,
        out_shape=[jax.ShapeDtypeStruct(shape, dtype) for shape, dtype in outs],
        in_specs=[pl.BlockSpec(memory_space=pltpu.SMEM)] * scalars
        + [pl.BlockSpec(memory_space=pltpu.VMEM)] * (len(args) - scalars),
        out_specs=[pl.BlockSpec(memory_space=pltpu.VMEM)] * len(outs),
        scratch_shapes=scratch,
        compiler_params=pltpu.CompilerParams(vmem_limit_bytes=VMEM_BYTES),
    )(*args)


def unpermute(grad, rows):
    cols = grad.shape[1]
    return grad.reshape(2, 2, -1, rows, cols).transpose(2, 1, 0, 3, 4).reshape(-1, cols)


def body_plot(plots, plot_grid, query_weight, key_weight, value_weight, out_weight, gate_weight, up_weight, down_weight,
              gain_attn, gain_mlp, cotangent):
    rows, d = query_weight.shape
    ff = gate_weight.shape[1]
    rows_down = down_weight.shape[0]
    x = lax.all_to_all(plots, "narrow", 0, 1, tiled=True)[0]
    cot = lax.all_to_all(cotangent, "narrow", 0, 1, tiled=True)[0]
    slots = x.shape[0]
    counts = plot_grid[:, 0] * plot_grid[:, 1]
    count = lax.dynamic_slice(counts, (lax.axis_index("narrow"),), (1,))
    gather = functools.partial(lax.all_gather, axis_name="wide", axis=0, tiled=True)
    gains = lax.all_gather(jnp.stack([gain_attn, gain_mlp]), "wide", axis=1, tiled=True).astype(F32)
    wq, wk, wv, wo = gather(query_weight), gather(key_weight), gather(value_weight), gather(out_weight)
    wg, wu, wd = gather(gate_weight), gather(up_weight), gather(down_weight)
    act = lambda dtype=BF16: ((slots, d), dtype)
    vm = lambda shape, dtype=BF16: pltpu.VMEM(shape, dtype)
    q, k, v, normed, mixed, lse, hidden = call(
        attend_forward,
        [act(), act(), act(), act(), act(), ((128, slots), F32), act(F32)],
        [vm((2, slots, 128)), vm((2, slots, 128)), vm((2, slots, 256)), vm((slots, 128), F32)],
        (count, x, gains[0:1], wq, wk, wv, wo),
    )
    output, dhid, g_down, g_gate, g_up, gg_mlp = call(
        mlp_both,
        [act(), act(F32), ((ff, d), BF16), ((d, ff), BF16), ((d, ff), BF16), ((1, d), F32)],
        [vm((d, slots)), vm((ff, slots)), vm((slots, ff)), vm((slots, ff))],
        (hidden, cot, gains[1:2], wg, wu, wd), 0,
    )
    gplots, g_q, g_k, g_v, g_out, gg_attn = call(
        attend_backward,
        [act(), ((d, d), BF16), ((d, d), BF16), ((d, d), BF16), ((d, d), BF16), ((1, d), F32)],
        [vm((slots, d)), vm((slots, d)), vm((128, slots), F32), vm((d, slots)), vm((4, slots, 128)), vm((2, slots, 128)),
         vm((2, slots, 128)), vm((2, slots, 128)), vm((2, 128, slots)), vm((slots, d)), vm((slots, d)), vm((slots, d)),
         vm((128, slots), F32)],
        (count, x, gains[0:1], wq, wk, wv, wo, q, k, v, normed, mixed, lse, dhid),
    )

    def reduce(grad, rows):
        part = lax.psum_scatter(unpermute(grad, rows), "wide", scatter_dimension=0, tiled=True)
        return lax.psum(part, "narrow").astype(F32)

    def reduce_gain(grad):
        total = lax.psum(grad[0], ("wide", "narrow"))
        return lax.dynamic_slice(total, (lax.axis_index("wide") * rows,), (rows,))

    back = lambda value: lax.all_to_all(value[None], "narrow", 1, 0, tiled=True)
    return (back(output), back(gplots), reduce(g_q, rows), reduce(g_k, rows), reduce(g_v, rows), reduce(g_out, rows),
            reduce(g_gate, rows), reduce(g_up, rows), reduce(g_down, rows_down), reduce_gain(gg_attn), reduce_gain(gg_mlp))


def body_for(mesh):
    plots_fit = mesh.shape["narrow"] == 2 and mesh.shape["wide"] == 16

    def body(plots, *rest):
        if plots_fit and plots.shape == (2, 512, HEADS * HEAD_DIM):
            return body_plot(plots, *rest)
        return body_general(plots, *rest)

    return body


def solution(mesh):
    return jax.shard_map(
        body_for(mesh),
        mesh=mesh,
        in_specs=(
            P("wide", "narrow", None),
            P("wide", None),
            P("wide", None),
            P("wide", None),
            P("wide", None),
            P("wide", None),
            P("wide", None),
            P("wide", None),
            P("wide", None),
            P("wide"),
            P("wide"),
            P("wide", "narrow", None),
        ),
        out_specs=(
            P("wide", "narrow", None),
            P("wide", "narrow", None),
            P("wide", None),
            P("wide", None),
            P("wide", None),
            P("wide", None),
            P("wide", None),
            P("wide", None),
            P("wide", None),
            P("wide"),
            P("wide"),
        ),
        check_vma=False,
    )
```

```python
import functools

import jax
import jax.numpy as jnp
from jax import lax
from jax.experimental import pallas as pl
from jax.experimental.pallas import tpu as pltpu
from jax.sharding import PartitionSpec as P

HEADS = 12
HEAD_DIM = 64


epsilon = 1e-06


def norm_rows(values, gain):
    return values * lax.rsqrt(jnp.mean(values * values, axis=-1, keepdims=True) + epsilon) * gain


def gated(gate_pre, up_pre):
    return jax.nn.gelu(gate_pre, approximate=True) * up_pre


def to_heads(tensor):
    return tensor.reshape(tensor.shape[0], tensor.shape[1], HEADS, HEAD_DIM).transpose(2, 0, 1, 3)


def from_heads(tensor):
    return tensor.transpose(1, 2, 0, 3).reshape(tensor.shape[1], tensor.shape[2], HEADS * HEAD_DIM)


def masked_scores(query_one, keys_one, valid):
    scores = jnp.einsum("pqe,pke->pqk", query_one, keys_one, preferred_element_type=jnp.float32)
    return jnp.where(valid[:, None, :], scores, -1e30)


def weight_grad(left, right):
    return jnp.einsum("psd,pse->de", left, right, preferred_element_type=jnp.float32)


def back_product(grad_rows, weight):
    return jnp.einsum("pse,de->psd", grad_rows, weight, preferred_element_type=jnp.float32)


def forward_pass(inputs, weights, valid):
    (
        query_weight,
        key_weight,
        value_weight,
        out_weight,
        gate_weight,
        up_weight,
        down_weight,
        gain_attn,
        gain_mlp,
    ) = weights
    normed = norm_rows(inputs, gain_attn.astype(jnp.float32)).astype(jnp.bfloat16)
    query = jnp.dot(normed, query_weight, preferred_element_type=jnp.float32).astype(jnp.bfloat16)
    keys_local = jnp.dot(normed, key_weight, preferred_element_type=jnp.float32).astype(
        jnp.bfloat16
    )
    values_local = jnp.dot(normed, value_weight, preferred_element_type=jnp.float32).astype(
        jnp.bfloat16
    )
    keys_all, values_all = (
        lax.all_gather(keys_local, "narrow", axis=1, tiled=True),
        lax.all_gather(values_local, "narrow", axis=1, tiled=True),
    )
    query_heads = to_heads(query)
    key_heads = to_heads(keys_all)
    value_heads = to_heads(values_all)

    def head_forward(operands):
        query_one, keys_one, values_one = operands
        scores = masked_scores(query_one, keys_one, valid)
        row_max = jnp.max(scores, axis=-1, keepdims=True)
        exponent = jnp.exp(scores - row_max)
        total = jnp.sum(exponent, axis=-1, keepdims=True)
        mixed = jnp.einsum(
            "pqk,pke->pqe",
            (exponent / total).astype(jnp.bfloat16),
            values_one,
            preferred_element_type=jnp.float32,
        )
        return (mixed.astype(jnp.bfloat16), (row_max + jnp.log(total))[..., 0])

    mixed_heads, log_total = lax.map(head_forward, (query_heads, key_heads, value_heads))
    attended = from_heads(mixed_heads)
    hidden_in = inputs + jnp.dot(attended, out_weight, preferred_element_type=jnp.float32)
    normed_mlp = norm_rows(hidden_in, gain_mlp.astype(jnp.float32)).astype(jnp.bfloat16)
    gate_pre = jnp.dot(normed_mlp, gate_weight, preferred_element_type=jnp.float32)
    up_pre = jnp.dot(normed_mlp, up_weight, preferred_element_type=jnp.float32)
    activated = gated(gate_pre, up_pre).astype(jnp.bfloat16)
    output = hidden_in + jnp.dot(activated, down_weight, preferred_element_type=jnp.float32)
    saved = (
        normed,
        query_heads,
        key_heads,
        value_heads,
        log_total,
        attended,
        hidden_in,
        normed_mlp,
        gate_pre,
        up_pre,
        activated,
    )
    return (output, saved)


def body_general(
    plots,
    plot_grid,
    query_weight,
    key_weight,
    value_weight,
    out_weight,
    gate_weight,
    up_weight,
    down_weight,
    gain_attn,
    gain_mlp,
    cotangent,
):
    shards = (
        query_weight,
        key_weight,
        value_weight,
        out_weight,
        gate_weight,
        up_weight,
        down_weight,
        gain_attn,
        gain_mlp,
    )
    inputs = plots.astype(jnp.float32)
    counts = plot_grid[:, 0] * plot_grid[:, 1]
    length = plots.shape[1] * lax.axis_size("narrow")
    valid = jnp.arange(length)[None, :] < counts[:, None]
    weights = (
        lax.all_gather(shards[0], "wide", axis=0, tiled=True),
        lax.all_gather(shards[1], "wide", axis=0, tiled=True),
        lax.all_gather(shards[2], "wide", axis=0, tiled=True),
        lax.all_gather(shards[3], "wide", axis=0, tiled=True),
        lax.all_gather(shards[4], "wide", axis=0, tiled=True),
        lax.all_gather(shards[5], "wide", axis=0, tiled=True),
        lax.all_gather(shards[6], "wide", axis=0, tiled=True),
        lax.all_gather(shards[7], "wide", axis=0, tiled=True),
        lax.all_gather(shards[8], "wide", axis=0, tiled=True),
    )
    output, saved = forward_pass(inputs, weights, valid)
    weights = (
        lax.all_gather(shards[0], "wide", axis=0, tiled=True),
        lax.all_gather(shards[1], "wide", axis=0, tiled=True),
        lax.all_gather(shards[2], "wide", axis=0, tiled=True),
        lax.all_gather(shards[3], "wide", axis=0, tiled=True),
        lax.all_gather(shards[4], "wide", axis=0, tiled=True),
        lax.all_gather(shards[5], "wide", axis=0, tiled=True),
        lax.all_gather(shards[6], "wide", axis=0, tiled=True),
        lax.all_gather(shards[7], "wide", axis=0, tiled=True),
        lax.all_gather(shards[8], "wide", axis=0, tiled=True),
    )
    rerun, saved = forward_pass(inputs, weights, valid)
    (
        normed,
        query_heads,
        key_heads,
        value_heads,
        log_total,
        attended,
        hidden_in,
        normed_mlp,
        gate_pre,
        up_pre,
        activated,
    ) = saved
    (
        full_query,
        full_key,
        full_value,
        full_out,
        full_gate,
        full_up,
        full_down,
        full_gain_attn,
        full_gain_mlp,
    ) = weights
    grad_output = cotangent.astype(jnp.float32)
    grad_branch = grad_output.astype(jnp.bfloat16)
    grad_down = weight_grad(activated, grad_branch)
    grad_act = back_product(grad_branch, full_down)
    gate_value, gate_pull = jax.vjp(gated, gate_pre, up_pre)
    grad_gate_pre, grad_up_pre = gate_pull(grad_act)
    grad_gate_low = grad_gate_pre.astype(jnp.bfloat16)
    grad_up_low = grad_up_pre.astype(jnp.bfloat16)
    grad_gate = weight_grad(normed_mlp, grad_gate_low)
    grad_up = weight_grad(normed_mlp, grad_up_low)
    grad_normed_mlp = back_product(grad_gate_low, full_gate) + back_product(grad_up_low, full_up)
    norm_value, norm_pull = jax.vjp(norm_rows, hidden_in, full_gain_mlp.astype(jnp.float32))
    grad_hidden_norm, grad_gain_mlp = norm_pull(grad_normed_mlp)
    grad_hidden = grad_output + grad_hidden_norm
    grad_hidden_low = grad_hidden.astype(jnp.bfloat16)
    grad_out = weight_grad(attended, grad_hidden_low)
    grad_attended = back_product(grad_hidden_low, full_out).astype(jnp.bfloat16)
    grad_heads = to_heads(grad_attended)

    def head_backward(operands):
        query_one, keys_one, values_one, log_one, grad_one = operands
        scores = masked_scores(query_one, keys_one, valid)
        attention = jnp.exp(scores - log_one[..., None])
        grad_soft = jnp.einsum(
            "pqe,pke->pqk", grad_one, values_one, preferred_element_type=jnp.float32
        )
        row_dot = jnp.sum(attention * grad_soft, axis=-1, keepdims=True)
        grad_scores = (attention * (grad_soft - row_dot)).astype(jnp.bfloat16)
        grad_query_one = jnp.einsum(
            "pqk,pke->pqe", grad_scores, keys_one, preferred_element_type=jnp.float32
        )
        grad_keys_one = jnp.einsum(
            "pqk,pqe->pke", grad_scores, query_one, preferred_element_type=jnp.float32
        )
        grad_values_one = jnp.einsum(
            "pqk,pqe->pke",
            attention.astype(jnp.bfloat16),
            grad_one,
            preferred_element_type=jnp.float32,
        )
        return (grad_query_one, grad_keys_one, grad_values_one)

    grad_query_heads, grad_key_heads, grad_value_heads = lax.map(
        head_backward, (query_heads, key_heads, value_heads, log_total, grad_heads)
    )
    grad_key_local, grad_value_local = (
        lax.psum_scatter(
            grad_key_heads.astype(jnp.bfloat16), "narrow", scatter_dimension=2, tiled=True
        ).astype(jnp.float32),
        lax.psum_scatter(
            grad_value_heads.astype(jnp.bfloat16), "narrow", scatter_dimension=2, tiled=True
        ).astype(jnp.float32),
    )
    grad_query_low = from_heads(grad_query_heads).astype(jnp.bfloat16)
    grad_key_low = from_heads(grad_key_local).astype(jnp.bfloat16)
    grad_value_low = from_heads(grad_value_local).astype(jnp.bfloat16)
    grad_query = weight_grad(normed, grad_query_low)
    grad_key = weight_grad(normed, grad_key_low)
    grad_value = weight_grad(normed, grad_value_low)
    grad_normed = (
        back_product(grad_query_low, full_query)
        + back_product(grad_key_low, full_key)
        + back_product(grad_value_low, full_value)
    )
    first_value, first_pull = jax.vjp(norm_rows, inputs, full_gain_attn.astype(jnp.float32))
    grad_input_norm, grad_gain_attn = first_pull(grad_normed)
    grad_plots = (grad_hidden + grad_input_norm).astype(jnp.bfloat16)
    owned = (
        lax.psum_scatter(
            grad_query.astype(jnp.bfloat16), "wide", scatter_dimension=0, tiled=True
        ).astype(jnp.float32),
        lax.psum_scatter(
            grad_key.astype(jnp.bfloat16), "wide", scatter_dimension=0, tiled=True
        ).astype(jnp.float32),
        lax.psum_scatter(
            grad_value.astype(jnp.bfloat16), "wide", scatter_dimension=0, tiled=True
        ).astype(jnp.float32),
        lax.psum_scatter(
            grad_out.astype(jnp.bfloat16), "wide", scatter_dimension=0, tiled=True
        ).astype(jnp.float32),
        lax.psum_scatter(
            grad_gate.astype(jnp.bfloat16), "wide", scatter_dimension=0, tiled=True
        ).astype(jnp.float32),
        lax.psum_scatter(
            grad_up.astype(jnp.bfloat16), "wide", scatter_dimension=0, tiled=True
        ).astype(jnp.float32),
        lax.psum_scatter(
            grad_down.astype(jnp.bfloat16), "wide", scatter_dimension=0, tiled=True
        ).astype(jnp.float32),
        lax.psum_scatter(
            grad_gain_attn.astype(jnp.bfloat16), "wide", scatter_dimension=0, tiled=True
        ).astype(jnp.float32),
        lax.psum_scatter(
            grad_gain_mlp.astype(jnp.bfloat16), "wide", scatter_dimension=0, tiled=True
        ).astype(jnp.float32),
    )
    summed = (
        lax.psum(owned[0].astype(jnp.bfloat16), "narrow").astype(jnp.float32),
        lax.psum(owned[1].astype(jnp.bfloat16), "narrow").astype(jnp.float32),
        lax.psum(owned[2].astype(jnp.bfloat16), "narrow").astype(jnp.float32),
        lax.psum(owned[3].astype(jnp.bfloat16), "narrow").astype(jnp.float32),
        lax.psum(owned[4].astype(jnp.bfloat16), "narrow").astype(jnp.float32),
        lax.psum(owned[5].astype(jnp.bfloat16), "narrow").astype(jnp.float32),
        lax.psum(owned[6].astype(jnp.bfloat16), "narrow").astype(jnp.float32),
        lax.psum(owned[7].astype(jnp.bfloat16), "narrow").astype(jnp.float32),
        lax.psum(owned[8].astype(jnp.bfloat16), "narrow").astype(jnp.float32),
    )
    return (
        output.astype(jnp.bfloat16),
        grad_plots,
        summed[0],
        summed[1],
        summed[2],
        summed[3],
        summed[4],
        summed[5],
        summed[6],
        summed[7],
        summed[8],
    )


F32, BF16 = jnp.float32, jnp.bfloat16
ROOT = 0.7978845608028654
CUBE = 0.044715
VMEM_BYTES = 60 << 20


def nn(left, right):
    return lax.dot_general(left, right, (((1,), (0,)), ((), ())), preferred_element_type=F32)


def nt(left, right):
    return lax.dot_general(left, right, (((1,), (1,)), ((), ())), preferred_element_type=F32)


def lanes_of(rows, width=128):
    return lax.broadcasted_iota(jnp.int32, (rows, width), 1)


def row_block(index, size):
    return pl.ds(pl.multiple_of(index * size, size), size)


def head_masks(pair, lane, flag):
    first = jnp.where(lane < 64, pair, jnp.where(lane == 64, flag, 0.0))
    second = jnp.where(lane >= 64, pair, jnp.where(lane == 0, flag, 0.0))
    return first.astype(BF16), second.astype(BF16)


MESH_ID = pl.DeviceIdType.MESH


class Place:
    def __init__(self):
        wide, self.y = lax.axis_index("wide"), lax.axis_index("narrow")
        self.z, self.x, self.c = wide // 4, (wide // 2) % 2, wide % 2
        self.wide = wide

    def block(self, z, x, c):
        return (z * 2 + x) * 2 + c

    def other_z(self, j):
        z = self.z
        return (z + 1 - 2 * (z % 2), (z + 2) % 4, 3 - z)[j]

    def to_z(self, j):
        return (self.block(self.other_z(j), self.x, self.c), self.y)

    def to_x(self):
        return (self.block(self.z, 1 - self.x, self.c), self.y)

    def to_core(self):
        return (self.block(self.z, self.x, 1 - self.c), self.y)

    def to_y(self):
        return (self.wide, 1 - self.y)

    def greet(self):
        barrier = pltpu.get_barrier_semaphore()
        partners = [self.to_z(0), self.to_z(1), self.to_z(2), self.to_x(), self.to_core(), self.to_y()]
        for partner in partners:
            pl.semaphore_signal(barrier, inc=1, device_id=partner, device_id_type=MESH_ID)
        pl.semaphore_wait(barrier, len(partners))


class Gather:
    def __init__(self, place, full, send, recv):
        self.place, self.full, self.sends, self.recvs = place, full, send, recv
        self.slot = 0

    def copy(self, block, target, slot):
        return pltpu.make_async_remote_copy(
            src_ref=self.full.at[block], dst_ref=self.full.at[block], send_sem=self.sends.at[slot],
            recv_sem=self.recvs.at[block], device_id=target, device_id_type=MESH_ID)

    def send(self, block, target):
        self.copy(block, target, self.slot).start()
        self.slot += 1

    def wait(self, block):
        self.copy(block, self.place.to_core(), 0).wait_recv()

    def start(self):
        p = self.place
        own = p.block(p.z, p.x, p.c)
        for j in (2, 1, 0):
            self.send(own, p.to_z(j))
        self.send(own, p.to_x())
        self.send(own, p.to_core())

    def pass_z(self, j):
        p = self.place
        block = p.block(p.other_z(j), p.x, p.c)
        self.wait(block)
        self.send(block, p.to_x())
        self.send(block, p.to_core())

    def pass_x(self, j):
        p = self.place
        block = p.block(p.z if j == 3 else p.other_z(j), 1 - p.x, p.c)
        self.wait(block)
        self.send(block, p.to_core())

    def end(self):
        p = self.place
        for z in range(4):
            for x in range(2):
                self.wait(p.block(z, x, 1 - p.c))

    def sent(self):
        for slot in range(15):
            self.copy(0, self.place.to_core(), slot).wait_send()


def gather_forward(count_ref, plots_ref, cot_ref, gain_a_ref, gain_m_ref, own_q, own_k, own_v, own_o, own_g, own_u, own_d,
                   q_ref, k_ref, v_ref, normed_ref, mixed_ref, lse_ref, hidden_ref, x_ref, cot_out, gains_ref,
                   out_q, out_k, out_v, out_o, out_g, out_u, out_d,
                   qh, kh, vh, lse_cols, wq, wk, wv, wo, wg, wu, wd, wgain, sends, recvs, half_sems, out_sems):
    half = plots_ref.shape[1]
    slots = 2 * half
    tile = 256
    tiles = slots // tile
    pairs = HEADS // 2
    d = plots_ref.shape[2]
    place = Place()
    fulls = (wgain, wq, wk, wv, wo, wg, wu, wd)
    for full, own in zip(fulls[1:], (own_q, own_k, own_v, own_o, own_g, own_u, own_d)):
        full[place.wide] = own[...]
    wgain[place.wide, 0:1, 0:own_q.shape[0]] = gain_a_ref[...].astype(F32)
    wgain[place.wide, 1:2, 0:own_q.shape[0]] = gain_m_ref[...].astype(F32)
    gathers = [Gather(place, full, sends.at[i], recvs.at[i]) for i, full in enumerate(fulls)]
    g_gain, g_q, g_k, g_v, g_o, g_g, g_u, g_d = gathers
    mine = pl.ds(pl.multiple_of(place.y * half, half), half)

    def half_copy(source, target, i):
        return pltpu.make_async_remote_copy(
            src_ref=source.at[1 - place.y], dst_ref=target.at[mine], send_sem=half_sems.at[2 * i],
            recv_sem=half_sems.at[2 * i + 1], device_id=place.to_y(), device_id_type=MESH_ID)

    place.greet()
    x_copy, cot_copy = half_copy(plots_ref, x_ref, 0), half_copy(cot_ref, cot_out, 1)
    x_copy.start()
    for g in (g_gain, g_q, g_k, g_v):
        g.start()
    x_ref[mine, :] = plots_ref[place.y]
    cot_out[mine, :] = cot_ref[place.y]

    def relay_z(g):
        for j in range(3):
            g.pass_z(j)

    def relay_x(g):
        for j in (3, 0, 1, 2):
            g.pass_x(j)

    relay_z(g_gain)
    relay_z(g_q)
    g_o.start()
    relay_z(g_k)
    g_g.start()
    relay_x(g_gain)
    relay_x(g_q)
    relay_z(g_v)
    g_gain.end()
    rows_own = own_q.shape[0]
    for w in range(16):
        for i in range(2):
            gains_ref[i:i + 1, w * rows_own:(w + 1) * rows_own] = wgain[w, i:i + 1, 0:rows_own]
    x_copy.wait()
    cot_copy.start()

    def normalise(t, carry):
        rows = row_block(t, tile)
        x = x_ref[rows, :].astype(F32)
        r = lax.rsqrt(jnp.mean(x * x, axis=-1, keepdims=True) + epsilon)
        normed_ref[rows, :] = (x * r * gains_ref[0:1, :]).astype(BF16)
        return carry

    lax.fori_loop(0, tiles, normalise, 0)

    def project(target, full):
        def step(t, carry):
            rows = row_block(t, tile)
            target[rows, :] = nn(normed_ref[rows, :], full[...].reshape(d, d)).astype(BF16)
            return carry

        lax.fori_loop(0, tiles, step, 0)

    relay_x(g_k)
    g_q.end()
    project(q_ref, wq)
    relay_x(g_v)
    g_k.end()
    project(k_ref, wk)
    relay_z(g_o)
    g_u.start()
    g_v.end()
    project(v_ref, wv)

    count = count_ref[0]
    lane = lanes_of(slots)
    slot = lax.broadcasted_iota(jnp.int32, (slots, 128), 0)
    bias = jnp.where(slot < count, 0.0, -1e30)
    lse_cols[...] = jnp.zeros_like(lse_cols)
    for h in range(2):
        vh[h, :, 128:] = jnp.ones((slots, 128), BF16)
    hooks = {
        0: [lambda: g_g.pass_z(0)], 1: [lambda: relay_x(g_o)], 2: [lambda: g_g.pass_z(1)], 4: [lambda: g_g.pass_z(2), lambda: g_d.start()],
        5: [lambda: g_g.pass_x(3)], 6: [lambda: g_g.pass_x(0)], 7: [lambda: g_g.pass_x(1)], 8: [lambda: g_u.pass_z(0)], 9: [lambda: g_g.pass_x(2)],
        10: [lambda: g_u.pass_z(1)], 13: [lambda: g_u.pass_z(2)], 14: [lambda: g_u.pass_x(3)], 15: [lambda: g_u.pass_x(0)],
        16: [lambda: g_d.pass_z(0)], 17: [lambda: g_u.pass_x(1)], 19: [lambda: g_d.pass_z(1), lambda: g_u.pass_x(2)],
        23: [lambda: g_d.pass_z(2)],
    }

    def step(s, carry):
        p, t = s // tiles, s % tiles
        cols = row_block(p, 128)
        for when, events in hooks.items():
            @pl.when(s == when)
            def _():
                for event in events:
                    event()

        @pl.when(t == 0)
        def _():
            kh[0], kh[1] = head_masks(k_ref[:, cols].astype(F32), lane, bias)
            qp = q_ref[:, cols].astype(F32)
            qh[0] = jnp.where(lane == 64, 1.0, qp).astype(BF16)
            qh[1] = jnp.where(lane == 0, 1.0, qp).astype(BF16)
            vh[0, :, :128], vh[1, :, :128] = head_masks(v_ref[:, cols].astype(F32), lane, 0.0)

        rows = row_block(t, tile)
        total = None
        cols_out = lse_cols[rows, :]
        for h in range(2):
            score = nt(qh[h, rows, :], kh[h])
            top = jnp.max(score, axis=1, keepdims=True)
            weight = jnp.exp(score - top).astype(BF16)
            acc = nn(weight, vh[h])
            part = acc[:, :128] / acc[:, 128:]
            total = part if total is None else total + part
            cols_out = jnp.where(lanes_of(tile) == 2 * p + h, top + jnp.log(acc[:, 128:]), cols_out)
        mixed_ref[rows, cols] = total.astype(BF16)
        lse_cols[rows, :] = cols_out
        return carry

    lax.fori_loop(0, pairs * tiles, step, 0)
    relay_x(g_d)
    g_o.end()

    def project_out(t, carry):
        rows = row_block(t, tile)
        hidden_ref[rows, :] = x_ref[rows, :].astype(F32) + nn(mixed_ref[rows, :], wo[...].reshape(d, d))
        lse_ref[:, rows] = jnp.transpose(lse_cols[rows, :])
        return carry

    lax.fori_loop(0, tiles, project_out, 0)
    g_g.end()
    g_u.end()
    g_d.end()
    outs = [pltpu.make_async_copy(full, out, out_sems.at[i])
            for i, (full, out) in enumerate(zip(fulls[1:], (out_q, out_k, out_v, out_o, out_g, out_u, out_d)))]
    for copy in outs:
        copy.start()
    for g in gathers:
        g.sent()
    cot_copy.wait()
    for copy in outs:
        copy.wait()


def permuted_store(target, index, value, block):
    blocks = target.shape[0] // block
    deep = blocks // 4
    turned = jnp.transpose(value)
    for w in range(blocks):
        z, x, c = w // 4, (w // 2) % 2, w % 2
        place = (c * 2 + x) * deep + z
        target[place * block:(place + 1) * block, index] = turned[w * block:(w + 1) * block, :]


def mlp_both(hidden_ref, cot_ref, gain_ref, wg_ref, wu_ref, wd_ref,
             out_ref, dhid_ref, gdown_ref, ggate_ref, gup_ref, ggain_ref,
             nmt, actt, dg_s, du_s):
    slots, d = hidden_ref.shape
    ff = wg_ref.shape[1]
    tile = 128
    blocks = 16
    ggain_ref[...] = jnp.zeros_like(ggain_ref)

    def step(t, carry):
        rows = row_block(t, tile)
        hidden = hidden_ref[rows, :]
        r = lax.rsqrt(jnp.mean(hidden * hidden, axis=-1, keepdims=True) + epsilon)
        gain = gain_ref[...]
        normed = (hidden * r * gain).astype(BF16)
        permuted_store(nmt, rows, normed, d // blocks)
        gate_pre = nn(normed, wg_ref[...])
        up_pre = nn(normed, wu_ref[...])
        square = gate_pre * gate_pre
        inner = ROOT * gate_pre * (1.0 + CUBE * square)
        th = jnp.tanh(inner)
        half = 0.5 * (1.0 + th)
        gelu = gate_pre * half
        slope = half + 0.5 * gate_pre * (1.0 - th * th) * (ROOT * (1.0 + 3.0 * CUBE * square))
        act = (gelu * up_pre).astype(BF16)
        permuted_store(actt, rows, act, ff // blocks)
        out_ref[rows, :] = (hidden + nn(act, wd_ref[...])).astype(BF16)
        dy = cot_ref[rows, :]
        d_act = nt(dy, wd_ref[...])
        dg = (d_act * up_pre * slope).astype(BF16)
        du = (d_act * gelu).astype(BF16)
        dg_s[rows, :] = dg
        du_s[rows, :] = du
        dn = nt(dg, wg_ref[...]) + nt(du, wu_ref[...])
        scaled = dn * gain
        mean = jnp.mean(scaled * hidden, axis=-1, keepdims=True)
        dhid_ref[rows, :] = dy.astype(F32) + r * scaled - hidden * (r * r * r * mean)
        ggain_ref[...] += jnp.sum(dn * hidden * r, axis=0, keepdims=True)
        return carry

    lax.fori_loop(0, slots // tile, step, 0)

    def down_step(n, carry):
        cols = row_block(n, 128)
        gdown_ref[:, cols] = nn(actt[...], cot_ref[:, cols]).astype(BF16)
        return carry

    lax.fori_loop(0, d // 128, down_step, 0)

    def gate_step(n, carry):
        cols = row_block(n, 256)
        ggate_ref[:, cols] = nn(nmt[...], dg_s[:, cols]).astype(BF16)
        gup_ref[:, cols] = nn(nmt[...], du_s[:, cols]).astype(BF16)
        return carry

    lax.fori_loop(0, ff // 256, gate_step, 0)


def attend_backward(count_ref, x_ref, gain_ref, wq_ref, wk_ref, wv_ref, wo_ref,
                    q_ref, k_ref, v_ref, normed_ref, mixed_ref, lse_ref, dhid_ref,
                    gplots_ref, gq_ref, gk_ref, gv_ref, gout_ref, ggain_ref,
                    dhl, dmix, dsum, turned, qh, kh, vh, dh, kt, dq_s, dk_s, dv_s, dqt):
    slots, d = x_ref.shape
    tile = 256
    tiles = slots // tile
    pairs = HEADS // 2
    blocks = 16
    head_row = lax.broadcasted_iota(jnp.int32, (128, d), 0)
    head_col = lax.broadcasted_iota(jnp.int32, (128, d), 1)
    pick = jnp.where(head_col // HEAD_DIM == head_row, 1.0, 0.0).astype(BF16)

    def first(t, carry):
        rows = row_block(t, tile)
        low = dhid_ref[rows, :].astype(BF16)
        dhl[rows, :] = low
        grad = nt(low, wo_ref[...]).astype(BF16)
        dmix[rows, :] = grad
        mixed = mixed_ref[rows, :]
        prod = grad.astype(F32) * mixed.astype(F32)
        high = prod.astype(BF16)
        rest = (prod - high.astype(F32)).astype(BF16)
        dsum[:, rows] = nt(pick, high) + nt(pick, rest)
        permuted_store(turned, rows, mixed, d // blocks)
        return carry

    lax.fori_loop(0, tiles, first, 0)

    def weight_grads(target, right):
        def step(n, carry):
            cols = row_block(n, 256)
            target[:, cols] = nn(turned[...], right[:, cols]).astype(BF16)
            return carry

        lax.fori_loop(0, d // 256, step, 0)

    weight_grads(gout_ref, dhl)
    count = count_ref[0]
    lane = lanes_of(slots)
    slot = lax.broadcasted_iota(jnp.int32, (slots, 128), 0)
    bias = jnp.where(slot < count, 0.0, -1e30)

    def pair_step(p, carry):
        cols = row_block(p, 128)
        kp = k_ref[:, cols].astype(F32)
        kh[0], kh[1] = head_masks(kp, lane, bias)
        for h in range(2):
            own = (lane < 64) if h == 0 else (lane >= 64)
            kt[h] = jnp.transpose(jnp.where(own, kp, 0.0)).astype(BF16)
        qp = q_ref[:, cols].astype(F32)
        qh[0] = jnp.where(lane == 64, 1.0, qp).astype(BF16)
        qh[1] = jnp.where(lane == 0, 1.0, qp).astype(BF16)
        qh[2], qh[3] = head_masks(qp, lane, 0.0)
        vh[0], vh[1] = head_masks(v_ref[:, cols].astype(F32), lane, 0.0)
        grad_pair = dmix[:, cols]
        dh[0], dh[1] = head_masks(grad_pair.astype(F32), lane, 0.0)
        dqt[...] = jnp.zeros_like(dqt)

        def tile_step(t, carry):
            rows = row_block(t, tile)
            d_k = d_v = None
            for h in range(2):
                score = nt(kh[h, rows, :], qh[h])
                weight = jnp.exp(score - lse_ref[pl.ds(2 * p + h, 1), :])
                d_att = nt(vh[h, rows, :], dmix[:, cols])
                d_score = (weight * (d_att - dsum[pl.ds(2 * p + h, 1), :])).astype(BF16)
                part_v = nn(weight.astype(BF16), dh[h])
                part_k = nn(d_score, qh[2 + h])
                d_v = part_v if d_v is None else d_v + part_v
                d_k = part_k if d_k is None else d_k + part_k
                dqt[...] += nn(kt[h, :, rows], d_score)
            dk_s[rows, cols] = d_k.astype(BF16)
            dv_s[rows, cols] = d_v.astype(BF16)
            return carry

        lax.fori_loop(0, tiles, tile_step, 0)
        dq_s[:, cols] = jnp.transpose(dqt[...]).astype(BF16)
        return carry

    lax.fori_loop(0, pairs, pair_step, 0)
    ggain_ref[...] = jnp.zeros_like(ggain_ref)

    def last(t, carry):
        rows = row_block(t, tile)
        permuted_store(turned, rows, normed_ref[rows, :], d // blocks)
        x = x_ref[rows, :].astype(F32)
        r = lax.rsqrt(jnp.mean(x * x, axis=-1, keepdims=True) + epsilon)
        dn = nt(dq_s[rows, :], wq_ref[...]) + nt(dk_s[rows, :], wk_ref[...]) + nt(dv_s[rows, :], wv_ref[...])
        scaled = dn * gain_ref[...]
        mean = jnp.mean(scaled * x, axis=-1, keepdims=True)
        gplots_ref[rows, :] = (dhid_ref[rows, :] + r * scaled - x * (r * r * r * mean)).astype(BF16)
        ggain_ref[...] += jnp.sum(dn * x * r, axis=0, keepdims=True)
        return carry

    lax.fori_loop(0, tiles, last, 0)
    weight_grads(gq_ref, dq_s)
    weight_grads(gk_ref, dk_s)
    weight_grads(gv_ref, dv_s)


def call(kernel, outs, scratch, args, scalars=1):
    return pl.pallas_call(
        kernel,
        out_shape=[jax.ShapeDtypeStruct(shape, dtype) for shape, dtype in outs],
        in_specs=[pl.BlockSpec(memory_space=pltpu.SMEM)] * scalars
        + [pl.BlockSpec(memory_space=pltpu.VMEM)] * (len(args) - scalars),
        out_specs=[pl.BlockSpec(memory_space=pltpu.VMEM)] * len(outs),
        scratch_shapes=scratch,
        compiler_params=pltpu.CompilerParams(vmem_limit_bytes=VMEM_BYTES),
    )(*args)


def unpermute(grad, rows):
    cols = grad.shape[1]
    return grad.reshape(2, 2, -1, rows, cols).transpose(2, 1, 0, 3, 4).reshape(-1, cols)


def body_plot(plots, plot_grid, query_weight, key_weight, value_weight, out_weight, gate_weight, up_weight, down_weight,
              gain_attn, gain_mlp, cotangent):
    rows, d = query_weight.shape
    ff = gate_weight.shape[1]
    rows_down = down_weight.shape[0]
    half = plots.shape[1]
    slots = 2 * half
    counts = plot_grid[:, 0] * plot_grid[:, 1]
    count = lax.dynamic_slice(counts, (lax.axis_index("narrow"),), (1,))
    act = lambda dtype=BF16: ((slots, d), dtype)
    vm = lambda shape, dtype=BF16: pltpu.VMEM(shape, dtype)
    fulls = [(16, rows, d)] * 4 + [(16, rows, ff)] * 2 + [(16, rows_down, d)]
    outs = [act(), act(), act(), act(), act(), ((128, slots), F32), act(F32), act(), act(), ((2, d), F32)]
    outs += [(shape, BF16) for shape in fulls]
    results = pl.pallas_call(
        gather_forward,
        out_shape=[jax.ShapeDtypeStruct(shape, dtype) for shape, dtype in outs],
        in_specs=[pl.BlockSpec(memory_space=pltpu.SMEM)] + [pl.BlockSpec(memory_space=pltpu.VMEM)] * 11,
        out_specs=[pl.BlockSpec(memory_space=pltpu.VMEM)] * 10 + [pl.BlockSpec(memory_space=pl.ANY)] * 7,
        scratch_shapes=[vm((2, slots, 128)), vm((2, slots, 128)), vm((2, slots, 256)), vm((slots, 128), F32)]
        + [vm(shape) for shape in fulls] + [vm((16, 8, 128), F32)]
        + [pltpu.SemaphoreType.DMA((8, 15)), pltpu.SemaphoreType.DMA((8, 16)), pltpu.SemaphoreType.DMA((4,)),
           pltpu.SemaphoreType.DMA((7,))],
        compiler_params=pltpu.CompilerParams(vmem_limit_bytes=VMEM_BYTES, collective_id=1, has_side_effects=True),
    )(count, plots, cotangent, gain_attn.reshape(1, -1), gain_mlp.reshape(1, -1), query_weight, key_weight, value_weight,
      out_weight, gate_weight, up_weight, down_weight)
    q, k, v, normed, mixed, lse, hidden, x, cot, gains = results[:10]
    wq, wk, wv, wo, wg, wu, wd = [w.reshape(-1, w.shape[2]) for w in results[10:]]
    output, dhid, g_down, g_gate, g_up, gg_mlp = call(
        mlp_both,
        [act(), act(F32), ((ff, d), BF16), ((d, ff), BF16), ((d, ff), BF16), ((1, d), F32)],
        [vm((d, slots)), vm((ff, slots)), vm((slots, ff)), vm((slots, ff))],
        (hidden, cot, gains[1:2], wg, wu, wd), 0,
    )
    gplots, g_q, g_k, g_v, g_out, gg_attn = call(
        attend_backward,
        [act(), ((d, d), BF16), ((d, d), BF16), ((d, d), BF16), ((d, d), BF16), ((1, d), F32)],
        [vm((slots, d)), vm((slots, d)), vm((128, slots), F32), vm((d, slots)), vm((4, slots, 128)), vm((2, slots, 128)),
         vm((2, slots, 128)), vm((2, slots, 128)), vm((2, 128, slots)), vm((slots, d)), vm((slots, d)), vm((slots, d)),
         vm((128, slots), F32)],
        (count, x, gains[0:1], wq, wk, wv, wo, q, k, v, normed, mixed, lse, dhid),
    )

    def reduce(grad, rows):
        part = lax.psum_scatter(unpermute(grad, rows), "wide", scatter_dimension=0, tiled=True)
        return lax.psum(part, "narrow").astype(F32)

    def reduce_gain(grad):
        total = lax.psum(grad[0], ("wide", "narrow"))
        return lax.dynamic_slice(total, (lax.axis_index("wide") * rows,), (rows,))

    back = lambda value: lax.all_to_all(value[None], "narrow", 1, 0, tiled=True)
    return (back(output), back(gplots), reduce(g_q, rows), reduce(g_k, rows), reduce(g_v, rows), reduce(g_out, rows),
            reduce(g_gate, rows), reduce(g_up, rows), reduce(g_down, rows_down), reduce_gain(gg_attn), reduce_gain(gg_mlp))


def body_for(mesh):
    plots_fit = mesh.shape["narrow"] == 2 and mesh.shape["wide"] == 16

    def body(plots, *rest):
        if plots_fit and plots.shape == (2, 512, HEADS * HEAD_DIM):
            return body_plot(plots, *rest)
        return body_general(plots, *rest)

    return body


def solution(mesh):
    return jax.shard_map(
        body_for(mesh),
        mesh=mesh,
        in_specs=(
            P("wide", "narrow", None),
            P("wide", None),
            P("wide", None),
            P("wide", None),
            P("wide", None),
            P("wide", None),
            P("wide", None),
            P("wide", None),
            P("wide", None),
            P("wide"),
            P("wide"),
            P("wide", "narrow", None),
        ),
        out_specs=(
            P("wide", "narrow", None),
            P("wide", "narrow", None),
            P("wide", None),
            P("wide", None),
            P("wide", None),
            P("wide", None),
            P("wide", None),
            P("wide", None),
            P("wide", None),
            P("wide"),
            P("wide"),
        ),
        check_vma=False,
    )
```

```python
import functools

import jax
import jax.numpy as jnp
from jax import lax
from jax.experimental import pallas as pl
from jax.experimental.pallas import tpu as pltpu
from jax.sharding import PartitionSpec as P

HEADS = 12
HEAD_DIM = 64


epsilon = 1e-06


def norm_rows(values, gain):
    return values * lax.rsqrt(jnp.mean(values * values, axis=-1, keepdims=True) + epsilon) * gain


def gated(gate_pre, up_pre):
    return jax.nn.gelu(gate_pre, approximate=True) * up_pre


def to_heads(tensor):
    return tensor.reshape(tensor.shape[0], tensor.shape[1], HEADS, HEAD_DIM).transpose(2, 0, 1, 3)


def from_heads(tensor):
    return tensor.transpose(1, 2, 0, 3).reshape(tensor.shape[1], tensor.shape[2], HEADS * HEAD_DIM)


def masked_scores(query_one, keys_one, valid):
    scores = jnp.einsum("pqe,pke->pqk", query_one, keys_one, preferred_element_type=jnp.float32)
    return jnp.where(valid[:, None, :], scores, -1e30)


def weight_grad(left, right):
    return jnp.einsum("psd,pse->de", left, right, preferred_element_type=jnp.float32)


def back_product(grad_rows, weight):
    return jnp.einsum("pse,de->psd", grad_rows, weight, preferred_element_type=jnp.float32)


def forward_pass(inputs, weights, valid):
    (
        query_weight,
        key_weight,
        value_weight,
        out_weight,
        gate_weight,
        up_weight,
        down_weight,
        gain_attn,
        gain_mlp,
    ) = weights
    normed = norm_rows(inputs, gain_attn.astype(jnp.float32)).astype(jnp.bfloat16)
    query = jnp.dot(normed, query_weight, preferred_element_type=jnp.float32).astype(jnp.bfloat16)
    keys_local = jnp.dot(normed, key_weight, preferred_element_type=jnp.float32).astype(
        jnp.bfloat16
    )
    values_local = jnp.dot(normed, value_weight, preferred_element_type=jnp.float32).astype(
        jnp.bfloat16
    )
    keys_all, values_all = (
        lax.all_gather(keys_local, "narrow", axis=1, tiled=True),
        lax.all_gather(values_local, "narrow", axis=1, tiled=True),
    )
    query_heads = to_heads(query)
    key_heads = to_heads(keys_all)
    value_heads = to_heads(values_all)

    def head_forward(operands):
        query_one, keys_one, values_one = operands
        scores = masked_scores(query_one, keys_one, valid)
        row_max = jnp.max(scores, axis=-1, keepdims=True)
        exponent = jnp.exp(scores - row_max)
        total = jnp.sum(exponent, axis=-1, keepdims=True)
        mixed = jnp.einsum(
            "pqk,pke->pqe",
            (exponent / total).astype(jnp.bfloat16),
            values_one,
            preferred_element_type=jnp.float32,
        )
        return (mixed.astype(jnp.bfloat16), (row_max + jnp.log(total))[..., 0])

    mixed_heads, log_total = lax.map(head_forward, (query_heads, key_heads, value_heads))
    attended = from_heads(mixed_heads)
    hidden_in = inputs + jnp.dot(attended, out_weight, preferred_element_type=jnp.float32)
    normed_mlp = norm_rows(hidden_in, gain_mlp.astype(jnp.float32)).astype(jnp.bfloat16)
    gate_pre = jnp.dot(normed_mlp, gate_weight, preferred_element_type=jnp.float32)
    up_pre = jnp.dot(normed_mlp, up_weight, preferred_element_type=jnp.float32)
    activated = gated(gate_pre, up_pre).astype(jnp.bfloat16)
    output = hidden_in + jnp.dot(activated, down_weight, preferred_element_type=jnp.float32)
    saved = (
        normed,
        query_heads,
        key_heads,
        value_heads,
        log_total,
        attended,
        hidden_in,
        normed_mlp,
        gate_pre,
        up_pre,
        activated,
    )
    return (output, saved)


def body_general(
    plots,
    plot_grid,
    query_weight,
    key_weight,
    value_weight,
    out_weight,
    gate_weight,
    up_weight,
    down_weight,
    gain_attn,
    gain_mlp,
    cotangent,
):
    shards = (
        query_weight,
        key_weight,
        value_weight,
        out_weight,
        gate_weight,
        up_weight,
        down_weight,
        gain_attn,
        gain_mlp,
    )
    inputs = plots.astype(jnp.float32)
    counts = plot_grid[:, 0] * plot_grid[:, 1]
    length = plots.shape[1] * lax.axis_size("narrow")
    valid = jnp.arange(length)[None, :] < counts[:, None]
    weights = (
        lax.all_gather(shards[0], "wide", axis=0, tiled=True),
        lax.all_gather(shards[1], "wide", axis=0, tiled=True),
        lax.all_gather(shards[2], "wide", axis=0, tiled=True),
        lax.all_gather(shards[3], "wide", axis=0, tiled=True),
        lax.all_gather(shards[4], "wide", axis=0, tiled=True),
        lax.all_gather(shards[5], "wide", axis=0, tiled=True),
        lax.all_gather(shards[6], "wide", axis=0, tiled=True),
        lax.all_gather(shards[7], "wide", axis=0, tiled=True),
        lax.all_gather(shards[8], "wide", axis=0, tiled=True),
    )
    output, saved = forward_pass(inputs, weights, valid)
    weights = (
        lax.all_gather(shards[0], "wide", axis=0, tiled=True),
        lax.all_gather(shards[1], "wide", axis=0, tiled=True),
        lax.all_gather(shards[2], "wide", axis=0, tiled=True),
        lax.all_gather(shards[3], "wide", axis=0, tiled=True),
        lax.all_gather(shards[4], "wide", axis=0, tiled=True),
        lax.all_gather(shards[5], "wide", axis=0, tiled=True),
        lax.all_gather(shards[6], "wide", axis=0, tiled=True),
        lax.all_gather(shards[7], "wide", axis=0, tiled=True),
        lax.all_gather(shards[8], "wide", axis=0, tiled=True),
    )
    rerun, saved = forward_pass(inputs, weights, valid)
    (
        normed,
        query_heads,
        key_heads,
        value_heads,
        log_total,
        attended,
        hidden_in,
        normed_mlp,
        gate_pre,
        up_pre,
        activated,
    ) = saved
    (
        full_query,
        full_key,
        full_value,
        full_out,
        full_gate,
        full_up,
        full_down,
        full_gain_attn,
        full_gain_mlp,
    ) = weights
    grad_output = cotangent.astype(jnp.float32)
    grad_branch = grad_output.astype(jnp.bfloat16)
    grad_down = weight_grad(activated, grad_branch)
    grad_act = back_product(grad_branch, full_down)
    gate_value, gate_pull = jax.vjp(gated, gate_pre, up_pre)
    grad_gate_pre, grad_up_pre = gate_pull(grad_act)
    grad_gate_low = grad_gate_pre.astype(jnp.bfloat16)
    grad_up_low = grad_up_pre.astype(jnp.bfloat16)
    grad_gate = weight_grad(normed_mlp, grad_gate_low)
    grad_up = weight_grad(normed_mlp, grad_up_low)
    grad_normed_mlp = back_product(grad_gate_low, full_gate) + back_product(grad_up_low, full_up)
    norm_value, norm_pull = jax.vjp(norm_rows, hidden_in, full_gain_mlp.astype(jnp.float32))
    grad_hidden_norm, grad_gain_mlp = norm_pull(grad_normed_mlp)
    grad_hidden = grad_output + grad_hidden_norm
    grad_hidden_low = grad_hidden.astype(jnp.bfloat16)
    grad_out = weight_grad(attended, grad_hidden_low)
    grad_attended = back_product(grad_hidden_low, full_out).astype(jnp.bfloat16)
    grad_heads = to_heads(grad_attended)

    def head_backward(operands):
        query_one, keys_one, values_one, log_one, grad_one = operands
        scores = masked_scores(query_one, keys_one, valid)
        attention = jnp.exp(scores - log_one[..., None])
        grad_soft = jnp.einsum(
            "pqe,pke->pqk", grad_one, values_one, preferred_element_type=jnp.float32
        )
        row_dot = jnp.sum(attention * grad_soft, axis=-1, keepdims=True)
        grad_scores = (attention * (grad_soft - row_dot)).astype(jnp.bfloat16)
        grad_query_one = jnp.einsum(
            "pqk,pke->pqe", grad_scores, keys_one, preferred_element_type=jnp.float32
        )
        grad_keys_one = jnp.einsum(
            "pqk,pqe->pke", grad_scores, query_one, preferred_element_type=jnp.float32
        )
        grad_values_one = jnp.einsum(
            "pqk,pqe->pke",
            attention.astype(jnp.bfloat16),
            grad_one,
            preferred_element_type=jnp.float32,
        )
        return (grad_query_one, grad_keys_one, grad_values_one)

    grad_query_heads, grad_key_heads, grad_value_heads = lax.map(
        head_backward, (query_heads, key_heads, value_heads, log_total, grad_heads)
    )
    grad_key_local, grad_value_local = (
        lax.psum_scatter(
            grad_key_heads.astype(jnp.bfloat16), "narrow", scatter_dimension=2, tiled=True
        ).astype(jnp.float32),
        lax.psum_scatter(
            grad_value_heads.astype(jnp.bfloat16), "narrow", scatter_dimension=2, tiled=True
        ).astype(jnp.float32),
    )
    grad_query_low = from_heads(grad_query_heads).astype(jnp.bfloat16)
    grad_key_low = from_heads(grad_key_local).astype(jnp.bfloat16)
    grad_value_low = from_heads(grad_value_local).astype(jnp.bfloat16)
    grad_query = weight_grad(normed, grad_query_low)
    grad_key = weight_grad(normed, grad_key_low)
    grad_value = weight_grad(normed, grad_value_low)
    grad_normed = (
        back_product(grad_query_low, full_query)
        + back_product(grad_key_low, full_key)
        + back_product(grad_value_low, full_value)
    )
    first_value, first_pull = jax.vjp(norm_rows, inputs, full_gain_attn.astype(jnp.float32))
    grad_input_norm, grad_gain_attn = first_pull(grad_normed)
    grad_plots = (grad_hidden + grad_input_norm).astype(jnp.bfloat16)
    owned = (
        lax.psum_scatter(
            grad_query.astype(jnp.bfloat16), "wide", scatter_dimension=0, tiled=True
        ).astype(jnp.float32),
        lax.psum_scatter(
            grad_key.astype(jnp.bfloat16), "wide", scatter_dimension=0, tiled=True
        ).astype(jnp.float32),
        lax.psum_scatter(
            grad_value.astype(jnp.bfloat16), "wide", scatter_dimension=0, tiled=True
        ).astype(jnp.float32),
        lax.psum_scatter(
            grad_out.astype(jnp.bfloat16), "wide", scatter_dimension=0, tiled=True
        ).astype(jnp.float32),
        lax.psum_scatter(
            grad_gate.astype(jnp.bfloat16), "wide", scatter_dimension=0, tiled=True
        ).astype(jnp.float32),
        lax.psum_scatter(
            grad_up.astype(jnp.bfloat16), "wide", scatter_dimension=0, tiled=True
        ).astype(jnp.float32),
        lax.psum_scatter(
            grad_down.astype(jnp.bfloat16), "wide", scatter_dimension=0, tiled=True
        ).astype(jnp.float32),
        lax.psum_scatter(
            grad_gain_attn.astype(jnp.bfloat16), "wide", scatter_dimension=0, tiled=True
        ).astype(jnp.float32),
        lax.psum_scatter(
            grad_gain_mlp.astype(jnp.bfloat16), "wide", scatter_dimension=0, tiled=True
        ).astype(jnp.float32),
    )
    summed = (
        lax.psum(owned[0].astype(jnp.bfloat16), "narrow").astype(jnp.float32),
        lax.psum(owned[1].astype(jnp.bfloat16), "narrow").astype(jnp.float32),
        lax.psum(owned[2].astype(jnp.bfloat16), "narrow").astype(jnp.float32),
        lax.psum(owned[3].astype(jnp.bfloat16), "narrow").astype(jnp.float32),
        lax.psum(owned[4].astype(jnp.bfloat16), "narrow").astype(jnp.float32),
        lax.psum(owned[5].astype(jnp.bfloat16), "narrow").astype(jnp.float32),
        lax.psum(owned[6].astype(jnp.bfloat16), "narrow").astype(jnp.float32),
        lax.psum(owned[7].astype(jnp.bfloat16), "narrow").astype(jnp.float32),
        lax.psum(owned[8].astype(jnp.bfloat16), "narrow").astype(jnp.float32),
    )
    return (
        output.astype(jnp.bfloat16),
        grad_plots,
        summed[0],
        summed[1],
        summed[2],
        summed[3],
        summed[4],
        summed[5],
        summed[6],
        summed[7],
        summed[8],
    )


F32, BF16 = jnp.float32, jnp.bfloat16
ROOT = 0.7978845608028654
CUBE = 0.044715
VMEM_BYTES = 60 << 20


def nn(left, right):
    return lax.dot_general(left, right, (((1,), (0,)), ((), ())), preferred_element_type=F32)


def nt(left, right):
    return lax.dot_general(left, right, (((1,), (1,)), ((), ())), preferred_element_type=F32)


def lanes_of(rows, width=128):
    return lax.broadcasted_iota(jnp.int32, (rows, width), 1)


def row_block(index, size):
    return pl.ds(pl.multiple_of(index * size, size), size)


def head_masks(pair, lane, flag):
    first = jnp.where(lane < 64, pair, jnp.where(lane == 64, flag, 0.0))
    second = jnp.where(lane >= 64, pair, jnp.where(lane == 0, flag, 0.0))
    return first.astype(BF16), second.astype(BF16)


MESH_ID = pl.DeviceIdType.MESH


class Place:
    def __init__(self):
        wide, self.y = lax.axis_index("wide"), lax.axis_index("narrow")
        self.z, self.x, self.c = wide // 4, (wide // 2) % 2, wide % 2
        self.wide = wide

    def block(self, z, x, c):
        return (z * 2 + x) * 2 + c

    def other_z(self, j):
        z = self.z
        return (z + 1 - 2 * (z % 2), (z + 2) % 4, 3 - z)[j]

    def to_z(self, j):
        return (self.block(self.other_z(j), self.x, self.c), self.y)

    def to_x(self):
        return (self.block(self.z, 1 - self.x, self.c), self.y)

    def to_core(self):
        return (self.block(self.z, self.x, 1 - self.c), self.y)

    def to_y(self):
        return (self.wide, 1 - self.y)

    def greet(self):
        barrier = pltpu.get_barrier_semaphore()
        partners = [self.to_z(0), self.to_z(1), self.to_z(2), self.to_x(), self.to_core(), self.to_y()]
        for partner in partners:
            pl.semaphore_signal(barrier, inc=1, device_id=partner, device_id_type=MESH_ID)
        pl.semaphore_wait(barrier, len(partners))


class Gather:
    def __init__(self, place, full, send, recv):
        self.place, self.full, self.sends, self.recvs = place, full, send, recv
        self.slot = 0

    def copy(self, block, target, slot):
        return pltpu.make_async_remote_copy(
            src_ref=self.full.at[block], dst_ref=self.full.at[block], send_sem=self.sends.at[slot],
            recv_sem=self.recvs.at[block], device_id=target, device_id_type=MESH_ID)

    def send(self, block, target):
        self.copy(block, target, self.slot).start()
        self.slot += 1

    def wait(self, block):
        self.copy(block, self.place.to_core(), 0).wait_recv()

    def start(self):
        p = self.place
        own = p.block(p.z, p.x, p.c)
        for j in (2, 1, 0):
            self.send(own, p.to_z(j))
        self.send(own, p.to_x())
        self.send(own, p.to_core())

    def pass_z(self, j):
        p = self.place
        block = p.block(p.other_z(j), p.x, p.c)
        self.wait(block)
        self.send(block, p.to_x())
        self.send(block, p.to_core())

    def pass_x(self, j):
        p = self.place
        block = p.block(p.z if j == 3 else p.other_z(j), 1 - p.x, p.c)
        self.wait(block)
        self.send(block, p.to_core())

    def end(self):
        p = self.place
        for z in range(4):
            for x in range(2):
                self.wait(p.block(z, x, 1 - p.c))

    def sent(self):
        for slot in range(15):
            self.copy(0, self.place.to_core(), slot).wait_send()


def gather_forward(count_ref, plots_ref, cot_ref, gain_a_ref, gain_m_ref, own_q, own_k, own_v, own_o, own_g, own_u, own_d,
                   q_ref, k_ref, v_ref, normed_ref, mixed_ref, lse_ref, hidden_ref, x_ref, cot_out, gains_ref,
                   out_q, out_k, out_v, out_o, out_g, out_u, out_d,
                   qh, kh, vh, lse_cols, wq, wk, wv, wo, wg, wu, wd, wgain, sends, recvs, half_sems, out_sems):
    half = plots_ref.shape[1]
    slots = 2 * half
    tile = 256
    tiles = slots // tile
    pairs = HEADS // 2
    d = plots_ref.shape[2]
    place = Place()
    fulls = (wgain, wq, wk, wv, wo, wg, wu, wd)
    for full, own in zip(fulls[1:], (own_q, own_k, own_v, own_o, own_g, own_u, own_d)):
        full[place.wide] = own[...]
    wgain[place.wide, 0:1, 0:own_q.shape[0]] = gain_a_ref[...].astype(F32)
    wgain[place.wide, 1:2, 0:own_q.shape[0]] = gain_m_ref[...].astype(F32)
    gathers = [Gather(place, full, sends.at[i], recvs.at[i]) for i, full in enumerate(fulls)]
    g_gain, g_q, g_k, g_v, g_o, g_g, g_u, g_d = gathers
    mine = pl.ds(pl.multiple_of(place.y * half, half), half)

    def half_copy(source, target, i):
        return pltpu.make_async_remote_copy(
            src_ref=source.at[1 - place.y], dst_ref=target.at[mine], send_sem=half_sems.at[2 * i],
            recv_sem=half_sems.at[2 * i + 1], device_id=place.to_y(), device_id_type=MESH_ID)

    place.greet()
    x_copy, cot_copy = half_copy(plots_ref, x_ref, 0), half_copy(cot_ref, cot_out, 1)
    x_copy.start()
    for g in (g_gain, g_q, g_k, g_v):
        g.start()
    x_ref[mine, :] = plots_ref[place.y]
    cot_out[mine, :] = cot_ref[place.y]

    def relay_z(g):
        for j in range(3):
            g.pass_z(j)

    def relay_x(g):
        for j in (3, 0, 1, 2):
            g.pass_x(j)

    relay_z(g_gain)
    relay_z(g_q)
    g_o.start()
    relay_z(g_k)
    g_g.start()
    relay_x(g_gain)
    relay_x(g_q)
    relay_z(g_v)
    g_gain.end()
    rows_own = own_q.shape[0]
    for w in range(16):
        for i in range(2):
            gains_ref[i:i + 1, w * rows_own:(w + 1) * rows_own] = wgain[w, i:i + 1, 0:rows_own]
    x_copy.wait()
    cot_copy.start()

    def normalise(t, carry):
        rows = row_block(t, tile)
        x = x_ref[rows, :].astype(F32)
        r = lax.rsqrt(jnp.mean(x * x, axis=-1, keepdims=True) + epsilon)
        normed_ref[rows, :] = (x * r * gains_ref[0:1, :]).astype(BF16)
        return carry

    lax.fori_loop(0, tiles, normalise, 0)

    def project(target, full):
        def step(t, carry):
            rows = row_block(t, tile)
            target[rows, :] = nn(normed_ref[rows, :], full[...].reshape(d, d)).astype(BF16)
            return carry

        lax.fori_loop(0, tiles, step, 0)

    relay_x(g_k)
    g_q.end()
    project(q_ref, wq)
    relay_x(g_v)
    g_k.end()
    project(k_ref, wk)
    relay_z(g_o)
    g_u.start()
    g_v.end()
    project(v_ref, wv)

    count = count_ref[0]
    lane = lanes_of(slots)
    slot = lax.broadcasted_iota(jnp.int32, (slots, 128), 0)
    bias = jnp.where(slot < count, 0.0, -1e30)
    lse_cols[...] = jnp.zeros_like(lse_cols)
    for h in range(2):
        vh[h, :, 128:] = jnp.ones((slots, 128), BF16)
    hooks = {
        0: [lambda: g_g.pass_z(0)], 1: [lambda: relay_x(g_o)], 2: [lambda: g_g.pass_z(1)], 4: [lambda: g_g.pass_z(2), lambda: g_d.start()],
        5: [lambda: g_g.pass_x(3)], 6: [lambda: g_g.pass_x(0)], 7: [lambda: g_g.pass_x(1)], 8: [lambda: g_u.pass_z(0)], 9: [lambda: g_g.pass_x(2)],
        10: [lambda: g_u.pass_z(1)], 13: [lambda: g_u.pass_z(2)], 14: [lambda: g_u.pass_x(3)], 15: [lambda: g_u.pass_x(0)],
        16: [lambda: g_d.pass_z(0)], 17: [lambda: g_u.pass_x(1)], 19: [lambda: g_d.pass_z(1), lambda: g_u.pass_x(2)],
        23: [lambda: g_d.pass_z(2)],
    }

    def step(s, carry):
        p, t = s // tiles, s % tiles
        cols = row_block(p, 128)
        for when, events in hooks.items():
            @pl.when(s == when)
            def _():
                for event in events:
                    event()

        @pl.when(t == 0)
        def _():
            kh[0], kh[1] = head_masks(k_ref[:, cols].astype(F32), lane, bias)
            qp = q_ref[:, cols].astype(F32)
            qh[0] = jnp.where(lane == 64, 1.0, qp).astype(BF16)
            qh[1] = jnp.where(lane == 0, 1.0, qp).astype(BF16)
            vh[0, :, :128], vh[1, :, :128] = head_masks(v_ref[:, cols].astype(F32), lane, 0.0)

        rows = row_block(t, tile)
        total = None
        cols_out = lse_cols[rows, :]
        for h in range(2):
            score = nt(qh[h, rows, :], kh[h])
            top = jnp.max(score, axis=1, keepdims=True)
            weight = jnp.exp(score - top).astype(BF16)
            acc = nn(weight, vh[h])
            part = acc[:, :128] / acc[:, 128:]
            total = part if total is None else total + part
            cols_out = jnp.where(lanes_of(tile) == 2 * p + h, top + jnp.log(acc[:, 128:]), cols_out)
        mixed_ref[rows, cols] = total.astype(BF16)
        lse_cols[rows, :] = cols_out
        return carry

    lax.fori_loop(0, pairs * tiles, step, 0)
    relay_x(g_d)
    g_o.end()

    def project_out(t, carry):
        rows = row_block(t, tile)
        hidden_ref[rows, :] = x_ref[rows, :].astype(F32) + nn(mixed_ref[rows, :], wo[...].reshape(d, d))
        lse_ref[:, rows] = jnp.transpose(lse_cols[rows, :])
        return carry

    lax.fori_loop(0, tiles, project_out, 0)
    g_g.end()
    g_u.end()
    g_d.end()
    outs = [pltpu.make_async_copy(full, out, out_sems.at[i])
            for i, (full, out) in enumerate(zip(fulls[1:], (out_q, out_k, out_v, out_o, out_g, out_u, out_d)))]
    for copy in outs:
        copy.start()
    for g in gathers:
        g.sent()
    cot_copy.wait()
    for copy in outs:
        copy.wait()


class Scatter:
    def __init__(self, place, mine, base, theirs, recv_c, recv_x, recv_z, recv_y, out, send, recv):
        self.place, self.mine, self.base, self.theirs = place, mine, base, theirs
        self.recv_c, self.recv_x, self.recv_z, self.recv_y, self.out = recv_c, recv_x, recv_z, recv_y, out
        self.sends, self.recvs = send, recv

    def copy(self, stage, source, target, device):
        return pltpu.make_async_remote_copy(
            src_ref=source, dst_ref=target, send_sem=self.sends.at[stage], recv_sem=self.recvs.at[stage],
            device_id=device, device_id_type=MESH_ID)

    def core_copy(self):
        return self.copy(0, self.theirs, self.recv_c, self.place.to_core())

    def x_copy(self):
        p = self.place
        return self.copy(1, self.mine.at[pl.ds(self.base + (1 - p.x) * 4, 4)], self.recv_x, p.to_x())

    def z_copy(self, j):
        p = self.place
        return self.copy(2 + j, self.mine.at[self.base + p.x * 4 + p.other_z(j)], self.recv_z.at[j], p.to_z(j))

    def y_copy(self):
        p = self.place
        return self.copy(5, self.mine.at[self.base + p.x * 4 + p.z], self.recv_y, p.to_y())

    def start(self):
        self.core_copy().start()

    def add_core(self):
        self.core_copy().wait_recv()

        def step(i, carry):
            self.mine[self.base + i] = self.mine[self.base + i] + self.recv_c[i]
            return carry

        lax.fori_loop(0, 8, step, 0)

    def send_x(self):
        self.x_copy().start()

    def add_x(self):
        self.x_copy().wait_recv()
        first = self.base + self.place.x * 4

        def step(i, carry):
            self.mine[first + i] = self.mine[first + i] + self.recv_x[i]
            return carry

        lax.fori_loop(0, 4, step, 0)
        for j in (2, 1, 0):
            self.z_copy(j).start()

    def add_z(self):
        for j in range(3):
            self.z_copy(j).wait_recv()
        own = self.base + self.place.x * 4 + self.place.z
        total = self.mine[own].astype(F32)
        for j in range(3):
            total = total + self.recv_z[j].astype(F32)
        self.mine[own] = total.astype(self.mine.dtype)
        self.y_copy().start()

    def add_y(self):
        self.y_copy().wait_recv()
        own = self.base + self.place.x * 4 + self.place.z
        self.out[...] = self.mine[own].astype(F32) + self.recv_y[...].astype(F32)

    def sent(self):
        self.core_copy().wait_send()
        self.x_copy().wait_send()
        for j in range(3):
            self.z_copy(j).wait_send()
        self.y_copy().wait_send()


def permuted_store(target, index, value, block):
    blocks = target.shape[0] // block
    deep = blocks // 4
    turned = jnp.transpose(value)
    for w in range(blocks):
        z, x, c = w // 4, (w // 2) % 2, w % 2
        place = (c * 2 + x) * deep + z
        target[place * block:(place + 1) * block, index] = turned[w * block:(w + 1) * block, :]


def mlp_both(hidden_ref, cot_ref, gain_ref, wg_ref, wu_ref, wd_ref,
             out_ref, dhid_ref, gdown_ref, ggate_ref, gup_ref, ggain_ref,
             nmt, actt, dg_s, du_s):
    slots, d = hidden_ref.shape
    ff = wg_ref.shape[1]
    tile = 128
    blocks = 16
    ggain_ref[...] = jnp.zeros_like(ggain_ref)

    def step(t, carry):
        rows = row_block(t, tile)
        hidden = hidden_ref[rows, :]
        r = lax.rsqrt(jnp.mean(hidden * hidden, axis=-1, keepdims=True) + epsilon)
        gain = gain_ref[...]
        normed = (hidden * r * gain).astype(BF16)
        permuted_store(nmt, rows, normed, d // blocks)
        gate_pre = nn(normed, wg_ref[...])
        up_pre = nn(normed, wu_ref[...])
        square = gate_pre * gate_pre
        inner = ROOT * gate_pre * (1.0 + CUBE * square)
        th = jnp.tanh(inner)
        half = 0.5 * (1.0 + th)
        gelu = gate_pre * half
        slope = half + 0.5 * gate_pre * (1.0 - th * th) * (ROOT * (1.0 + 3.0 * CUBE * square))
        act = (gelu * up_pre).astype(BF16)
        permuted_store(actt, rows, act, ff // blocks)
        out_ref[rows, :] = (hidden + nn(act, wd_ref[...])).astype(BF16)
        dy = cot_ref[rows, :]
        d_act = nt(dy, wd_ref[...])
        dg = (d_act * up_pre * slope).astype(BF16)
        du = (d_act * gelu).astype(BF16)
        dg_s[rows, :] = dg
        du_s[rows, :] = du
        dn = nt(dg, wg_ref[...]) + nt(du, wu_ref[...])
        scaled = dn * gain
        mean = jnp.mean(scaled * hidden, axis=-1, keepdims=True)
        dhid_ref[rows, :] = dy.astype(F32) + r * scaled - hidden * (r * r * r * mean)
        ggain_ref[...] += jnp.sum(dn * hidden * r, axis=0, keepdims=True)
        return carry

    lax.fori_loop(0, slots // tile, step, 0)

    def down_step(n, carry):
        cols = row_block(n, 128)
        gdown_ref[:, cols] = nn(actt[...], cot_ref[:, cols]).astype(BF16)
        return carry

    lax.fori_loop(0, d // 128, down_step, 0)

    def gate_step(n, carry):
        cols = row_block(n, 256)
        ggate_ref[:, cols] = nn(nmt[...], dg_s[:, cols]).astype(BF16)
        gup_ref[:, cols] = nn(nmt[...], du_s[:, cols]).astype(BF16)
        return carry

    lax.fori_loop(0, ff // 256, gate_step, 0)


def scatter_backward(count_ref, x_hbm, gains_ref, wq_hbm, wk_hbm, wv_hbm, wo_hbm, q_hbm, k_hbm, v_hbm, mixed_hbm, lse_ref,
                     dhid_hbm, block_hbm, gdown_hbm, ggate_hbm, gup_hbm, gmlp_ref,
                     block_out, gplots_out, sum_q, sum_k, sum_v, sum_o, sum_g, sum_u, sum_d, sum_gain,
                     x_s, wq, wk, wv, wo, q_s, k_s, v_s, mixed_s, dhid_s, dhl, dmix, dsum, mixed_t, normed_t, ggain,
                     qh, kh, vh, dh, kt, dqt, own_d, own_g, own_u, own_gain, gq, gk, gv, go,
                     c_d, c_g, c_u, c_q, c_k, c_v, c_o, c_gain, x_d, x_g, x_u, x_q, x_k, x_v, x_o, x_gain,
                     z_d, z_g, z_u, z_q, z_k, z_v, z_o, z_gain, y_d, y_g, y_u, y_q, y_k, y_v, y_o, y_gain,
                     sends, recvs, load_sems, out_sems):
    slots, d = x_s.shape
    half = slots // 2
    tile = 256
    tiles = slots // tile
    pairs = HEADS // 2
    rows_own = d // 16
    place = Place()
    ours = pl.ds(place.c * 8, 8)
    pairs_in = ((dhid_hbm, dhid_s), (wo_hbm, wo), (mixed_hbm, mixed_s), (x_hbm, x_s), (gdown_hbm.at[ours], own_d),
                (ggate_hbm.at[ours], own_g), (gup_hbm.at[ours], own_u), (q_hbm, q_s), (k_hbm, k_s), (v_hbm, v_s),
                (wq_hbm, wq), (wk_hbm, wk), (wv_hbm, wv))
    loads = [pltpu.make_async_copy(a, b, load_sems.at[i]) for i, (a, b) in enumerate(pairs_in)]
    for load in loads:
        load.start()
    theirs = pl.ds((1 - place.c) * 8, 8)

    def scatter(i, mine, base, other, c, x, z, y, out):
        return Scatter(place, mine, base, other, c, x, z, y, out, sends.at[i], recvs.at[i])

    s_d = scatter(0, own_d, 0, gdown_hbm.at[theirs], c_d, x_d, z_d, y_d, sum_d)
    s_g = scatter(1, own_g, 0, ggate_hbm.at[theirs], c_g, x_g, z_g, y_g, sum_g)
    s_u = scatter(2, own_u, 0, gup_hbm.at[theirs], c_u, x_u, z_u, y_u, sum_u)
    base = place.c * 8
    s_o = scatter(3, go, base, go.at[theirs], c_o, x_o, z_o, y_o, sum_o)
    s_q = scatter(4, gq, base, gq.at[theirs], c_q, x_q, z_q, y_q, sum_q)
    s_k = scatter(5, gk, base, gk.at[theirs], c_k, x_k, z_k, y_k, sum_k)
    s_v = scatter(6, gv, base, gv.at[theirs], c_v, x_v, z_v, y_v, sum_v)
    s_n = scatter(7, own_gain, base, own_gain.at[theirs], c_gain, x_gain, z_gain, y_gain, sum_gain)
    mine = pl.ds(pl.multiple_of(place.y * half, half), half)
    other = pl.ds(pl.multiple_of((1 - place.y) * half, half), half)

    def half_out(source, target, i):
        far = pltpu.make_async_remote_copy(
            src_ref=source.at[other], dst_ref=target.at[place.y], send_sem=out_sems.at[3 * i],
            recv_sem=out_sems.at[3 * i + 1], device_id=place.to_y(), device_id_type=MESH_ID)
        near = pltpu.make_async_copy(source.at[mine], target.at[place.y], out_sems.at[3 * i + 2])
        return far, near

    place.greet()
    block_far, block_near = half_out(block_hbm, block_out, 0)
    s_d.start()
    block_far.start()
    s_g.start()
    s_u.start()
    block_near.start()

    head_row = lax.broadcasted_iota(jnp.int32, (128, d), 0)
    head_col = lax.broadcasted_iota(jnp.int32, (128, d), 1)
    pick = jnp.where(head_col // HEAD_DIM == head_row, 1.0, 0.0).astype(BF16)
    for i in range(5):
        loads[i].wait()
    s_d.add_core()
    s_d.send_x()

    def first(t, carry):
        rows = row_block(t, tile)
        low = dhid_s[rows, :].astype(BF16)
        dhl[rows, :] = low
        grad = nt(low, wo[...].reshape(d, d)).astype(BF16)
        dmix[rows, :] = grad
        mixed = mixed_s[rows, :]
        prod = grad.astype(F32) * mixed.astype(F32)
        high = prod.astype(BF16)
        rest = (prod - high.astype(F32)).astype(BF16)
        dsum[:, rows] = nt(pick, high) + nt(pick, rest)
        permuted_store(mixed_t, rows, mixed, rows_own)
        x = x_s[rows, :].astype(F32)
        r = lax.rsqrt(jnp.mean(x * x, axis=-1, keepdims=True) + epsilon)
        permuted_store(normed_t, rows, (x * r * gains_ref[0:1, :]).astype(BF16), rows_own)
        return carry

    lax.fori_loop(0, tiles, first, 0)

    def weight_grads(target, left, right):
        def step(n, carry):
            cols = row_block(n, 256)
            target[:, :, cols] = nn(left[...], right[:, cols]).astype(BF16).reshape(16, rows_own, 256)
            return carry

        lax.fori_loop(0, d // 256, step, 0)

    weight_grads(go, mixed_t, dhl)
    s_o.start()
    for load in loads[5:]:
        load.wait()
    s_g.add_core()
    s_u.add_core()
    s_o.add_core()
    count = count_ref[0]
    lane = lanes_of(slots)
    slot = lax.broadcasted_iota(jnp.int32, (slots, 128), 0)
    bias = jnp.where(slot < count, 0.0, -1e30)
    hooks = {
        6: [s_g.send_x], 7: [s_d.add_x], 13: [s_o.send_x], 14: [s_g.add_x], 16: [s_d.add_z, s_u.send_x],
        17: [s_o.add_x], 19: [s_d.add_y], 22: [s_g.add_z],
    }

    def step(s, carry):
        p, t = s // tiles, s % tiles
        cols = row_block(p, 128)
        for when, events in hooks.items():
            @pl.when(s == when)
            def _():
                for event in events:
                    event()

        @pl.when(t == 0)
        def _():
            kp = k_s[:, cols].astype(F32)
            kh[0], kh[1] = head_masks(kp, lane, bias)
            for h in range(2):
                own = (lane < 64) if h == 0 else (lane >= 64)
                kt[h] = jnp.transpose(jnp.where(own, kp, 0.0)).astype(BF16)
            qp = q_s[:, cols].astype(F32)
            qh[0] = jnp.where(lane == 64, 1.0, qp).astype(BF16)
            qh[1] = jnp.where(lane == 0, 1.0, qp).astype(BF16)
            qh[2], qh[3] = head_masks(qp, lane, 0.0)
            vh[0], vh[1] = head_masks(v_s[:, cols].astype(F32), lane, 0.0)
            dh[0], dh[1] = head_masks(dmix[:, cols].astype(F32), lane, 0.0)
            dqt[...] = jnp.zeros_like(dqt)

        rows = row_block(t, tile)
        d_k = d_v = None
        for h in range(2):
            score = nt(kh[h, rows, :], qh[h])
            weight = jnp.exp(score - lse_ref[pl.ds(2 * p + h, 1), :])
            d_att = nt(vh[h, rows, :], dmix[:, cols])
            d_score = (weight * (d_att - dsum[pl.ds(2 * p + h, 1), :])).astype(BF16)
            part_v = nn(weight.astype(BF16), dh[h])
            part_k = nn(d_score, qh[2 + h])
            d_v = part_v if d_v is None else d_v + part_v
            d_k = part_k if d_k is None else d_k + part_k
            dqt[...] += nn(kt[h, :, rows], d_score)
        k_s[rows, cols] = d_k.astype(BF16)
        v_s[rows, cols] = d_v.astype(BF16)

        @pl.when(t == tiles - 1)
        def _():
            q_s[:, cols] = jnp.transpose(dqt[...]).astype(BF16)

        return carry

    lax.fori_loop(0, pairs * tiles, step, 0)
    for target, right, out in ((gq, q_s, s_q), (gk, k_s, s_k), (gv, v_s, s_v)):
        weight_grads(target, normed_t, right)
        out.start()
    s_u.add_x()
    for s in (s_q, s_k, s_v):
        s.add_core()
        s.send_x()
    ggain[...] = jnp.zeros_like(ggain)
    gplots = dhl

    def last(i, carry):
        t = (i + (tiles // 2) * (1 - place.y)) % tiles
        rows = row_block(t, tile)
        x = x_s[rows, :].astype(F32)
        r = lax.rsqrt(jnp.mean(x * x, axis=-1, keepdims=True) + epsilon)
        dn = (nt(q_s[rows, :], wq[...].reshape(d, d)) + nt(k_s[rows, :], wk[...].reshape(d, d))
              + nt(v_s[rows, :], wv[...].reshape(d, d)))
        scaled = dn * gains_ref[0:1, :]
        mean = jnp.mean(scaled * x, axis=-1, keepdims=True)
        gplots[rows, :] = (dhid_s[rows, :] + r * scaled - x * (r * r * r * mean)).astype(BF16)
        ggain[...] += jnp.sum(dn * x * r, axis=0, keepdims=True)
        return carry

    gplots_far, gplots_near = half_out(gplots, gplots_out, 1)
    lax.fori_loop(0, tiles // 2, last, 0)
    gplots_far.start()
    s_o.add_z()
    lax.fori_loop(tiles // 2, tiles, last, 0)
    gplots_near.start()
    for w in range(16):
        z, x, c = w // 4, (w // 2) % 2, w % 2
        spot = (c * 2 + x) * 4 + z
        cols = slice(w * rows_own, (w + 1) * rows_own)
        own_gain[spot, 0:1, 0:rows_own] = ggain[0:1, cols]
        own_gain[spot, 1:2, 0:rows_own] = gmlp_ref[0:1, cols]
    s_n.start()
    s_u.add_z()
    s_n.add_core()
    s_n.send_x()
    for s in (s_q, s_k, s_v, s_n):
        s.add_x()
    s_g.add_y()
    s_o.add_y()
    for s in (s_q, s_k, s_v, s_n):
        s.add_z()
    for s in (s_u, s_q, s_k, s_v, s_n):
        s.add_y()
    for s in (s_d, s_g, s_u, s_o, s_q, s_k, s_v, s_n):
        s.sent()
    block_far.wait()
    block_near.wait()
    gplots_far.wait()
    gplots_near.wait()


def call(kernel, outs, scratch, args, scalars=1):
    return pl.pallas_call(
        kernel,
        out_shape=[jax.ShapeDtypeStruct(shape, dtype) for shape, dtype in outs],
        in_specs=[pl.BlockSpec(memory_space=pltpu.SMEM)] * scalars
        + [pl.BlockSpec(memory_space=pltpu.VMEM)] * (len(args) - scalars),
        out_specs=[pl.BlockSpec(memory_space=pltpu.VMEM)] * len(outs),
        scratch_shapes=scratch,
        compiler_params=pltpu.CompilerParams(vmem_limit_bytes=VMEM_BYTES),
    )(*args)


def body_plot(plots, plot_grid, query_weight, key_weight, value_weight, out_weight, gate_weight, up_weight, down_weight,
              gain_attn, gain_mlp, cotangent):
    rows, d = query_weight.shape
    ff = gate_weight.shape[1]
    rows_down = down_weight.shape[0]
    half = plots.shape[1]
    slots = 2 * half
    counts = plot_grid[:, 0] * plot_grid[:, 1]
    count = lax.dynamic_slice(counts, (lax.axis_index("narrow"),), (1,))
    act = lambda dtype=BF16: ((slots, d), dtype)
    vm = lambda shape, dtype=BF16: pltpu.VMEM(shape, dtype)
    fulls = [(16, rows, d)] * 4 + [(16, rows, ff)] * 2 + [(16, rows_down, d)]
    outs = [act(), act(), act(), act(), act(), ((128, slots), F32), act(F32), act(), act(), ((2, d), F32)]
    outs += [(shape, BF16) for shape in fulls]
    results = pl.pallas_call(
        gather_forward,
        out_shape=[jax.ShapeDtypeStruct(shape, dtype) for shape, dtype in outs],
        in_specs=[pl.BlockSpec(memory_space=pltpu.SMEM)] + [pl.BlockSpec(memory_space=pltpu.VMEM)] * 11,
        out_specs=[pl.BlockSpec(memory_space=pltpu.VMEM)] * 10 + [pl.BlockSpec(memory_space=pl.ANY)] * 7,
        scratch_shapes=[vm((2, slots, 128)), vm((2, slots, 128)), vm((2, slots, 256)), vm((slots, 128), F32)]
        + [vm(shape) for shape in fulls] + [vm((16, 8, 128), F32)]
        + [pltpu.SemaphoreType.DMA((8, 15)), pltpu.SemaphoreType.DMA((8, 16)), pltpu.SemaphoreType.DMA((4,)),
           pltpu.SemaphoreType.DMA((7,))],
        compiler_params=pltpu.CompilerParams(vmem_limit_bytes=VMEM_BYTES, collective_id=1, has_side_effects=True),
    )(count, plots, cotangent, gain_attn.reshape(1, -1), gain_mlp.reshape(1, -1), query_weight, key_weight, value_weight,
      out_weight, gate_weight, up_weight, down_weight)
    q, k, v, normed, mixed, lse, hidden, x, cot, gains = results[:10]
    wq, wk, wv, wo = results[10:14]
    wg, wu, wd = [w.reshape(-1, w.shape[2]) for w in results[14:]]
    output, dhid, g_down, g_gate, g_up, gg_mlp = call(
        mlp_both,
        [act(), act(F32), ((ff, d), BF16), ((d, ff), BF16), ((d, ff), BF16), ((1, d), F32)],
        [vm((d, slots)), vm((ff, slots)), vm((slots, ff)), vm((slots, ff))],
        (hidden, cot, gains[1:2], wg, wu, wd), 0,
    )
    shapes = [(rows_down, d), (rows, ff), (rows, ff), (rows, d), (rows, d), (rows, d), (rows, d)]
    scatters = shapes + [(8, 128)]
    dtypes = [BF16] * 7 + [F32]
    spaces = [pl.BlockSpec(memory_space=pltpu.SMEM), pl.BlockSpec(memory_space=pl.ANY), pl.BlockSpec(memory_space=pltpu.VMEM)]
    spaces += [pl.BlockSpec(memory_space=pl.ANY)] * 8 + [pl.BlockSpec(memory_space=pltpu.VMEM)]
    spaces += [pl.BlockSpec(memory_space=pl.ANY)] * 5 + [pl.BlockSpec(memory_space=pltpu.VMEM)]
    sums = [(rows, d)] * 4 + [(rows, ff)] * 2 + [(rows_down, d), (8, 128)]
    big = lambda dtype=BF16: pltpu.VMEM((slots, d), dtype)
    full = lambda: vm((16, rows, d))
    stages = lambda lead: [vm(lead + shape, dtype) for shape, dtype in zip(scatters, dtypes)]
    results = pl.pallas_call(
        scatter_backward,
        out_shape=[jax.ShapeDtypeStruct(plots.shape, BF16)] * 2 + [jax.ShapeDtypeStruct(shape, F32) for shape in sums],
        in_specs=spaces,
        out_specs=[pl.BlockSpec(memory_space=pl.ANY)] * 2 + [pl.BlockSpec(memory_space=pltpu.VMEM)] * 8,
        scratch_shapes=[big(), full(), full(), full(), full(), big(), big(), big(), big(), big(F32), big(), big(),
                        vm((128, slots), F32), vm((d, slots)), vm((d, slots)), vm((1, d), F32),
                        vm((4, slots, 128)), vm((2, slots, 128)), vm((2, slots, 128)), vm((2, slots, 128)),
                        vm((2, 128, slots)), vm((128, slots), F32),
                        vm((8, rows_down, d)), vm((8, rows, ff)), vm((8, rows, ff)), vm((16, 8, 128), F32),
                        full(), full(), full(), full()]
        + stages((8,)) + stages((4,)) + stages((3,)) + stages(())
        + [pltpu.SemaphoreType.DMA((8, 6)), pltpu.SemaphoreType.DMA((8, 6)), pltpu.SemaphoreType.DMA((13,)),
           pltpu.SemaphoreType.DMA((6,))],
        compiler_params=pltpu.CompilerParams(vmem_limit_bytes=VMEM_BYTES, collective_id=2, has_side_effects=True),
    )(count, x, gains, wq, wk, wv, wo, q, k, v, mixed, lse, dhid, output, g_down.reshape(16, rows_down, d),
      g_gate.reshape(16, rows, ff), g_up.reshape(16, rows, ff), gg_mlp)
    return (*results[:9], results[9][0, :rows], results[9][1, :rows])


def body_for(mesh):
    plots_fit = mesh.shape["narrow"] == 2 and mesh.shape["wide"] == 16

    def body(plots, *rest):
        if plots_fit and plots.shape == (2, 512, HEADS * HEAD_DIM):
            return body_plot(plots, *rest)
        return body_general(plots, *rest)

    return body


def solution(mesh):
    return jax.shard_map(
        body_for(mesh),
        mesh=mesh,
        in_specs=(
            P("wide", "narrow", None),
            P("wide", None),
            P("wide", None),
            P("wide", None),
            P("wide", None),
            P("wide", None),
            P("wide", None),
            P("wide", None),
            P("wide", None),
            P("wide"),
            P("wide"),
            P("wide", "narrow", None),
        ),
        out_specs=(
            P("wide", "narrow", None),
            P("wide", "narrow", None),
            P("wide", None),
            P("wide", None),
            P("wide", None),
            P("wide", None),
            P("wide", None),
            P("wide", None),
            P("wide", None),
            P("wide"),
            P("wide"),
        ),
        check_vma=False,
    )
```

```python
import functools

import jax
import jax.numpy as jnp
from jax import lax
from jax.experimental import pallas as pl
from jax.experimental.pallas import tpu as pltpu
from jax.sharding import PartitionSpec as P

HEADS = 12
HEAD_DIM = 64


epsilon = 1e-06


def norm_rows(values, gain):
    return values * lax.rsqrt(jnp.mean(values * values, axis=-1, keepdims=True) + epsilon) * gain


def gated(gate_pre, up_pre):
    return jax.nn.gelu(gate_pre, approximate=True) * up_pre


def to_heads(tensor):
    return tensor.reshape(tensor.shape[0], tensor.shape[1], HEADS, HEAD_DIM).transpose(2, 0, 1, 3)


def from_heads(tensor):
    return tensor.transpose(1, 2, 0, 3).reshape(tensor.shape[1], tensor.shape[2], HEADS * HEAD_DIM)


def masked_scores(query_one, keys_one, valid):
    scores = jnp.einsum("pqe,pke->pqk", query_one, keys_one, preferred_element_type=jnp.float32)
    return jnp.where(valid[:, None, :], scores, -1e30)


def weight_grad(left, right):
    return jnp.einsum("psd,pse->de", left, right, preferred_element_type=jnp.float32)


def back_product(grad_rows, weight):
    return jnp.einsum("pse,de->psd", grad_rows, weight, preferred_element_type=jnp.float32)


def forward_pass(inputs, weights, valid):
    (
        query_weight,
        key_weight,
        value_weight,
        out_weight,
        gate_weight,
        up_weight,
        down_weight,
        gain_attn,
        gain_mlp,
    ) = weights
    normed = norm_rows(inputs, gain_attn.astype(jnp.float32)).astype(jnp.bfloat16)
    query = jnp.dot(normed, query_weight, preferred_element_type=jnp.float32).astype(jnp.bfloat16)
    keys_local = jnp.dot(normed, key_weight, preferred_element_type=jnp.float32).astype(
        jnp.bfloat16
    )
    values_local = jnp.dot(normed, value_weight, preferred_element_type=jnp.float32).astype(
        jnp.bfloat16
    )
    keys_all, values_all = (
        lax.all_gather(keys_local, "narrow", axis=1, tiled=True),
        lax.all_gather(values_local, "narrow", axis=1, tiled=True),
    )
    query_heads = to_heads(query)
    key_heads = to_heads(keys_all)
    value_heads = to_heads(values_all)

    def head_forward(operands):
        query_one, keys_one, values_one = operands
        scores = masked_scores(query_one, keys_one, valid)
        row_max = jnp.max(scores, axis=-1, keepdims=True)
        exponent = jnp.exp(scores - row_max)
        total = jnp.sum(exponent, axis=-1, keepdims=True)
        mixed = jnp.einsum(
            "pqk,pke->pqe",
            (exponent / total).astype(jnp.bfloat16),
            values_one,
            preferred_element_type=jnp.float32,
        )
        return (mixed.astype(jnp.bfloat16), (row_max + jnp.log(total))[..., 0])

    mixed_heads, log_total = lax.map(head_forward, (query_heads, key_heads, value_heads))
    attended = from_heads(mixed_heads)
    hidden_in = inputs + jnp.dot(attended, out_weight, preferred_element_type=jnp.float32)
    normed_mlp = norm_rows(hidden_in, gain_mlp.astype(jnp.float32)).astype(jnp.bfloat16)
    gate_pre = jnp.dot(normed_mlp, gate_weight, preferred_element_type=jnp.float32)
    up_pre = jnp.dot(normed_mlp, up_weight, preferred_element_type=jnp.float32)
    activated = gated(gate_pre, up_pre).astype(jnp.bfloat16)
    output = hidden_in + jnp.dot(activated, down_weight, preferred_element_type=jnp.float32)
    saved = (
        normed,
        query_heads,
        key_heads,
        value_heads,
        log_total,
        attended,
        hidden_in,
        normed_mlp,
        gate_pre,
        up_pre,
        activated,
    )
    return (output, saved)


def body_general(
    plots,
    plot_grid,
    query_weight,
    key_weight,
    value_weight,
    out_weight,
    gate_weight,
    up_weight,
    down_weight,
    gain_attn,
    gain_mlp,
    cotangent,
):
    shards = (
        query_weight,
        key_weight,
        value_weight,
        out_weight,
        gate_weight,
        up_weight,
        down_weight,
        gain_attn,
        gain_mlp,
    )
    inputs = plots.astype(jnp.float32)
    counts = plot_grid[:, 0] * plot_grid[:, 1]
    length = plots.shape[1] * lax.axis_size("narrow")
    valid = jnp.arange(length)[None, :] < counts[:, None]
    weights = (
        lax.all_gather(shards[0], "wide", axis=0, tiled=True),
        lax.all_gather(shards[1], "wide", axis=0, tiled=True),
        lax.all_gather(shards[2], "wide", axis=0, tiled=True),
        lax.all_gather(shards[3], "wide", axis=0, tiled=True),
        lax.all_gather(shards[4], "wide", axis=0, tiled=True),
        lax.all_gather(shards[5], "wide", axis=0, tiled=True),
        lax.all_gather(shards[6], "wide", axis=0, tiled=True),
        lax.all_gather(shards[7], "wide", axis=0, tiled=True),
        lax.all_gather(shards[8], "wide", axis=0, tiled=True),
    )
    output, saved = forward_pass(inputs, weights, valid)
    weights = (
        lax.all_gather(shards[0], "wide", axis=0, tiled=True),
        lax.all_gather(shards[1], "wide", axis=0, tiled=True),
        lax.all_gather(shards[2], "wide", axis=0, tiled=True),
        lax.all_gather(shards[3], "wide", axis=0, tiled=True),
        lax.all_gather(shards[4], "wide", axis=0, tiled=True),
        lax.all_gather(shards[5], "wide", axis=0, tiled=True),
        lax.all_gather(shards[6], "wide", axis=0, tiled=True),
        lax.all_gather(shards[7], "wide", axis=0, tiled=True),
        lax.all_gather(shards[8], "wide", axis=0, tiled=True),
    )
    rerun, saved = forward_pass(inputs, weights, valid)
    (
        normed,
        query_heads,
        key_heads,
        value_heads,
        log_total,
        attended,
        hidden_in,
        normed_mlp,
        gate_pre,
        up_pre,
        activated,
    ) = saved
    (
        full_query,
        full_key,
        full_value,
        full_out,
        full_gate,
        full_up,
        full_down,
        full_gain_attn,
        full_gain_mlp,
    ) = weights
    grad_output = cotangent.astype(jnp.float32)
    grad_branch = grad_output.astype(jnp.bfloat16)
    grad_down = weight_grad(activated, grad_branch)
    grad_act = back_product(grad_branch, full_down)
    gate_value, gate_pull = jax.vjp(gated, gate_pre, up_pre)
    grad_gate_pre, grad_up_pre = gate_pull(grad_act)
    grad_gate_low = grad_gate_pre.astype(jnp.bfloat16)
    grad_up_low = grad_up_pre.astype(jnp.bfloat16)
    grad_gate = weight_grad(normed_mlp, grad_gate_low)
    grad_up = weight_grad(normed_mlp, grad_up_low)
    grad_normed_mlp = back_product(grad_gate_low, full_gate) + back_product(grad_up_low, full_up)
    norm_value, norm_pull = jax.vjp(norm_rows, hidden_in, full_gain_mlp.astype(jnp.float32))
    grad_hidden_norm, grad_gain_mlp = norm_pull(grad_normed_mlp)
    grad_hidden = grad_output + grad_hidden_norm
    grad_hidden_low = grad_hidden.astype(jnp.bfloat16)
    grad_out = weight_grad(attended, grad_hidden_low)
    grad_attended = back_product(grad_hidden_low, full_out).astype(jnp.bfloat16)
    grad_heads = to_heads(grad_attended)

    def head_backward(operands):
        query_one, keys_one, values_one, log_one, grad_one = operands
        scores = masked_scores(query_one, keys_one, valid)
        attention = jnp.exp(scores - log_one[..., None])
        grad_soft = jnp.einsum(
            "pqe,pke->pqk", grad_one, values_one, preferred_element_type=jnp.float32
        )
        row_dot = jnp.sum(attention * grad_soft, axis=-1, keepdims=True)
        grad_scores = (attention * (grad_soft - row_dot)).astype(jnp.bfloat16)
        grad_query_one = jnp.einsum(
            "pqk,pke->pqe", grad_scores, keys_one, preferred_element_type=jnp.float32
        )
        grad_keys_one = jnp.einsum(
            "pqk,pqe->pke", grad_scores, query_one, preferred_element_type=jnp.float32
        )
        grad_values_one = jnp.einsum(
            "pqk,pqe->pke",
            attention.astype(jnp.bfloat16),
            grad_one,
            preferred_element_type=jnp.float32,
        )
        return (grad_query_one, grad_keys_one, grad_values_one)

    grad_query_heads, grad_key_heads, grad_value_heads = lax.map(
        head_backward, (query_heads, key_heads, value_heads, log_total, grad_heads)
    )
    grad_key_local, grad_value_local = (
        lax.psum_scatter(
            grad_key_heads.astype(jnp.bfloat16), "narrow", scatter_dimension=2, tiled=True
        ).astype(jnp.float32),
        lax.psum_scatter(
            grad_value_heads.astype(jnp.bfloat16), "narrow", scatter_dimension=2, tiled=True
        ).astype(jnp.float32),
    )
    grad_query_low = from_heads(grad_query_heads).astype(jnp.bfloat16)
    grad_key_low = from_heads(grad_key_local).astype(jnp.bfloat16)
    grad_value_low = from_heads(grad_value_local).astype(jnp.bfloat16)
    grad_query = weight_grad(normed, grad_query_low)
    grad_key = weight_grad(normed, grad_key_low)
    grad_value = weight_grad(normed, grad_value_low)
    grad_normed = (
        back_product(grad_query_low, full_query)
        + back_product(grad_key_low, full_key)
        + back_product(grad_value_low, full_value)
    )
    first_value, first_pull = jax.vjp(norm_rows, inputs, full_gain_attn.astype(jnp.float32))
    grad_input_norm, grad_gain_attn = first_pull(grad_normed)
    grad_plots = (grad_hidden + grad_input_norm).astype(jnp.bfloat16)
    owned = (
        lax.psum_scatter(
            grad_query.astype(jnp.bfloat16), "wide", scatter_dimension=0, tiled=True
        ).astype(jnp.float32),
        lax.psum_scatter(
            grad_key.astype(jnp.bfloat16), "wide", scatter_dimension=0, tiled=True
        ).astype(jnp.float32),
        lax.psum_scatter(
            grad_value.astype(jnp.bfloat16), "wide", scatter_dimension=0, tiled=True
        ).astype(jnp.float32),
        lax.psum_scatter(
            grad_out.astype(jnp.bfloat16), "wide", scatter_dimension=0, tiled=True
        ).astype(jnp.float32),
        lax.psum_scatter(
            grad_gate.astype(jnp.bfloat16), "wide", scatter_dimension=0, tiled=True
        ).astype(jnp.float32),
        lax.psum_scatter(
            grad_up.astype(jnp.bfloat16), "wide", scatter_dimension=0, tiled=True
        ).astype(jnp.float32),
        lax.psum_scatter(
            grad_down.astype(jnp.bfloat16), "wide", scatter_dimension=0, tiled=True
        ).astype(jnp.float32),
        lax.psum_scatter(
            grad_gain_attn.astype(jnp.bfloat16), "wide", scatter_dimension=0, tiled=True
        ).astype(jnp.float32),
        lax.psum_scatter(
            grad_gain_mlp.astype(jnp.bfloat16), "wide", scatter_dimension=0, tiled=True
        ).astype(jnp.float32),
    )
    summed = (
        lax.psum(owned[0].astype(jnp.bfloat16), "narrow").astype(jnp.float32),
        lax.psum(owned[1].astype(jnp.bfloat16), "narrow").astype(jnp.float32),
        lax.psum(owned[2].astype(jnp.bfloat16), "narrow").astype(jnp.float32),
        lax.psum(owned[3].astype(jnp.bfloat16), "narrow").astype(jnp.float32),
        lax.psum(owned[4].astype(jnp.bfloat16), "narrow").astype(jnp.float32),
        lax.psum(owned[5].astype(jnp.bfloat16), "narrow").astype(jnp.float32),
        lax.psum(owned[6].astype(jnp.bfloat16), "narrow").astype(jnp.float32),
        lax.psum(owned[7].astype(jnp.bfloat16), "narrow").astype(jnp.float32),
        lax.psum(owned[8].astype(jnp.bfloat16), "narrow").astype(jnp.float32),
    )
    return (
        output.astype(jnp.bfloat16),
        grad_plots,
        summed[0],
        summed[1],
        summed[2],
        summed[3],
        summed[4],
        summed[5],
        summed[6],
        summed[7],
        summed[8],
    )


F32, BF16 = jnp.float32, jnp.bfloat16
ROOT = 0.7978845608028654
CUBE = 0.044715
VMEM_BYTES = 60 << 20


def nn(left, right):
    return lax.dot_general(left, right, (((1,), (0,)), ((), ())), preferred_element_type=F32)


def nt(left, right):
    return lax.dot_general(left, right, (((1,), (1,)), ((), ())), preferred_element_type=F32)


def lanes_of(rows, width=128):
    return lax.broadcasted_iota(jnp.int32, (rows, width), 1)


def row_block(index, size):
    return pl.ds(pl.multiple_of(index * size, size), size)


def head_masks(pair, lane, flag):
    first = jnp.where(lane < 64, pair, jnp.where(lane == 64, flag, 0.0))
    second = jnp.where(lane >= 64, pair, jnp.where(lane == 0, flag, 0.0))
    return first.astype(BF16), second.astype(BF16)


MESH_ID = pl.DeviceIdType.MESH


class Place:
    def __init__(self):
        wide, self.y = lax.axis_index("wide"), lax.axis_index("narrow")
        self.z, self.x, self.c = wide // 4, (wide // 2) % 2, wide % 2
        self.wide = wide

    def block(self, z, x, c):
        return (z * 2 + x) * 2 + c

    def other_z(self, j):
        z = self.z
        return (z + 1 - 2 * (z % 2), (z + 2) % 4, 3 - z)[j]

    def to_z(self, j):
        return (self.block(self.other_z(j), self.x, self.c), self.y)

    def at_z(self, z):
        return (self.block(z, self.x, self.c), self.y)

    def to_x(self):
        return (self.block(self.z, 1 - self.x, self.c), self.y)

    def to_core(self):
        return (self.block(self.z, self.x, 1 - self.c), self.y)

    def to_y(self):
        return (self.wide, 1 - self.y)

    def greet(self):
        barrier = pltpu.get_barrier_semaphore()
        partners = [self.to_z(0), self.to_z(1), self.to_z(2), self.to_x(), self.to_core(), self.to_y()]
        for partner in partners:
            pl.semaphore_signal(barrier, inc=1, device_id=partner, device_id_type=MESH_ID)
        pl.semaphore_wait(barrier, len(partners))


class Gather:
    def __init__(self, place, full, send, recv, halves):
        self.place, self.full, self.sends, self.recvs, self.halves = place, full, send, recv, halves
        self.width = full.shape[2] // 2
        self.pending = {}

    def view(self, block, half):
        if self.halves:
            return self.full.at[block, :, row_block(half, self.width)]
        return self.full.at[block]

    def copy(self, block, half, target, slot):
        view = self.view(block, half)
        return pltpu.make_async_remote_copy(
            src_ref=view, dst_ref=view, send_sem=self.sends.at[slot], recv_sem=self.recvs.at[block * 2 + half],
            device_id=target, device_id_type=MESH_ID)

    def send(self, name, block, half, target, when=None):
        slot = self.pending.setdefault(name, (len(self.pending), when))[0]
        if when is None:
            self.copy(block, half, target, slot).start()
        else:
            pl.when(when())(lambda: self.copy(block, half, target, slot).start())

    def wait(self, block, half):
        self.copy(block, half, self.place.to_core(), 0).wait_recv()

    def first(self):
        return self.place.y if self.halves else 0

    def start(self):
        p = self.place
        own = p.block(p.z, p.x, p.c)
        self.send("up", own, self.first(), p.at_z(p.z + 1), lambda: p.z < 3)
        self.send("down", own, self.first(), p.at_z(p.z - 1), lambda: p.z > 0)
        self.send("x", own, self.first(), p.to_x())
        for half in range(2 if self.halves else 1):
            self.send(("core", half), own, half, p.to_core())

    def pass_z(self, hops):
        p = self.place
        z = p.z + hops
        onward = p.z + (1 if hops < 0 else -1)
        block = p.block(z, p.x, p.c)

        def there():
            return (p.z >= -hops) if hops < 0 else (p.z <= 3 - hops)

        def inside():
            return jnp.logical_and(there(), (p.z < 3) if hops < 0 else (p.z > 0))

        pl.when(there())(lambda: self.wait(block, self.first()))
        self.send(("z", hops), block, self.first(), p.at_z(onward), inside)
        self.send(("zx", hops), block, self.first(), p.to_x(), there)
        if self.halves:
            self.send(("zy", hops), block, self.first(), p.to_y(), there)
        self.send(("zc", hops), block, self.first(), p.to_core(), there)

    def pass_x(self, hops):
        p = self.place
        block = p.block((p.z + hops) % 4, 1 - p.x, p.c)
        self.wait(block, self.first())
        if self.halves:
            self.send(("xy", hops), block, self.first(), p.to_y())
        self.send(("xc", hops), block, self.first(), p.to_core())

    def pass_y(self, hops, across):
        p = self.place
        block = p.block((p.z + hops) % 4, 1 - p.x if across else p.x, p.c)
        self.wait(block, 1 - p.y)
        self.send(("yc", hops, across), block, 1 - p.y, p.to_core())

    def end(self):
        p = self.place
        for z in range(4):
            for x in range(2):
                for half in range(2 if self.halves else 1):
                    self.wait(p.block(z, x, 1 - p.c), half)

    def sent(self):
        for slot, when in self.pending.values():
            wait = lambda slot=slot: self.copy(0, 0, self.place.to_core(), slot).wait_send()
            if when is None:
                wait()
            else:
                pl.when(when())(wait)

    def pass_both(self, hops):
        self.pass_z(-hops)
        self.pass_z(hops)

    def relay_z(self):
        for hops in (1, 2, 3):
            self.pass_both(hops)

    def relay_x(self):
        for hops in (0, 1, 3, 2):
            self.pass_x(hops)

    def relay_y(self):
        if self.halves:
            for hops in (1, 3, 2):
                self.pass_y(hops, False)
            for hops in (0, 1, 3, 2):
                self.pass_y(hops, True)


def relay_order(gathers, ahead):
    order = [gather.start for gather in gathers[:ahead]]
    for i in range(len(gathers) + 1):
        along_z, along_x = [], []
        if i < len(gathers):
            for hops in (1, 2, 3):
                along_z.append(functools.partial(gathers[i].pass_both, hops))
        if i > 0:
            for hops in (0, 1, 3, 2):
                along_x.append(functools.partial(gathers[i - 1].pass_x, hops))
        if i + ahead < len(gathers):
            along_z.insert(1, gathers[i + ahead].start)
        while along_z or along_x:
            if along_z:
                order.append(along_z.pop(0))
            if along_x:
                order.append(along_x.pop(0))
    return order


def gather_forward(count_ref, plots_hbm, cot_hbm, gain_a_ref, gain_m_ref, own_q, own_k, own_v, own_o, own_g, own_u, own_d,
                   q_out, k_out, v_out, mixed_out, lse_ref, hidden_out, x_out, cot_out, gains_ref,
                   out_q, out_k, out_v, out_o, out_g, out_u, out_d,
                   x_s, cot_s, q_s, k_s, v_s, normed, mixed, hidden,
                   qh, kh, vh, lse_cols, wq, wk, wv, wo, wg, wu, wd, wgain, sends, recvs, half_sems, out_sems):
    half = plots_hbm.shape[1]
    slots = 2 * half
    d = plots_hbm.shape[2]
    tile = 512
    tiles = slots // tile
    pairs = HEADS // 2
    place = Place()
    mine = pl.ds(pl.multiple_of(place.y * half, half), half)

    def half_copies(source, target, i):
        far = pltpu.make_async_remote_copy(
            src_ref=source.at[1 - place.y], dst_ref=target.at[mine], send_sem=half_sems.at[3 * i],
            recv_sem=half_sems.at[3 * i + 1], device_id=place.to_y(), device_id_type=MESH_ID)
        near = pltpu.make_async_copy(source.at[place.y], target.at[mine], half_sems.at[3 * i + 2])
        return far, near

    x_far, x_near = half_copies(plots_hbm, x_s, 0)
    cot_far, cot_near = half_copies(cot_hbm, cot_s, 1)
    x_near.start()
    cot_near.start()
    fulls = (wgain, wq, wk, wv, wo, wg, wu, wd)
    for full, own in zip(fulls[1:], (own_q, own_k, own_v, own_o, own_g, own_u, own_d)):
        full[place.wide] = own[...]
    wgain[place.wide, 0:1, 0:own_q.shape[0]] = gain_a_ref[...].astype(F32)
    wgain[place.wide, 1:2, 0:own_q.shape[0]] = gain_m_ref[...].astype(F32)
    gathers = [Gather(place, full, sends.at[i], recvs.at[i], full is wg or full is wu) for i, full in enumerate(fulls)]
    g_gain, g_q, g_k, g_v, g_o, g_g, g_u, g_d = gathers
    copies = []

    def put(source, target):
        copy = pltpu.make_async_copy(source, target, out_sems.at[len(copies)])
        copy.start()
        copies.append(copy)

    place.greet()
    x_far.start()
    g_gain.start()
    order = relay_order(gathers[1:], 2)

    def relay(events):
        for event in events:
            event()

    def find(gather, kind, hops):
        for i, event in enumerate(order):
            if getattr(event, "func", None) == kind and event.args == (hops,):
                return i + 1
        raise ValueError(hops)

    done_q = find(g_q, g_q.pass_x, 2)
    done_k = find(g_k, g_k.pass_x, 2)
    done_v = find(g_v, g_v.pass_x, 2)
    relay(order[:done_q])
    g_gain.relay_z()
    g_gain.relay_x()
    g_gain.end()
    rows_own = own_q.shape[0]
    for w in range(16):
        for i in range(2):
            gains_ref[i:i + 1, w * rows_own:(w + 1) * rows_own] = wgain[w, i:i + 1, 0:rows_own]
    relay(order[done_q:done_k])
    x_far.wait_recv()
    x_near.wait()
    cot_far.start()
    put(x_s, x_out)

    def normalise(t, carry):
        rows = row_block(t, 256)
        x = x_s[rows, :].astype(F32)
        r = lax.rsqrt(jnp.mean(x * x, axis=-1, keepdims=True) + epsilon)
        normed[rows, :] = (x * r * gains_ref[0:1, :]).astype(BF16)
        return carry

    lax.fori_loop(0, slots // 256, normalise, 0)

    def project(target, full, out, kept):
        def step(t, carry):
            rows = row_block(t, tile)
            target[rows, :] = nn(normed[rows, :], full[...].reshape(d, d)).astype(BF16)
            return carry

        lax.fori_loop(0, tiles, step, 0)
        put(target, out)
        put(full, kept)

    g_q.end()
    project(q_s, wq, q_out, out_q)
    relay(order[done_k:done_v])
    g_k.end()
    project(k_s, wk, k_out, out_k)
    g_v.end()
    project(v_s, wv, v_out, out_v)

    count = count_ref[0]
    lane = lanes_of(slots)
    slot = lax.broadcasted_iota(jnp.int32, (slots, 128), 0)
    bias = jnp.where(slot < count, 0.0, -1e30)
    lse_cols[...] = jnp.zeros_like(lse_cols)
    for h in range(2):
        vh[h, :, 128:] = jnp.ones((slots, 128), BF16)
    steps = pairs * tiles
    late = order[done_v:]
    first, per = 6, 2.0
    cuts = [min(len(late), int(first + per * s)) for s in range(steps)]
    hooks = [late[:cuts[0]]] + [late[cuts[s - 1]:cuts[s]] for s in range(1, steps)]

    def step(s, carry):
        p, t = s // tiles, s % tiles
        cols = row_block(p, 128)
        for when, events in enumerate(hooks):
            pl.when(s == when)(functools.partial(relay, events))

        @pl.when(t == 0)
        def _():
            kh[0], kh[1] = head_masks(k_s[:, cols].astype(F32), lane, bias)
            qp = q_s[:, cols].astype(F32)
            qh[0] = jnp.where(lane == 64, 1.0, qp).astype(BF16)
            qh[1] = jnp.where(lane == 0, 1.0, qp).astype(BF16)
            vh[0, :, :128], vh[1, :, :128] = head_masks(v_s[:, cols].astype(F32), lane, 0.0)

        rows = row_block(t, tile)
        total = None
        cols_out = lse_cols[rows, :]
        scores = [nt(qh[h, rows, :], kh[h]) for h in range(2)]
        for h in range(2):
            top = jnp.max(scores[h], axis=1, keepdims=True)
            weight = jnp.exp(scores[h] - top).astype(BF16)
            acc = nn(weight, vh[h])
            part = acc[:, :128] / acc[:, 128:]
            total = part if total is None else total + part
            cols_out = jnp.where(lanes_of(tile) == 2 * p + h, top + jnp.log(acc[:, 128:]), cols_out)
        mixed[rows, cols] = total.astype(BF16)
        lse_cols[rows, :] = cols_out
        return carry

    lax.fori_loop(0, steps, step, 0)
    put(mixed, mixed_out)
    rest = late[cuts[-1]:]
    g_o.end()
    put(wo, out_o)

    def project_out(t, carry):
        rows = row_block(t, 256)
        hidden[rows, :] = x_s[rows, :].astype(F32) + nn(mixed[rows, :], wo[...].reshape(d, d))
        lse_ref[:, rows] = jnp.transpose(lse_cols[rows, :])
        return carry

    lax.fori_loop(0, slots // 256, project_out, 0)
    put(hidden, hidden_out)
    relay(rest)
    cot_far.wait_recv()
    cot_near.wait()
    put(cot_s, cot_out)
    g_g.relay_y()
    g_g.end()
    put(wg, out_g)
    g_u.relay_y()
    g_u.end()
    put(wu, out_u)
    g_d.end()
    put(wd, out_d)
    for g in gathers:
        g.sent()
    x_far.wait_send()
    cot_far.wait_send()
    for copy in copies:
        copy.wait()


class Scatter:
    def __init__(self, place, grad, start, width, stages, at, out, send, recv):
        self.place, self.grad, self.cols, self.at = place, grad, pl.ds(start, width), pl.ds(at, width)
        self.recv_c, self.recv_x, self.recv_z, self.recv_y = stages
        self.out, self.sends, self.recvs = out, send, recv

    def copy(self, stage, source, target, device):
        return pltpu.make_async_remote_copy(
            src_ref=source, dst_ref=target, send_sem=self.sends.at[stage], recv_sem=self.recvs.at[stage],
            device_id=device, device_id_type=MESH_ID)

    def core_copy(self):
        p = self.place
        return self.copy(0, self.grad.at[:, :, 1 - p.c, :, self.cols], self.recv_c.at[:, :, :, self.at], p.to_core())

    def x_copy(self):
        p = self.place
        return self.copy(1, self.grad.at[:, 1 - p.x, p.c, :, self.cols], self.recv_x.at[:, :, self.at], p.to_x())

    def z_copy(self, j):
        p = self.place
        return self.copy(2 + j, self.grad.at[p.other_z(j), p.x, p.c, :, self.cols], self.recv_z.at[j, :, self.at], p.to_z(j))

    def y_copy(self):
        p = self.place
        return self.copy(5, self.grad.at[p.z, p.x, p.c, :, self.cols], self.recv_y.at[:, self.at], p.to_y())

    def start(self):
        self.core_copy().start()

    def add_core(self):
        self.core_copy().wait_recv()
        c = self.place.c

        def step(i, carry):
            z, x = i // 2, i % 2
            self.grad[z, x, c, :, self.cols] = self.grad[z, x, c, :, self.cols] + self.recv_c[z, x, :, self.at]
            return carry

        lax.fori_loop(0, 8, step, 0)

    def send_x(self):
        self.x_copy().start()

    def add_x(self):
        self.x_copy().wait_recv()
        x, c = self.place.x, self.place.c

        def step(z, carry):
            self.grad[z, x, c, :, self.cols] = self.grad[z, x, c, :, self.cols] + self.recv_x[z, :, self.at]
            return carry

        lax.fori_loop(0, 4, step, 0)
        for j in (2, 1, 0):
            self.z_copy(j).start()

    def add_z(self):
        for j in range(3):
            self.z_copy(j).wait_recv()
        z, x, c = self.place.z, self.place.x, self.place.c
        total = self.grad[z, x, c, :, self.cols].astype(F32)
        for j in range(3):
            total = total + self.recv_z[j, :, self.at].astype(F32)
        self.grad[z, x, c, :, self.cols] = total.astype(self.grad.dtype)
        self.y_copy().start()

    def add_y(self):
        self.y_copy().wait_recv()
        z, x, c = self.place.z, self.place.x, self.place.c
        self.out[:, self.cols] = self.grad[z, x, c, :, self.cols].astype(F32) + self.recv_y[:, self.at].astype(F32)

    def sent(self):
        self.core_copy().wait_send()
        self.x_copy().wait_send()
        for j in range(3):
            self.z_copy(j).wait_send()
        self.y_copy().wait_send()


CHUNKS = 4


def scatter_backward(count_ref, x_hbm, gains_ref, wq_hbm, wk_hbm, wv_hbm, wo_hbm, wg_hbm, wu_hbm, wd_hbm, q_hbm, k_hbm, v_hbm,
                     mixed_hbm, lse_ref, hidden_hbm, cot_hbm,
                     block_out, gplots_out, sum_q, sum_k, sum_v, sum_o, sum_g, sum_u, sum_d, sum_gain,
                     wq, wk, wv, wo, wg, wu, wd, x_s, q_s, k_s, v_s, mixed_s, cot_s, acc, dn_s, low_s, turned, block_s, actt,
                     dsum, ggain, gmlp, qh, kh, vh, dh, kt, dqt, own_gain,
                     c_g, c_u, c_d, c_o, c_n, x_g, x_u, x_d, x_q, x_k, x_v, x_o, x_n,
                     z_g, z_u, z_d, z_q, z_k, z_v, z_o, z_n, y_g, y_u, y_d, y_q, y_k, y_v, y_o, y_n,
                     sends, recvs, load_sems, out_sems):
    slots, d = x_s.shape
    ff = wg.shape[4]
    half = slots // 2
    tile = 256
    tiles = slots // tile
    rows_own = wq.shape[3]
    place = Place()
    count_loads = []

    def load(source, target):
        copy = pltpu.make_async_copy(source, target, load_sems.at[len(count_loads)])
        count_loads.append(copy)
        copy.start()
        return copy

    get_hidden = load(hidden_hbm, acc)
    get_mlp = [load(wg_hbm, wg), load(wu_hbm, wu), load(cot_hbm, cot_s), load(wd_hbm, wd)]
    get_mid = [load(wo_hbm, wo), load(mixed_hbm, mixed_s), load(x_hbm, x_s)]
    get_last = [load(wq_hbm, wq), load(wk_hbm, wk), load(wv_hbm, wv)]
    scatters = []

    def scatter(grad, start, width, stages, at, out):
        i = len(scatters)
        scatters.append(Scatter(place, grad, start, width, stages, at, out, sends.at[i], recvs.at[i]))
        return scatters[-1]

    width = ff // CHUNKS
    s_gu = []
    for f in range(CHUNKS):
        s_gu.append([scatter(wg, f * width, width, (c_g, x_g, z_g, y_g), f * width, sum_g),
                     scatter(wu, f * width, width, (c_u, x_u, z_u, y_u), f * width, sum_u)])
    s_d = scatter(wd, 0, d, (c_d, x_d, z_d, y_d), 0, sum_d)
    s_o = scatter(wo, 0, d, (c_o, x_o, z_o, y_o), 0, sum_o)
    thirds = 3
    wide = d // thirds
    s_qkv = []
    for i in range(thirds):
        s_qkv.append([scatter(wq, i * wide, wide, (c_g.at[:, :, :, pl.ds(0, d)], x_q, z_q, y_q), i * wide, sum_q),
                      scatter(wk, i * wide, wide, (c_g.at[:, :, :, pl.ds(d, d)], x_k, z_k, y_k), i * wide, sum_k),
                      scatter(wv, i * wide, wide, (c_u.at[:, :, :, pl.ds(0, d)], x_v, z_v, y_v), i * wide, sum_v)])
    s_n = scatter(own_gain, 0, 128, (c_n, x_n, z_n, y_n), 0, sum_gain)
    mine = pl.ds(pl.multiple_of(place.y * half, half), half)
    other = pl.ds(pl.multiple_of((1 - place.y) * half, half), half)

    def half_out(source, target, i):
        far = pltpu.make_async_remote_copy(
            src_ref=source.at[other], dst_ref=target.at[place.y], send_sem=out_sems.at[3 * i],
            recv_sem=out_sems.at[3 * i + 1], device_id=place.to_y(), device_id_type=MESH_ID)
        near = pltpu.make_async_copy(source.at[mine], target.at[place.y], out_sems.at[3 * i + 2])
        return far, near

    place.greet()
    get_hidden.wait()

    def norm_step(t, carry):
        rows = row_block(t, tile)
        hidden = acc[rows, :]
        r = lax.rsqrt(jnp.mean(hidden * hidden, axis=-1, keepdims=True) + epsilon)
        normed = (hidden * r * gains_ref[1:2, :]).astype(BF16)
        low_s[rows, :] = normed
        turned[:, rows] = jnp.transpose(normed)
        dn_s[rows, :] = jnp.zeros_like(hidden)
        return carry

    lax.fori_loop(0, tiles, norm_step, 0)
    for copy in get_mlp:
        copy.wait()
    chunk = pl.ds(0, width)

    def flat(ref, start):
        return ref[:, :, :, :, pl.ds(start, width)].reshape(d, width)

    def run(events):
        for event in events:
            event()

    def each(kind, group):
        return [functools.partial(kind, s) for s in group]

    C, AC, SX, AX, AZ, AY = Scatter.start, Scatter.add_core, Scatter.send_x, Scatter.add_x, Scatter.add_z, Scatter.add_y
    for f in range(CHUNKS):
        start = f * width

        def elem(t, carry):
            rows = row_block(t, tile)
            gate_pre = nn(low_s[rows, :], flat(wg, start))
            up_pre = nn(low_s[rows, :], flat(wu, start))
            d_act = nt(cot_s[rows, :], wd[f].reshape(width, d))
            square = gate_pre * gate_pre
            th = jnp.tanh(gate_pre * (ROOT + (ROOT * CUBE) * square))
            part = 0.5 + 0.5 * th
            gelu = gate_pre * part
            slope = part + gelu * (1.0 - th) * (ROOT + (3.0 * CUBE * ROOT) * square)
            act = (gelu * up_pre).astype(BF16)
            q_s[rows, chunk] = act
            actt[:, rows] = jnp.transpose(act)
            k_s[rows, chunk] = (d_act * up_pre * slope).astype(BF16)
            v_s[rows, chunk] = (d_act * gelu).astype(BF16)
            return carry

        lax.fori_loop(0, tiles, elem, 0)
        if f >= 2:
            run(each(AX, s_gu[f - 2]))
        if f >= 1:
            for s in s_gu[f - 1]:
                s.add_core()
                s.send_x()

        def add_up(t, carry):
            rows = row_block(t, tile)
            acc[rows, :] += nn(q_s[rows, chunk], wd[f].reshape(width, d))
            dn_s[rows, :] += nt(k_s[rows, chunk], flat(wg, start)) + nt(v_s[rows, chunk], flat(wu, start))
            return carry

        lax.fori_loop(0, tiles, add_up, 0)
        if f >= 3:
            run(each(AZ, s_gu[f - 3]))
        wg[:, :, :, :, pl.ds(start, width)] = nn(turned[...], k_s[:, chunk]).astype(BF16).reshape(wg.shape[:4] + (width,))
        s_gu[f][0].start()
        wu[:, :, :, :, pl.ds(start, width)] = nn(turned[...], v_s[:, chunk]).astype(BF16).reshape(wg.shape[:4] + (width,))
        s_gu[f][1].start()
        wd[f] = nn(actt[...], cot_s[...]).astype(BF16).reshape(wd.shape[1:])
    get_last += [load(q_hbm, q_s), load(k_hbm, k_s), load(v_hbm, v_s)]
    s_d.start()

    def block_step(t, carry):
        rows = row_block(t, tile)
        block_s[rows, :] = acc[rows, :].astype(BF16)
        return carry

    lax.fori_loop(0, tiles, block_step, 0)
    get_hidden = load(hidden_hbm, acc)
    block_far, block_near = half_out(block_s, block_out, 0)
    block_far.start()
    block_near.start()
    run(each(AX, s_gu[2]))
    for s in s_gu[3]:
        s.add_core()
        s.send_x()
    for copy in get_mid:
        copy.wait()
    head_row = lax.broadcasted_iota(jnp.int32, (128, d), 0)
    head_col = lax.broadcasted_iota(jnp.int32, (128, d), 1)
    pick = jnp.where(head_col // HEAD_DIM == head_row, 1.0, 0.0).astype(BF16)
    gmlp[...] = jnp.zeros_like(gmlp)
    run(each(AZ, s_gu[1]))
    run(each(AY, s_gu[0]))
    s_d.add_core()
    get_hidden.wait()

    def first(t, carry):
        rows = row_block(t, tile)
        hidden = acc[rows, :]
        dn = dn_s[rows, :]
        r = lax.rsqrt(jnp.mean(hidden * hidden, axis=-1, keepdims=True) + epsilon)
        scaled = dn * gains_ref[1:2, :]
        mean = jnp.mean(scaled * hidden, axis=-1, keepdims=True)
        dhid = cot_s[rows, :].astype(F32) + r * scaled - hidden * (r * r * r * mean)
        gmlp[...] += jnp.sum(dn * hidden * r, axis=0, keepdims=True)
        dn_s[rows, :] = dhid
        acc[rows, :] = jnp.zeros_like(dhid)
        low = dhid.astype(BF16)
        low_s[rows, :] = low
        grad = nt(low, wo[...].reshape(d, d)).astype(BF16)
        cot_s[rows, :] = grad
        mixed = mixed_s[rows, :]
        prod = grad.astype(F32) * mixed.astype(F32)
        high = prod.astype(BF16)
        rest = (prod - high.astype(F32)).astype(BF16)
        dsum[:, rows] = nt(pick, high) + nt(pick, rest)
        turned[:, rows] = jnp.transpose(mixed)
        return carry

    lax.fori_loop(0, tiles, first, 0)
    dmix = cot_s

    def weight_grads(target, right, start):
        cols = pl.ds(start, wide)
        target[:, :, :, :, cols] = nn(turned[...], right[:, cols]).astype(BF16).reshape(4, 2, 2, rows_own, wide)

    for i in range(thirds):
        weight_grads(wo, low_s, i * wide)
    s_o.start()

    def norm_again(t, carry):
        rows = row_block(t, tile)
        x = x_s[rows, :].astype(F32)
        r = lax.rsqrt(jnp.mean(x * x, axis=-1, keepdims=True) + epsilon)
        turned[:, rows] = jnp.transpose((x * r * gains_ref[0:1, :]).astype(BF16))
        return carry

    lax.fori_loop(0, tiles, norm_again, 0)
    for copy in get_last:
        copy.wait()
    s_o.add_core()
    count = count_ref[0]
    lane = lanes_of(slots)
    slot = lax.broadcasted_iota(jnp.int32, (slots, 128), 0)
    bias = jnp.where(slot < count, 0.0, -1e30)
    pairs = HEADS // 2 // thirds
    per = pairs * tiles
    hooks = {
        0: each(AY, s_gu[1]), 1: each(AX, s_gu[3]) + each(SX, [s_d]), 2: each(AZ, s_gu[2]), 5: each(AY, s_gu[2]),
        7: each(AZ, s_gu[3]), 9: each(AX, [s_d]) + each(SX, [s_o]), 10: each(AC, s_qkv[0]), 11: each(AY, s_gu[3]),
        13: each(AX, [s_o]) + each(SX, s_qkv[0]), 16: each(AC, s_qkv[1]), 17: each(AX, s_qkv[0]) + each(SX, s_qkv[1]),
        18: each(AZ, [s_o]), 19: each(AZ, [s_d]), 21: each(AZ, s_qkv[0]) + each(AY, [s_o]),
        22: each(AX, s_qkv[1]), 23: each(AY, [s_d]),
    }

    def pair_step(s, carry, third):
        p, t = s // tiles + third * pairs, s % tiles
        cols = row_block(p, 128)
        for when, events in hooks.items():
            if third * per <= when < (third + 1) * per:
                pl.when(s == when - third * per)(functools.partial(run, events))

        @pl.when(t == 0)
        def _():
            kp = k_s[:, cols].astype(F32)
            kh[0], kh[1] = head_masks(kp, lane, bias)
            for h in range(2):
                own = (lane < 64) if h == 0 else (lane >= 64)
                kt[h] = jnp.transpose(jnp.where(own, kp, 0.0)).astype(BF16)
            qp = q_s[:, cols].astype(F32)
            qh[0] = jnp.where(lane == 64, 1.0, qp).astype(BF16)
            qh[1] = jnp.where(lane == 0, 1.0, qp).astype(BF16)
            qh[2], qh[3] = head_masks(qp, lane, 0.0)
            vh[0], vh[1] = head_masks(v_s[:, cols].astype(F32), lane, 0.0)
            dh[0], dh[1] = head_masks(dmix[:, cols].astype(F32), lane, 0.0)
            dqt[...] = jnp.zeros_like(dqt)

        rows = row_block(t, tile)
        d_k = d_v = d_q = None
        scores = [nt(kh[h, rows, :], qh[h]) for h in range(2)]
        d_atts = [nt(vh[h, rows, :], dmix[:, cols]) for h in range(2)]
        for h in range(2):
            weight = jnp.exp(scores[h] - lse_ref[pl.ds(2 * p + h, 1), :])
            d_score = (weight * (d_atts[h] - dsum[pl.ds(2 * p + h, 1), :])).astype(BF16)
            part_v = nn(weight.astype(BF16), dh[h])
            part_k = nn(d_score, qh[2 + h])
            part_q = nn(kt[h, :, rows], d_score)
            d_v = part_v if d_v is None else d_v + part_v
            d_k = part_k if d_k is None else d_k + part_k
            d_q = part_q if d_q is None else d_q + part_q
        dqt[...] += d_q
        k_s[rows, cols] = d_k.astype(BF16)
        v_s[rows, cols] = d_v.astype(BF16)

        @pl.when(t == tiles - 1)
        def _():
            q_s[:, cols] = jnp.transpose(dqt[...]).astype(BF16)

        return carry

    ggain[...] = jnp.zeros_like(ggain)
    gplots = low_s
    for third in range(thirds):
        lax.fori_loop(0, per, functools.partial(pair_step, third=third), 0)
        start = third * wide
        cols = pl.ds(start, wide)

        def flat_third(ref):
            return ref[:, :, :, :, cols].reshape(d, wide)

        def add_third(t, carry):
            rows = row_block(t, tile)
            acc[rows, :] += (nt(q_s[rows, cols], flat_third(wq)) + nt(k_s[rows, cols], flat_third(wk))
                             + nt(v_s[rows, cols], flat_third(wv)))
            return carry

        lax.fori_loop(0, tiles, add_third, 0)
        for target, right, out in zip((wq, wk, wv), (q_s, k_s, v_s), s_qkv[third]):
            weight_grads(target, right, start)
            out.start()

    def last(i, carry):
        t = (i + (tiles // 2) * (1 - place.y)) % tiles
        rows = row_block(t, tile)
        x = x_s[rows, :].astype(F32)
        dn = acc[rows, :]
        r = lax.rsqrt(jnp.mean(x * x, axis=-1, keepdims=True) + epsilon)
        scaled = dn * gains_ref[0:1, :]
        mean = jnp.mean(scaled * x, axis=-1, keepdims=True)
        gplots[rows, :] = (dn_s[rows, :] + r * scaled - x * (r * r * r * mean)).astype(BF16)
        ggain[...] += jnp.sum(dn * x * r, axis=0, keepdims=True)
        return carry

    gplots_far, gplots_near = half_out(gplots, gplots_out, 1)
    lax.fori_loop(0, tiles // 2, last, 0)
    gplots_far.start()
    for s in s_qkv[2]:
        s.add_core()
        s.send_x()
    lax.fori_loop(tiles // 2, tiles, last, 0)
    gplots_near.start()
    for w in range(16):
        z, x, c = w // 4, (w // 2) % 2, w % 2
        cols = slice(w * rows_own, (w + 1) * rows_own)
        own_gain[z, x, c, 0:1, 0:rows_own] = ggain[0:1, cols]
        own_gain[z, x, c, 1:2, 0:rows_own] = gmlp[0:1, cols]
    s_n.start()
    run(each(AY, s_qkv[0]))
    run(each(AZ, s_qkv[1]))
    s_n.add_core()
    s_n.send_x()
    for s in s_qkv[2] + [s_n]:
        s.add_x()
    run(each(AY, s_qkv[1]))
    for s in s_qkv[2] + [s_n]:
        s.add_z()
    for s in s_qkv[2] + [s_n]:
        s.add_y()
    for s in scatters:
        s.sent()
    block_far.wait()
    block_near.wait()
    gplots_far.wait()
    gplots_near.wait()


def body_plot(plots, plot_grid, query_weight, key_weight, value_weight, out_weight, gate_weight, up_weight, down_weight,
              gain_attn, gain_mlp, cotangent):
    rows, d = query_weight.shape
    ff = gate_weight.shape[1]
    rows_down = down_weight.shape[0]
    half = plots.shape[1]
    slots = 2 * half
    counts = plot_grid[:, 0] * plot_grid[:, 1]
    count = lax.dynamic_slice(counts, (lax.axis_index("narrow"),), (1,))
    act = lambda dtype=BF16: ((slots, d), dtype)
    vm = lambda shape, dtype=BF16: pltpu.VMEM(shape, dtype)
    fulls = [(16, rows, d)] * 4 + [(16, rows, ff)] * 2 + [(16, rows_down, d)]
    outs = [act(), act(), act(), act(), ((128, slots), F32), act(F32), act(), act(), ((2, d), F32)]
    outs += [(shape, BF16) for shape in fulls]
    any_spec, vmem_spec = pl.BlockSpec(memory_space=pl.ANY), pl.BlockSpec(memory_space=pltpu.VMEM)
    results = pl.pallas_call(
        gather_forward,
        out_shape=[jax.ShapeDtypeStruct(shape, dtype) for shape, dtype in outs],
        in_specs=[pl.BlockSpec(memory_space=pltpu.SMEM)] + [any_spec] * 2 + [vmem_spec] * 9,
        out_specs=[any_spec] * 4 + [vmem_spec] + [any_spec] * 3 + [vmem_spec] + [any_spec] * 7,
        scratch_shapes=[vm((slots, d)) for _ in range(7)] + [vm((slots, d), F32)]
        + [vm((2, slots, 128)), vm((2, slots, 128)), vm((2, slots, 256)), vm((slots, 128), F32)]
        + [vm(shape) for shape in fulls] + [vm((16, 8, 128), F32)]
        + [pltpu.SemaphoreType.DMA((8, 48)), pltpu.SemaphoreType.DMA((8, 32)), pltpu.SemaphoreType.DMA((6,)),
           pltpu.SemaphoreType.DMA((14,))],
        compiler_params=pltpu.CompilerParams(vmem_limit_bytes=VMEM_BYTES, collective_id=1, has_side_effects=True),
    )(count, plots, cotangent, gain_attn.reshape(1, -1), gain_mlp.reshape(1, -1), query_weight, key_weight, value_weight,
      out_weight, gate_weight, up_weight, down_weight)
    q, k, v, mixed, lse, hidden, x, cot, gains = results[:9]
    weights = [w.reshape((4, 2, 2) + w.shape[1:]) for w in results[9:]]
    sums = [(rows, d)] * 4 + [(rows, ff)] * 2 + [(rows_down, d), (8, 128)]
    wide_f32 = (8, 128)
    big = lambda dtype=BF16: pltpu.VMEM((slots, d), dtype)
    stage = {"g": (rows, ff), "u": (rows, ff), "d": (rows_down, d), "q": (rows, d), "k": (rows, d), "v": (rows, d),
             "o": (rows, d), "n": wide_f32}
    stages = lambda names, lead: [vm(lead + stage[n], F32 if n == "n" else BF16) for n in names]
    groups = 2 * CHUNKS + 2 + 9 + 1
    results = pl.pallas_call(
        scatter_backward,
        out_shape=[jax.ShapeDtypeStruct(plots.shape, BF16)] * 2 + [jax.ShapeDtypeStruct(shape, F32) for shape in sums],
        in_specs=[pl.BlockSpec(memory_space=pltpu.SMEM), any_spec, vmem_spec] + [any_spec] * 11 + [vmem_spec] + [any_spec] * 2,
        out_specs=[any_spec] * 2 + [vmem_spec] * 8,
        scratch_shapes=[vm(w.shape) for w in weights]
        + [big() for _ in range(6)] + [big(F32), big(F32), big(), vm((d, slots)), big(), vm((ff // CHUNKS, slots))]
        + [vm((128, slots), F32), vm((1, d), F32), vm((1, d), F32)]
        + [vm((4, slots, 128)), vm((2, slots, 128)), vm((2, slots, 128)), vm((2, slots, 128)), vm((2, 128, slots)),
           vm((128, slots), F32), vm((4, 2, 2, 8, 128), F32)]
        + stages("gudon", (4, 2)) + stages("gudqkvon", (4,)) + stages("gudqkvon", (3,)) + stages("gudqkvon", ())
        + [pltpu.SemaphoreType.DMA((groups, 6)), pltpu.SemaphoreType.DMA((groups, 6)), pltpu.SemaphoreType.DMA((16,)),
           pltpu.SemaphoreType.DMA((6,))],
        compiler_params=pltpu.CompilerParams(vmem_limit_bytes=VMEM_BYTES, collective_id=2, has_side_effects=True),
    )(count, x, gains, *weights, q, k, v, mixed, lse, hidden, cot)
    return (*results[:9], results[9][0, :rows], results[9][1, :rows])


def body_for(mesh):
    plots_fit = mesh.shape["narrow"] == 2 and mesh.shape["wide"] == 16

    def body(plots, *rest):
        if plots_fit and plots.shape == (2, 512, HEADS * HEAD_DIM):
            return body_plot(plots, *rest)
        return body_general(plots, *rest)

    return body


def solution(mesh):
    return jax.shard_map(
        body_for(mesh),
        mesh=mesh,
        in_specs=(
            P("wide", "narrow", None),
            P("wide", None),
            P("wide", None),
            P("wide", None),
            P("wide", None),
            P("wide", None),
            P("wide", None),
            P("wide", None),
            P("wide", None),
            P("wide"),
            P("wide"),
            P("wide", "narrow", None),
        ),
        out_specs=(
            P("wide", "narrow", None),
            P("wide", "narrow", None),
            P("wide", None),
            P("wide", None),
            P("wide", None),
            P("wide", None),
            P("wide", None),
            P("wide", None),
            P("wide", None),
            P("wide"),
            P("wide"),
        ),
        check_vma=False,
    )
```

```python
import functools

import jax
import jax.numpy as jnp
from jax import lax
from jax.experimental import pallas as pl
from jax.experimental.pallas import tpu as pltpu
from jax.sharding import PartitionSpec as P

HEADS = 12
HEAD_DIM = 64


epsilon = 1e-06


def norm_rows(values, gain):
    return values * lax.rsqrt(jnp.mean(values * values, axis=-1, keepdims=True) + epsilon) * gain


def gated(gate_pre, up_pre):
    return jax.nn.gelu(gate_pre, approximate=True) * up_pre


def to_heads(tensor):
    return tensor.reshape(tensor.shape[0], tensor.shape[1], HEADS, HEAD_DIM).transpose(2, 0, 1, 3)


def from_heads(tensor):
    return tensor.transpose(1, 2, 0, 3).reshape(tensor.shape[1], tensor.shape[2], HEADS * HEAD_DIM)


def masked_scores(query_one, keys_one, valid):
    scores = jnp.einsum("pqe,pke->pqk", query_one, keys_one, preferred_element_type=jnp.float32)
    return jnp.where(valid[:, None, :], scores, -1e30)


def weight_grad(left, right):
    return jnp.einsum("psd,pse->de", left, right, preferred_element_type=jnp.float32)


def back_product(grad_rows, weight):
    return jnp.einsum("pse,de->psd", grad_rows, weight, preferred_element_type=jnp.float32)


def forward_pass(inputs, weights, valid):
    (
        query_weight,
        key_weight,
        value_weight,
        out_weight,
        gate_weight,
        up_weight,
        down_weight,
        gain_attn,
        gain_mlp,
    ) = weights
    normed = norm_rows(inputs, gain_attn.astype(jnp.float32)).astype(jnp.bfloat16)
    query = jnp.dot(normed, query_weight, preferred_element_type=jnp.float32).astype(jnp.bfloat16)
    keys_local = jnp.dot(normed, key_weight, preferred_element_type=jnp.float32).astype(
        jnp.bfloat16
    )
    values_local = jnp.dot(normed, value_weight, preferred_element_type=jnp.float32).astype(
        jnp.bfloat16
    )
    keys_all, values_all = (
        lax.all_gather(keys_local, "narrow", axis=1, tiled=True),
        lax.all_gather(values_local, "narrow", axis=1, tiled=True),
    )
    query_heads = to_heads(query)
    key_heads = to_heads(keys_all)
    value_heads = to_heads(values_all)

    def head_forward(operands):
        query_one, keys_one, values_one = operands
        scores = masked_scores(query_one, keys_one, valid)
        row_max = jnp.max(scores, axis=-1, keepdims=True)
        exponent = jnp.exp(scores - row_max)
        total = jnp.sum(exponent, axis=-1, keepdims=True)
        mixed = jnp.einsum(
            "pqk,pke->pqe",
            (exponent / total).astype(jnp.bfloat16),
            values_one,
            preferred_element_type=jnp.float32,
        )
        return (mixed.astype(jnp.bfloat16), (row_max + jnp.log(total))[..., 0])

    mixed_heads, log_total = lax.map(head_forward, (query_heads, key_heads, value_heads))
    attended = from_heads(mixed_heads)
    hidden_in = inputs + jnp.dot(attended, out_weight, preferred_element_type=jnp.float32)
    normed_mlp = norm_rows(hidden_in, gain_mlp.astype(jnp.float32)).astype(jnp.bfloat16)
    gate_pre = jnp.dot(normed_mlp, gate_weight, preferred_element_type=jnp.float32)
    up_pre = jnp.dot(normed_mlp, up_weight, preferred_element_type=jnp.float32)
    activated = gated(gate_pre, up_pre).astype(jnp.bfloat16)
    output = hidden_in + jnp.dot(activated, down_weight, preferred_element_type=jnp.float32)
    saved = (
        normed,
        query_heads,
        key_heads,
        value_heads,
        log_total,
        attended,
        hidden_in,
        normed_mlp,
        gate_pre,
        up_pre,
        activated,
    )
    return (output, saved)


def body_general(
    plots,
    plot_grid,
    query_weight,
    key_weight,
    value_weight,
    out_weight,
    gate_weight,
    up_weight,
    down_weight,
    gain_attn,
    gain_mlp,
    cotangent,
):
    shards = (
        query_weight,
        key_weight,
        value_weight,
        out_weight,
        gate_weight,
        up_weight,
        down_weight,
        gain_attn,
        gain_mlp,
    )
    inputs = plots.astype(jnp.float32)
    counts = plot_grid[:, 0] * plot_grid[:, 1]
    length = plots.shape[1] * lax.axis_size("narrow")
    valid = jnp.arange(length)[None, :] < counts[:, None]
    weights = (
        lax.all_gather(shards[0], "wide", axis=0, tiled=True),
        lax.all_gather(shards[1], "wide", axis=0, tiled=True),
        lax.all_gather(shards[2], "wide", axis=0, tiled=True),
        lax.all_gather(shards[3], "wide", axis=0, tiled=True),
        lax.all_gather(shards[4], "wide", axis=0, tiled=True),
        lax.all_gather(shards[5], "wide", axis=0, tiled=True),
        lax.all_gather(shards[6], "wide", axis=0, tiled=True),
        lax.all_gather(shards[7], "wide", axis=0, tiled=True),
        lax.all_gather(shards[8], "wide", axis=0, tiled=True),
    )
    output, saved = forward_pass(inputs, weights, valid)
    weights = (
        lax.all_gather(shards[0], "wide", axis=0, tiled=True),
        lax.all_gather(shards[1], "wide", axis=0, tiled=True),
        lax.all_gather(shards[2], "wide", axis=0, tiled=True),
        lax.all_gather(shards[3], "wide", axis=0, tiled=True),
        lax.all_gather(shards[4], "wide", axis=0, tiled=True),
        lax.all_gather(shards[5], "wide", axis=0, tiled=True),
        lax.all_gather(shards[6], "wide", axis=0, tiled=True),
        lax.all_gather(shards[7], "wide", axis=0, tiled=True),
        lax.all_gather(shards[8], "wide", axis=0, tiled=True),
    )
    rerun, saved = forward_pass(inputs, weights, valid)
    (
        normed,
        query_heads,
        key_heads,
        value_heads,
        log_total,
        attended,
        hidden_in,
        normed_mlp,
        gate_pre,
        up_pre,
        activated,
    ) = saved
    (
        full_query,
        full_key,
        full_value,
        full_out,
        full_gate,
        full_up,
        full_down,
        full_gain_attn,
        full_gain_mlp,
    ) = weights
    grad_output = cotangent.astype(jnp.float32)
    grad_branch = grad_output.astype(jnp.bfloat16)
    grad_down = weight_grad(activated, grad_branch)
    grad_act = back_product(grad_branch, full_down)
    gate_value, gate_pull = jax.vjp(gated, gate_pre, up_pre)
    grad_gate_pre, grad_up_pre = gate_pull(grad_act)
    grad_gate_low = grad_gate_pre.astype(jnp.bfloat16)
    grad_up_low = grad_up_pre.astype(jnp.bfloat16)
    grad_gate = weight_grad(normed_mlp, grad_gate_low)
    grad_up = weight_grad(normed_mlp, grad_up_low)
    grad_normed_mlp = back_product(grad_gate_low, full_gate) + back_product(grad_up_low, full_up)
    norm_value, norm_pull = jax.vjp(norm_rows, hidden_in, full_gain_mlp.astype(jnp.float32))
    grad_hidden_norm, grad_gain_mlp = norm_pull(grad_normed_mlp)
    grad_hidden = grad_output + grad_hidden_norm
    grad_hidden_low = grad_hidden.astype(jnp.bfloat16)
    grad_out = weight_grad(attended, grad_hidden_low)
    grad_attended = back_product(grad_hidden_low, full_out).astype(jnp.bfloat16)
    grad_heads = to_heads(grad_attended)

    def head_backward(operands):
        query_one, keys_one, values_one, log_one, grad_one = operands
        scores = masked_scores(query_one, keys_one, valid)
        attention = jnp.exp(scores - log_one[..., None])
        grad_soft = jnp.einsum(
            "pqe,pke->pqk", grad_one, values_one, preferred_element_type=jnp.float32
        )
        row_dot = jnp.sum(attention * grad_soft, axis=-1, keepdims=True)
        grad_scores = (attention * (grad_soft - row_dot)).astype(jnp.bfloat16)
        grad_query_one = jnp.einsum(
            "pqk,pke->pqe", grad_scores, keys_one, preferred_element_type=jnp.float32
        )
        grad_keys_one = jnp.einsum(
            "pqk,pqe->pke", grad_scores, query_one, preferred_element_type=jnp.float32
        )
        grad_values_one = jnp.einsum(
            "pqk,pqe->pke",
            attention.astype(jnp.bfloat16),
            grad_one,
            preferred_element_type=jnp.float32,
        )
        return (grad_query_one, grad_keys_one, grad_values_one)

    grad_query_heads, grad_key_heads, grad_value_heads = lax.map(
        head_backward, (query_heads, key_heads, value_heads, log_total, grad_heads)
    )
    grad_key_local, grad_value_local = (
        lax.psum_scatter(
            grad_key_heads.astype(jnp.bfloat16), "narrow", scatter_dimension=2, tiled=True
        ).astype(jnp.float32),
        lax.psum_scatter(
            grad_value_heads.astype(jnp.bfloat16), "narrow", scatter_dimension=2, tiled=True
        ).astype(jnp.float32),
    )
    grad_query_low = from_heads(grad_query_heads).astype(jnp.bfloat16)
    grad_key_low = from_heads(grad_key_local).astype(jnp.bfloat16)
    grad_value_low = from_heads(grad_value_local).astype(jnp.bfloat16)
    grad_query = weight_grad(normed, grad_query_low)
    grad_key = weight_grad(normed, grad_key_low)
    grad_value = weight_grad(normed, grad_value_low)
    grad_normed = (
        back_product(grad_query_low, full_query)
        + back_product(grad_key_low, full_key)
        + back_product(grad_value_low, full_value)
    )
    first_value, first_pull = jax.vjp(norm_rows, inputs, full_gain_attn.astype(jnp.float32))
    grad_input_norm, grad_gain_attn = first_pull(grad_normed)
    grad_plots = (grad_hidden + grad_input_norm).astype(jnp.bfloat16)
    owned = (
        lax.psum_scatter(
            grad_query.astype(jnp.bfloat16), "wide", scatter_dimension=0, tiled=True
        ).astype(jnp.float32),
        lax.psum_scatter(
            grad_key.astype(jnp.bfloat16), "wide", scatter_dimension=0, tiled=True
        ).astype(jnp.float32),
        lax.psum_scatter(
            grad_value.astype(jnp.bfloat16), "wide", scatter_dimension=0, tiled=True
        ).astype(jnp.float32),
        lax.psum_scatter(
            grad_out.astype(jnp.bfloat16), "wide", scatter_dimension=0, tiled=True
        ).astype(jnp.float32),
        lax.psum_scatter(
            grad_gate.astype(jnp.bfloat16), "wide", scatter_dimension=0, tiled=True
        ).astype(jnp.float32),
        lax.psum_scatter(
            grad_up.astype(jnp.bfloat16), "wide", scatter_dimension=0, tiled=True
        ).astype(jnp.float32),
        lax.psum_scatter(
            grad_down.astype(jnp.bfloat16), "wide", scatter_dimension=0, tiled=True
        ).astype(jnp.float32),
        lax.psum_scatter(
            grad_gain_attn.astype(jnp.bfloat16), "wide", scatter_dimension=0, tiled=True
        ).astype(jnp.float32),
        lax.psum_scatter(
            grad_gain_mlp.astype(jnp.bfloat16), "wide", scatter_dimension=0, tiled=True
        ).astype(jnp.float32),
    )
    summed = (
        lax.psum(owned[0].astype(jnp.bfloat16), "narrow").astype(jnp.float32),
        lax.psum(owned[1].astype(jnp.bfloat16), "narrow").astype(jnp.float32),
        lax.psum(owned[2].astype(jnp.bfloat16), "narrow").astype(jnp.float32),
        lax.psum(owned[3].astype(jnp.bfloat16), "narrow").astype(jnp.float32),
        lax.psum(owned[4].astype(jnp.bfloat16), "narrow").astype(jnp.float32),
        lax.psum(owned[5].astype(jnp.bfloat16), "narrow").astype(jnp.float32),
        lax.psum(owned[6].astype(jnp.bfloat16), "narrow").astype(jnp.float32),
        lax.psum(owned[7].astype(jnp.bfloat16), "narrow").astype(jnp.float32),
        lax.psum(owned[8].astype(jnp.bfloat16), "narrow").astype(jnp.float32),
    )
    return (
        output.astype(jnp.bfloat16),
        grad_plots,
        summed[0],
        summed[1],
        summed[2],
        summed[3],
        summed[4],
        summed[5],
        summed[6],
        summed[7],
        summed[8],
    )


F32, BF16 = jnp.float32, jnp.bfloat16
ROOT = 0.7978845608028654
CUBE = 0.044715
VMEM_BYTES = 62 << 20


def nn(left, right):
    return lax.dot_general(left, right, (((1,), (0,)), ((), ())), preferred_element_type=F32)


def nt(left, right):
    return lax.dot_general(left, right, (((1,), (1,)), ((), ())), preferred_element_type=F32)


def lanes_of(rows, width=128):
    return lax.broadcasted_iota(jnp.int32, (rows, width), 1)


def row_block(index, size):
    return pl.ds(pl.multiple_of(index * size, size), size)


def head_masks(pair, lane, flag):
    first = jnp.where(lane < 64, pair, jnp.where(lane == 64, flag, 0.0))
    second = jnp.where(lane >= 64, pair, jnp.where(lane == 0, flag, 0.0))
    return first.astype(BF16), second.astype(BF16)


MESH_ID = pl.DeviceIdType.MESH


class Place:
    def __init__(self):
        wide, self.y = lax.axis_index("wide"), lax.axis_index("narrow")
        self.z, self.x, self.c = wide // 4, (wide // 2) % 2, wide % 2
        self.wide = wide

    def block(self, z, x, c):
        return (z * 2 + x) * 2 + c

    def other_z(self, j):
        z = self.z
        return (z + 1 - 2 * (z % 2), (z + 2) % 4, 3 - z)[j]

    def to_z(self, j):
        return (self.block(self.other_z(j), self.x, self.c), self.y)

    def at_z(self, z):
        return (self.block(z, self.x, self.c), self.y)

    def to_x(self):
        return (self.block(self.z, 1 - self.x, self.c), self.y)

    def to_core(self):
        return (self.block(self.z, self.x, 1 - self.c), self.y)

    def to_y(self):
        return (self.wide, 1 - self.y)

    def greet(self):
        barrier = pltpu.get_barrier_semaphore()
        partners = [self.to_z(0), self.to_z(1), self.to_z(2), self.to_x(), self.to_core(), self.to_y()]
        for partner in partners:
            pl.semaphore_signal(barrier, inc=1, device_id=partner, device_id_type=MESH_ID)
        pl.semaphore_wait(barrier, len(partners))


class Gather:
    def __init__(self, place, full, send, recv, halves):
        self.place, self.full, self.sends, self.recvs, self.halves = place, full, send, recv, halves
        self.width = full.shape[4] // 2
        self.pending = {}
        self.settled = set()

    def view(self, spot, half):
        if self.halves:
            return self.full.at[(*spot, slice(None), row_block(half, self.width))]
        return self.full.at[spot]

    def copy(self, spot, half, target, slot):
        view = self.view(spot, half)
        block = self.place.block(*spot)
        return pltpu.make_async_remote_copy(
            src_ref=view, dst_ref=view, send_sem=self.sends.at[slot], recv_sem=self.recvs.at[block * 2 + half],
            device_id=target, device_id_type=MESH_ID)

    def send(self, name, spot, half, target, when=None):
        slot = self.pending.setdefault(name, (len(self.pending), when))[0]
        if when is None:
            self.copy(spot, half, target, slot).start()
        else:
            pl.when(when())(lambda: self.copy(spot, half, target, slot).start())

    def wait(self, spot, half):
        self.copy(spot, half, self.place.to_core(), 0).wait_recv()

    def first(self):
        return self.place.y if self.halves else 0

    def start(self):
        p = self.place
        own = (p.z, p.x, p.c)
        self.send("up", own, self.first(), p.at_z(p.z + 1), lambda: p.z < 3)
        self.send("down", own, self.first(), p.at_z(p.z - 1), lambda: p.z > 0)
        self.send("x", own, self.first(), p.to_x())
        for half in range(2 if self.halves else 1):
            self.send(("core", half), own, half, p.to_core())

    def pass_z(self, hops):
        p = self.place
        z = p.z + hops
        onward = p.z + (1 if hops < 0 else -1)
        block = (z, p.x, p.c)

        def there():
            return (p.z >= -hops) if hops < 0 else (p.z <= 3 - hops)

        def inside():
            return jnp.logical_and(there(), (p.z < 3) if hops < 0 else (p.z > 0))

        pl.when(there())(lambda: self.wait(block, self.first()))
        self.send(("z", hops), block, self.first(), p.at_z(onward), inside)
        self.send(("zx", hops), block, self.first(), p.to_x(), there)
        if self.halves:
            self.send(("zy", hops), block, self.first(), p.to_y(), there)
        self.send(("zc", hops), block, self.first(), p.to_core(), there)

    def pass_x(self, hops):
        p = self.place
        block = ((p.z + hops) % 4, 1 - p.x, p.c)
        self.wait(block, self.first())
        if self.halves:
            self.send(("xy", hops), block, self.first(), p.to_y())
        self.send(("xc", hops), block, self.first(), p.to_core())

    def pass_y(self, hops, across):
        p = self.place
        block = ((p.z + hops) % 4, 1 - p.x if across else p.x, p.c)
        self.wait(block, 1 - p.y)
        self.send(("yc", hops, across), block, 1 - p.y, p.to_core())

    def end(self, half=0):
        p = self.place
        for z in range(4):
            for x in range(2):
                self.wait((z, x, 1 - p.c), half)

    def sent(self):
        for name, (slot, when) in self.pending.items():
            if name in self.settled:
                continue
            self.settled.add(name)
            wait = lambda slot=slot: self.copy((0, 0, 0), 0, self.place.to_core(), slot).wait_send()
            if when is None:
                wait()
            else:
                pl.when(when())(wait)

    def pass_both(self, hops):
        self.pass_z(-hops)
        self.pass_z(hops)

    def relay_z(self):
        for hops in (1, 2, 3):
            self.pass_both(hops)

    def relay_x(self):
        for hops in (0, 1, 3, 2):
            self.pass_x(hops)

    def relay_y(self):
        if self.halves:
            for hops in (1, 3, 2):
                self.pass_y(hops, False)
            for hops in (0, 1, 3, 2):
                self.pass_y(hops, True)


def relay_order(gathers, ahead):
    order = [gather.start for gather in gathers[:ahead]]
    for i in range(len(gathers) + 1):
        along_z, along_x = [], []
        if i < len(gathers):
            for hops in (1, 2, 3):
                along_z.append(functools.partial(gathers[i].pass_both, hops))
        if i > 0:
            for hops in (0, 1, 3, 2):
                along_x.append(functools.partial(gathers[i - 1].pass_x, hops))
        if i + ahead < len(gathers):
            along_z.insert(1, gathers[i + ahead].start)
        while along_z or along_x:
            if along_z:
                order.append(along_z.pop(0))
            if along_x:
                order.append(along_x.pop(0))
    return order


class Scatter:
    def __init__(self, place, grad, start, width, stages, at, out, send, recv):
        self.place, self.grad, self.cols, self.at = place, grad, pl.ds(start, width), pl.ds(at, width)
        self.recv_c, self.recv_x, self.recv_z, self.recv_y = stages
        self.out, self.sends, self.recvs = out, send, recv

    def copy(self, stage, source, target, device):
        return pltpu.make_async_remote_copy(
            src_ref=source, dst_ref=target, send_sem=self.sends.at[stage], recv_sem=self.recvs.at[stage],
            device_id=device, device_id_type=MESH_ID)

    def core_copy(self):
        p = self.place
        return self.copy(0, self.grad.at[:, :, 1 - p.c, :, self.cols], self.recv_c.at[:, :, :, self.at], p.to_core())

    def x_copy(self):
        p = self.place
        return self.copy(1, self.grad.at[:, 1 - p.x, p.c, :, self.cols], self.recv_x.at[:, :, self.at], p.to_x())

    def z_copy(self, j):
        p = self.place
        return self.copy(2 + j, self.grad.at[p.other_z(j), p.x, p.c, :, self.cols], self.recv_z.at[j, :, self.at], p.to_z(j))

    def y_copy(self):
        p = self.place
        return self.copy(5, self.grad.at[p.z, p.x, p.c, :, self.cols], self.recv_y.at[:, self.at], p.to_y())

    def start(self):
        self.core_copy().start()

    def add_core(self):
        self.core_copy().wait_recv()
        c = self.place.c

        def step(i, carry):
            z, x = i // 2, i % 2
            self.grad[z, x, c, :, self.cols] = self.grad[z, x, c, :, self.cols] + self.recv_c[z, x, :, self.at]
            return carry

        lax.fori_loop(0, 8, step, 0)

    def send_x(self):
        self.x_copy().start()

    def add_x(self):
        self.x_copy().wait_recv()
        x, c = self.place.x, self.place.c

        def step(z, carry):
            self.grad[z, x, c, :, self.cols] = self.grad[z, x, c, :, self.cols] + self.recv_x[z, :, self.at]
            return carry

        lax.fori_loop(0, 4, step, 0)
        for j in (2, 1, 0):
            self.z_copy(j).start()

    def add_z(self):
        for j in range(3):
            self.z_copy(j).wait_recv()
        z, x, c = self.place.z, self.place.x, self.place.c
        total = self.grad[z, x, c, :, self.cols].astype(F32)
        for j in range(3):
            total = total + self.recv_z[j, :, self.at].astype(F32)
        self.grad[z, x, c, :, self.cols] = total.astype(self.grad.dtype)
        self.y_copy().start()

    def add_y(self):
        self.y_copy().wait_recv()
        z, x, c = self.place.z, self.place.x, self.place.c
        self.out[:, self.cols] = self.grad[z, x, c, :, self.cols].astype(F32) + self.recv_y[:, self.at].astype(F32)

    def sent(self):
        self.core_copy().wait_send()
        self.x_copy().wait_send()
        for j in range(3):
            self.z_copy(j).wait_send()
        self.y_copy().wait_send()


CHUNKS = 4


def layer(count_ref, plots_hbm, cot_hbm, gain_a_ref, gain_m_ref, own_q, own_k, own_v, own_o, own_g, own_u, own_d,
          block_out, gplots_out, sum_q, sum_k, sum_v, sum_o, sum_g, sum_u, sum_d, sum_gain, park_q, park_k, park_v, park_h,
          wq, wk, wv, wo, wg, wu, wd, x_s, q_s, k_s, v_s, mixed_s, cot_s, acc, dn_s, low_s, turned, block_s, actt,
          dsum, lse_ref, gains_ref, ggain, gmlp, qh, kh, vh, dh, kt, dqt, own_gain, wgain,
          c_g, c_u, c_d, c_o, c_n, x_g, x_u, x_d, x_q, x_k, x_v, x_o, x_n,
          z_g, z_u, z_d, z_q, z_k, z_v, z_o, z_n, y_g, y_u, y_d, y_q, y_k, y_v, y_o, y_n,
          sends_w, recvs_w, half_sems, park_sems, sends, recvs, load_sems, out_sems):
    half = plots_hbm.shape[1]
    slots = 2 * half
    d = plots_hbm.shape[2]
    tile_f = 512
    tiles_f = slots // tile_f
    pairs_f = HEADS // 2
    tile = 256
    tiles = slots // tile
    ff = wg.shape[4]
    place = Place()
    mine = pl.ds(pl.multiple_of(place.y * half, half), half)

    def half_copies(source, target, i):
        far = pltpu.make_async_remote_copy(
            src_ref=source.at[1 - place.y], dst_ref=target.at[mine], send_sem=half_sems.at[3 * i],
            recv_sem=half_sems.at[3 * i + 1], device_id=place.to_y(), device_id_type=MESH_ID)
        near = pltpu.make_async_copy(source.at[place.y], target.at[mine], half_sems.at[3 * i + 2])
        return far, near

    x_far, x_near = half_copies(plots_hbm, x_s, 0)
    cot_far, cot_near = half_copies(cot_hbm, cot_s, 1)
    x_near.start()
    cot_near.start()
    fulls = (wgain, wq, wk, wv, wo, wd, wg, wu)
    here = (place.z, place.x, place.c)
    for full, own in zip(fulls[1:], (own_q, own_k, own_v, own_o, own_d, own_g, own_u)):
        full[here] = own[...]
    rows_own = own_q.shape[0]
    wgain[(*here, slice(0, 1), slice(0, rows_own))] = gain_a_ref[...].astype(F32)
    wgain[(*here, slice(1, 2), slice(0, rows_own))] = gain_m_ref[...].astype(F32)
    gathers = [Gather(place, full, sends_w.at[i], recvs_w.at[i], full is wg or full is wu) for i, full in enumerate(fulls)]
    g_gain, g_q, g_k, g_v, g_o, g_d, g_g, g_u = gathers
    copies = []

    def put(source, target):
        copy = pltpu.make_async_copy(source, target, park_sems.at[len(copies)])
        copy.start()
        copies.append(copy)

    place.greet()
    x_far.start()
    g_gain.start()
    order = relay_order(gathers[1:], 2)

    def relay(events):
        for event in events:
            event()

    def find(gather, kind, hops):
        for i, event in enumerate(order):
            if getattr(event, "func", None) == kind and event.args == (hops,):
                return i + 1
        raise ValueError(hops)

    done_q = find(g_q, g_q.pass_x, 2)
    done_k = find(g_k, g_k.pass_x, 2)
    done_v = find(g_v, g_v.pass_x, 2)
    relay(order[:done_q])
    g_gain.relay_z()
    g_gain.relay_x()
    g_gain.end()
    for w in range(16):
        for i in range(2):
            gains_ref[i:i + 1, w * rows_own:(w + 1) * rows_own] = wgain[w // 4, (w // 2) % 2, w % 2, i:i + 1, 0:rows_own]
    relay(order[done_q:done_k])
    x_far.wait_recv()
    x_near.wait()
    cot_far.start()

    def normalise(t, carry):
        rows = row_block(t, 256)
        x = x_s[rows, :].astype(F32)
        r = lax.rsqrt(jnp.mean(x * x, axis=-1, keepdims=True) + epsilon)
        low_s[rows, :] = (x * r * gains_ref[0:1, :]).astype(BF16)
        return carry

    lax.fori_loop(0, slots // 256, normalise, 0)

    def project(target, full, out):
        def step(t, carry):
            rows = row_block(t, 512)
            target[rows, :] = nn(low_s[rows, :], full[...].reshape(d, d)).astype(BF16)
            return carry

        lax.fori_loop(0, slots // 512, step, 0)
        put(target, out)

    g_q.end()
    project(q_s, wq, park_q)
    relay(order[done_k:done_v])
    g_k.end()
    project(k_s, wk, park_k)
    g_v.end()
    project(v_s, wv, park_v)

    count = count_ref[0]
    lane = lanes_of(slots)
    slot = lax.broadcasted_iota(jnp.int32, (slots, 128), 0)
    bias = jnp.where(slot < count, 0.0, -1e30)
    lse_cols = pl.ds(0, 128)
    dn_s[:, lse_cols] = jnp.zeros((slots, 128), F32)
    values = [pl.ds(256 * h, 128) for h in range(2)]
    values_ones = [pl.ds(256 * h, 256) for h in range(2)]
    for h in range(2):
        block_s[:, 256 * h + 128:256 * h + 256] = jnp.ones((slots, 128), BF16)
    steps = pairs_f * tiles_f
    late = order[done_v:]
    first, per = 4, 1.7
    cuts = [min(len(late), int(first + per * s)) for s in range(steps)]
    hooks = [late[:cuts[0]]] + [late[cuts[s - 1]:cuts[s]] for s in range(1, steps)]

    def forward_step(s, carry):
        p, t = s // tiles_f, s % tiles_f
        cols = row_block(p, 128)
        for when, events in enumerate(hooks):
            pl.when(s == when)(functools.partial(relay, events))

        @pl.when(t == 0)
        def _():
            kh[0], kh[1] = head_masks(k_s[:, cols].astype(F32), lane, bias)
            qp = q_s[:, cols].astype(F32)
            qh[0] = jnp.where(lane == 64, 1.0, qp).astype(BF16)
            qh[1] = jnp.where(lane == 0, 1.0, qp).astype(BF16)
            block_s[:, values[0]], block_s[:, values[1]] = head_masks(v_s[:, cols].astype(F32), lane, 0.0)

        rows = row_block(t, tile_f)
        total = None
        cols_out = dn_s[rows, lse_cols]
        scores = [nt(qh[h, rows, :], kh[h]) for h in range(2)]
        for h in range(2):
            top = jnp.max(scores[h], axis=1, keepdims=True)
            weight = jnp.exp(scores[h] - top).astype(BF16)
            out = nn(weight, block_s[:, values_ones[h]])
            part = out[:, :128] / out[:, 128:]
            total = part if total is None else total + part
            cols_out = jnp.where(lanes_of(tile_f) == 2 * p + h, top + jnp.log(out[:, 128:]), cols_out)
        mixed_s[rows, cols] = total.astype(BF16)
        dn_s[rows, lse_cols] = cols_out
        return carry

    lax.fori_loop(0, steps, forward_step, 0)
    g_o.end()

    def project_out(t, carry):
        rows = row_block(t, tile)
        hidden = x_s[rows, :].astype(F32) + nn(mixed_s[rows, :], wo[...].reshape(d, d))
        acc[rows, :] = hidden
        lse_ref[:, rows] = jnp.transpose(dn_s[rows, lse_cols])
        r = lax.rsqrt(jnp.mean(hidden * hidden, axis=-1, keepdims=True) + epsilon)
        low = (hidden * r * gains_ref[1:2, :]).astype(BF16)
        low_s[rows, :] = low
        turned[:, rows] = jnp.transpose(low)
        dn_s[rows, :] = jnp.zeros_like(hidden)
        return carry

    lax.fori_loop(0, tiles, project_out, 0)
    put(acc, park_h)
    relay(late[cuts[-1]:])
    cot_far.wait_recv()
    cot_near.wait()
    g_d.end()
    g_g.end(place.y)
    g_u.end(place.y)
    for g in (g_gain, g_q, g_k, g_v, g_o, g_d):
        g.sent()
    for copy in copies:
        copy.wait()

    def load(source, target, i):
        copy = pltpu.make_async_copy(source, target, load_sems.at[i])
        copy.start()
        return copy

    scatters = []

    def scatter(grad, start, width, stages, at, out, i=None):
        i = len(scatters) if i is None else i
        scatters.append(Scatter(place, grad, start, width, stages, at, out, sends.at[i], recvs.at[i]))
        return scatters[-1]

    width = ff // CHUNKS
    s_gu = []
    chunks = [(f + 2 * place.y) % CHUNKS for f in range(CHUNKS)]
    starts = [pl.multiple_of(f * width, width) for f in chunks]
    for f, start in zip(chunks, starts):
        s_gu.append([scatter(wg, start, width, (c_g, x_g, z_g, y_g), start, sum_g, 2 * f),
                     scatter(wu, start, width, (c_u, x_u, z_u, y_u), start, sum_u, 2 * f + 1)])
    s_d = scatter(wd, 0, d, (c_d, x_d, z_d, y_d), 0, sum_d)
    s_o = scatter(wo, 0, d, (c_o, x_o, z_o, y_o), 0, sum_o)
    thirds = 3
    wide = d // thirds
    s_qkv = []
    for i in range(thirds):
        s_qkv.append([scatter(wq, i * wide, wide, (c_g.at[:, :, :, pl.ds(0, d)], x_q, z_q, y_q), i * wide, sum_q),
                      scatter(wk, i * wide, wide, (c_g.at[:, :, :, pl.ds(d, d)], x_k, z_k, y_k), i * wide, sum_k),
                      scatter(wv, i * wide, wide, (c_u.at[:, :, :, pl.ds(0, d)], x_v, z_v, y_v), i * wide, sum_v)])
    s_n = scatter(own_gain, 0, 128, (c_n, x_n, z_n, y_n), 0, sum_gain)
    other = pl.ds(pl.multiple_of((1 - place.y) * half, half), half)

    def half_out(source, target, i):
        far = pltpu.make_async_remote_copy(
            src_ref=source.at[other], dst_ref=target.at[place.y], send_sem=out_sems.at[3 * i],
            recv_sem=out_sems.at[3 * i + 1], device_id=place.to_y(), device_id_type=MESH_ID)
        near = pltpu.make_async_copy(source.at[mine], target.at[place.y], out_sems.at[3 * i + 2])
        return far, near

    chunk = pl.ds(0, width)

    def flat(ref, start):
        return ref[:, :, :, :, pl.ds(start, width)].reshape(d, width)

    def run(events):
        for event in events:
            event()

    def each(kind, group):
        return [functools.partial(kind, s) for s in group]

    C, AC, SX, AX, AZ, AY = Scatter.start, Scatter.add_core, Scatter.send_x, Scatter.add_x, Scatter.add_z, Scatter.add_y
    for f, (spot, start) in enumerate(zip(chunks, starts)):
        if f == 2:
            g_u.relay_y()
            g_g.end(1 - place.y)
            g_u.end(1 - place.y)

        def elem(t, carry):
            rows = row_block(t, 512)
            gate_pre = nn(low_s[rows, :], flat(wg, start))
            up_pre = nn(low_s[rows, :], flat(wu, start))
            d_act = nt(cot_s[rows, :], wd[spot].reshape(width, d))
            square = gate_pre * gate_pre
            th = jnp.tanh(gate_pre * (ROOT + (ROOT * CUBE) * square))
            part = 0.5 + 0.5 * th
            gelu = gate_pre * part
            slope = part + gelu * (1.0 - th) * (ROOT + (3.0 * CUBE * ROOT) * square)
            act = (gelu * up_pre).astype(BF16)
            q_s[rows, chunk] = act
            actt[:, rows] = jnp.transpose(act)
            k_s[rows, chunk] = (d_act * up_pre * slope).astype(BF16)
            v_s[rows, chunk] = (d_act * gelu).astype(BF16)
            return carry

        lax.fori_loop(0, slots // 512, elem, 0)
        if f == 0:
            g_g.relay_y()
        if f >= 2:
            run(each(AX, s_gu[f - 2]))
        if f >= 1:
            for s in s_gu[f - 1]:
                s.add_core()
                s.send_x()

        def add_up(t, carry):
            rows = row_block(t, 512)
            acc[rows, :] += nn(q_s[rows, chunk], wd[spot].reshape(width, d))
            dn_s[rows, :] += nt(k_s[rows, chunk], flat(wg, start)) + nt(v_s[rows, chunk], flat(wu, start))
            return carry

        lax.fori_loop(0, slots // 512, add_up, 0)
        if f >= 3:
            run(each(AZ, s_gu[f - 3]))
        if f in (0, 2):
            g_g.sent()
        wg[:, :, :, :, pl.ds(start, width)] = nn(turned[...], k_s[:, chunk]).astype(BF16).reshape(wg.shape[:4] + (width,))
        s_gu[f][0].start()
        if f in (0, 2):
            g_u.sent()
        wu[:, :, :, :, pl.ds(start, width)] = nn(turned[...], v_s[:, chunk]).astype(BF16).reshape(wg.shape[:4] + (width,))
        s_gu[f][1].start()
        wd[spot] = nn(actt[...], cot_s[...]).astype(BF16).reshape(wd.shape[1:])
    get_last = [load(park_q, q_s, 0), load(park_k, k_s, 1), load(park_v, v_s, 2)]
    s_d.start()

    def block_step(t, carry):
        rows = row_block(t, tile)
        block_s[rows, :] = acc[rows, :].astype(BF16)
        return carry

    lax.fori_loop(0, tiles, block_step, 0)
    get_hidden = load(park_h, acc, 3)
    block_far, block_near = half_out(block_s, block_out, 0)
    block_far.start()
    block_near.start()
    run(each(AX, s_gu[2]))
    for s in s_gu[3]:
        s.add_core()
        s.send_x()
    head_row = lax.broadcasted_iota(jnp.int32, (128, d), 0)
    head_col = lax.broadcasted_iota(jnp.int32, (128, d), 1)
    pick = jnp.where(head_col // HEAD_DIM == head_row, 1.0, 0.0).astype(BF16)
    gmlp[...] = jnp.zeros_like(gmlp)
    run(each(AZ, s_gu[1]))
    s_d.add_core()
    get_hidden.wait()

    def first(t, carry):
        rows = row_block(t, tile)
        hidden = acc[rows, :]
        dn = dn_s[rows, :]
        r = lax.rsqrt(jnp.mean(hidden * hidden, axis=-1, keepdims=True) + epsilon)
        scaled = dn * gains_ref[1:2, :]
        mean = jnp.mean(scaled * hidden, axis=-1, keepdims=True)
        dhid = cot_s[rows, :].astype(F32) + r * scaled - hidden * (r * r * r * mean)
        gmlp[...] += jnp.sum(dn * hidden * r, axis=0, keepdims=True)
        dn_s[rows, :] = dhid
        acc[rows, :] = jnp.zeros_like(dhid)
        low = dhid.astype(BF16)
        low_s[rows, :] = low
        grad = nt(low, wo[...].reshape(d, d)).astype(BF16)
        cot_s[rows, :] = grad
        mixed = mixed_s[rows, :]
        prod = grad.astype(F32) * mixed.astype(F32)
        high = prod.astype(BF16)
        rest = (prod - high.astype(F32)).astype(BF16)
        dsum[:, rows] = nt(pick, high) + nt(pick, rest)
        turned[:, rows] = jnp.transpose(mixed)
        return carry

    lax.fori_loop(0, tiles, first, 0)
    dmix = cot_s

    def weight_grads(target, right, start):
        cols = pl.ds(start, wide)
        target[:, :, :, :, cols] = nn(turned[...], right[:, cols]).astype(BF16).reshape(4, 2, 2, rows_own, wide)

    for i in range(thirds):
        weight_grads(wo, low_s, i * wide)
    s_o.start()

    def norm_again(t, carry):
        rows = row_block(t, tile)
        x = x_s[rows, :].astype(F32)
        r = lax.rsqrt(jnp.mean(x * x, axis=-1, keepdims=True) + epsilon)
        turned[:, rows] = jnp.transpose((x * r * gains_ref[0:1, :]).astype(BF16))
        return carry

    lax.fori_loop(0, tiles, norm_again, 0)
    for copy in get_last:
        copy.wait()
    s_o.add_core()
    pairs = HEADS // 2 // thirds
    per = pairs * tiles
    hooks = {
        1: each(AX, s_gu[3]) + each(SX, [s_d]), 2: each(AZ, s_gu[2]), 8: each(AY, s_gu[2]),
        7: each(AZ, s_gu[3]), 9: each(AX, [s_d]) + each(SX, [s_o]), 10: each(AC, s_qkv[0]), 11: each(AY, s_gu[3]) + each(AY, s_gu[0]), 12: each(AY, s_gu[1]),
        13: each(AX, [s_o]) + each(SX, s_qkv[0]), 16: each(AC, s_qkv[1]), 17: each(AX, s_qkv[0]) + each(SX, s_qkv[1]),
        18: each(AZ, [s_o]), 19: each(AZ, [s_d]), 21: each(AZ, s_qkv[0]) + each(AY, [s_o]),
        22: each(AX, s_qkv[1]), 23: each(AY, [s_d]),
    }

    def pair_step(s, carry, third):
        p, t = s // tiles + third * pairs, s % tiles
        cols = row_block(p, 128)
        for when, events in hooks.items():
            if third * per <= when < (third + 1) * per:
                pl.when(s == when - third * per)(functools.partial(run, events))

        @pl.when(t == 0)
        def _():
            kp = k_s[:, cols].astype(F32)
            kh[0], kh[1] = head_masks(kp, lane, bias)
            for h in range(2):
                own = (lane < 64) if h == 0 else (lane >= 64)
                kt[h] = jnp.transpose(jnp.where(own, kp, 0.0)).astype(BF16)
            qp = q_s[:, cols].astype(F32)
            qh[0] = jnp.where(lane == 64, 1.0, qp).astype(BF16)
            qh[1] = jnp.where(lane == 0, 1.0, qp).astype(BF16)
            qh[2], qh[3] = head_masks(qp, lane, 0.0)
            vh[0], vh[1] = head_masks(v_s[:, cols].astype(F32), lane, 0.0)
            dh[0], dh[1] = head_masks(dmix[:, cols].astype(F32), lane, 0.0)
            dqt[...] = jnp.zeros_like(dqt)

        rows = row_block(t, tile)
        d_k = d_v = d_q = None
        scores = [nt(kh[h, rows, :], qh[h]) for h in range(2)]
        d_atts = [nt(vh[h, rows, :], dmix[:, cols]) for h in range(2)]
        for h in range(2):
            weight = jnp.exp(scores[h] - lse_ref[pl.ds(2 * p + h, 1), :])
            d_score = (weight * (d_atts[h] - dsum[pl.ds(2 * p + h, 1), :])).astype(BF16)
            part_v = nn(weight.astype(BF16), dh[h])
            part_k = nn(d_score, qh[2 + h])
            part_q = nn(kt[h, :, rows], d_score)
            d_v = part_v if d_v is None else d_v + part_v
            d_k = part_k if d_k is None else d_k + part_k
            d_q = part_q if d_q is None else d_q + part_q
        dqt[...] += d_q
        k_s[rows, cols] = d_k.astype(BF16)
        v_s[rows, cols] = d_v.astype(BF16)

        @pl.when(t == tiles - 1)
        def _():
            q_s[:, cols] = jnp.transpose(dqt[...]).astype(BF16)

        return carry

    ggain[...] = jnp.zeros_like(ggain)
    gplots = low_s
    for third in range(thirds):
        lax.fori_loop(0, per, functools.partial(pair_step, third=third), 0)
        start = third * wide
        cols = pl.ds(start, wide)

        def flat_third(ref):
            return ref[:, :, :, :, cols].reshape(d, wide)

        def add_third(t, carry):
            rows = row_block(t, tile)
            acc[rows, :] += (nt(q_s[rows, cols], flat_third(wq)) + nt(k_s[rows, cols], flat_third(wk))
                             + nt(v_s[rows, cols], flat_third(wv)))
            return carry

        lax.fori_loop(0, tiles, add_third, 0)
        for target, right, out in zip((wq, wk, wv), (q_s, k_s, v_s), s_qkv[third]):
            weight_grads(target, right, start)
            out.start()

    def last(i, carry):
        t = (i + (tiles // 2) * (1 - place.y)) % tiles
        rows = row_block(t, tile)
        x = x_s[rows, :].astype(F32)
        dn = acc[rows, :]
        r = lax.rsqrt(jnp.mean(x * x, axis=-1, keepdims=True) + epsilon)
        scaled = dn * gains_ref[0:1, :]
        mean = jnp.mean(scaled * x, axis=-1, keepdims=True)
        gplots[rows, :] = (dn_s[rows, :] + r * scaled - x * (r * r * r * mean)).astype(BF16)
        ggain[...] += jnp.sum(dn * x * r, axis=0, keepdims=True)
        return carry

    gplots_far, gplots_near = half_out(gplots, gplots_out, 1)
    lax.fori_loop(0, tiles // 2, last, 0)
    gplots_far.start()
    for s in s_qkv[2]:
        s.add_core()
        s.send_x()
    lax.fori_loop(tiles // 2, tiles, last, 0)
    gplots_near.start()
    for w in range(16):
        z, x, c = w // 4, (w // 2) % 2, w % 2
        cols = slice(w * rows_own, (w + 1) * rows_own)
        own_gain[z, x, c, 0:1, 0:rows_own] = ggain[0:1, cols]
        own_gain[z, x, c, 1:2, 0:rows_own] = gmlp[0:1, cols]
    s_n.start()
    run(each(AY, s_qkv[0]))
    run(each(AZ, s_qkv[1]))
    s_n.add_core()
    s_n.send_x()
    for s in s_qkv[2] + [s_n]:
        s.add_x()
    run(each(AY, s_qkv[1]))
    for s in s_qkv[2] + [s_n]:
        s.add_z()
    for s in s_qkv[2] + [s_n]:
        s.add_y()
    for s in scatters + gathers:
        s.sent()
    x_far.wait_send()
    cot_far.wait_send()
    block_far.wait()
    block_near.wait()
    gplots_far.wait()
    gplots_near.wait()


def body_plot(plots, plot_grid, query_weight, key_weight, value_weight, out_weight, gate_weight, up_weight, down_weight,
              gain_attn, gain_mlp, cotangent):
    rows, d = query_weight.shape
    ff = gate_weight.shape[1]
    rows_down = down_weight.shape[0]
    half = plots.shape[1]
    slots = 2 * half
    counts = plot_grid[:, 0] * plot_grid[:, 1]
    count = lax.dynamic_slice(counts, (lax.axis_index("narrow"),), (1,))
    vm = lambda shape, dtype=BF16: pltpu.VMEM(shape, dtype)
    weights = [(4, 2, 2) + w.shape for w in (query_weight, key_weight, value_weight, out_weight, gate_weight, up_weight,
                                             down_weight)]
    sums = [(rows, d)] * 4 + [(rows, ff)] * 2 + [(rows_down, d), (8, 128)]
    any_spec, vmem_spec = pl.BlockSpec(memory_space=pl.ANY), pl.BlockSpec(memory_space=pltpu.VMEM)
    big = lambda dtype=BF16: pltpu.VMEM((slots, d), dtype)
    stage = {"g": (rows, ff), "u": (rows, ff), "d": (rows_down, d), "q": (rows, d), "k": (rows, d), "v": (rows, d),
             "o": (rows, d), "n": (8, 128)}
    stages = lambda names, lead: [vm(lead + stage[n], F32 if n == "n" else BF16) for n in names]
    dma = pltpu.SemaphoreType.DMA
    groups = 2 * CHUNKS + 2 + 9 + 1
    results = pl.pallas_call(
        layer,
        out_shape=[jax.ShapeDtypeStruct(plots.shape, BF16)] * 2 + [jax.ShapeDtypeStruct(shape, F32) for shape in sums]
        + [jax.ShapeDtypeStruct((slots, d), BF16)] * 3 + [jax.ShapeDtypeStruct((slots, d), F32)],
        in_specs=[pl.BlockSpec(memory_space=pltpu.SMEM)] + [any_spec] * 2 + [vmem_spec] * 9,
        out_specs=[any_spec] * 2 + [vmem_spec] * 8 + [any_spec] * 4,
        scratch_shapes=[vm(shape) for shape in weights]
        + [big() for _ in range(6)] + [big(F32), big(F32), big(), vm((d, slots)), big(), vm((ff // CHUNKS, slots))]
        + [vm((128, slots), F32), vm((128, slots), F32), vm((2, d), F32), vm((1, d), F32), vm((1, d), F32)]
        + [vm((4, slots, 128)), vm((2, slots, 128)), vm((2, slots, 128)), vm((2, slots, 128)), vm((2, 128, slots)),
           vm((128, slots), F32), vm((4, 2, 2, 8, 128), F32), vm((4, 2, 2, 8, 128), F32)]
        + stages("gudon", (4, 2)) + stages("gudqkvon", (4,)) + stages("gudqkvon", (3,)) + stages("gudqkvon", ())
        + [dma((8, 48)), dma((8, 32)), dma((6,)), dma((4,)), dma((groups, 6)), dma((groups, 6)), dma((4,)), dma((6,))],
        compiler_params=pltpu.CompilerParams(vmem_limit_bytes=VMEM_BYTES, collective_id=1, has_side_effects=True),
    )(count, plots, cotangent, gain_attn.reshape(1, -1), gain_mlp.reshape(1, -1), query_weight, key_weight, value_weight,
      out_weight, gate_weight, up_weight, down_weight)
    return (*results[:9], results[9][0, :rows], results[9][1, :rows])


def body_for(mesh):
    plots_fit = mesh.shape["narrow"] == 2 and mesh.shape["wide"] == 16

    def body(plots, *rest):
        if plots_fit and plots.shape == (2, 512, HEADS * HEAD_DIM):
            return body_plot(plots, *rest)
        return body_general(plots, *rest)

    return body


def solution(mesh):
    return jax.shard_map(
        body_for(mesh),
        mesh=mesh,
        in_specs=(
            P("wide", "narrow", None),
            P("wide", None),
            P("wide", None),
            P("wide", None),
            P("wide", None),
            P("wide", None),
            P("wide", None),
            P("wide", None),
            P("wide", None),
            P("wide"),
            P("wide"),
            P("wide", "narrow", None),
        ),
        out_specs=(
            P("wide", "narrow", None),
            P("wide", "narrow", None),
            P("wide", None),
            P("wide", None),
            P("wide", None),
            P("wide", None),
            P("wide", None),
            P("wide", None),
            P("wide", None),
            P("wide"),
            P("wide"),
        ),
        check_vma=False,
    )
```

```python
import functools

import jax
import jax.numpy as jnp
from jax import lax
from jax.experimental import pallas as pl
from jax.experimental.pallas import tpu as pltpu
from jax.sharding import PartitionSpec as P

HEADS = 12
HEAD_DIM = 64


epsilon = 1e-06


def norm_rows(values, gain):
    return values * lax.rsqrt(jnp.mean(values * values, axis=-1, keepdims=True) + epsilon) * gain


def gated(gate_pre, up_pre):
    return jax.nn.gelu(gate_pre, approximate=True) * up_pre


def to_heads(tensor):
    return tensor.reshape(tensor.shape[0], tensor.shape[1], HEADS, HEAD_DIM).transpose(2, 0, 1, 3)


def from_heads(tensor):
    return tensor.transpose(1, 2, 0, 3).reshape(tensor.shape[1], tensor.shape[2], HEADS * HEAD_DIM)


def masked_scores(query_one, keys_one, valid):
    scores = jnp.einsum("pqe,pke->pqk", query_one, keys_one, preferred_element_type=jnp.float32)
    return jnp.where(valid[:, None, :], scores, -1e30)


def weight_grad(left, right):
    return jnp.einsum("psd,pse->de", left, right, preferred_element_type=jnp.float32)


def back_product(grad_rows, weight):
    return jnp.einsum("pse,de->psd", grad_rows, weight, preferred_element_type=jnp.float32)


def forward_pass(inputs, weights, valid):
    (
        query_weight,
        key_weight,
        value_weight,
        out_weight,
        gate_weight,
        up_weight,
        down_weight,
        gain_attn,
        gain_mlp,
    ) = weights
    normed = norm_rows(inputs, gain_attn.astype(jnp.float32)).astype(jnp.bfloat16)
    query = jnp.dot(normed, query_weight, preferred_element_type=jnp.float32).astype(jnp.bfloat16)
    keys_local = jnp.dot(normed, key_weight, preferred_element_type=jnp.float32).astype(
        jnp.bfloat16
    )
    values_local = jnp.dot(normed, value_weight, preferred_element_type=jnp.float32).astype(
        jnp.bfloat16
    )
    keys_all, values_all = (
        lax.all_gather(keys_local, "narrow", axis=1, tiled=True),
        lax.all_gather(values_local, "narrow", axis=1, tiled=True),
    )
    query_heads = to_heads(query)
    key_heads = to_heads(keys_all)
    value_heads = to_heads(values_all)

    def head_forward(operands):
        query_one, keys_one, values_one = operands
        scores = masked_scores(query_one, keys_one, valid)
        row_max = jnp.max(scores, axis=-1, keepdims=True)
        exponent = jnp.exp(scores - row_max)
        total = jnp.sum(exponent, axis=-1, keepdims=True)
        mixed = jnp.einsum(
            "pqk,pke->pqe",
            (exponent / total).astype(jnp.bfloat16),
            values_one,
            preferred_element_type=jnp.float32,
        )
        return (mixed.astype(jnp.bfloat16), (row_max + jnp.log(total))[..., 0])

    mixed_heads, log_total = lax.map(head_forward, (query_heads, key_heads, value_heads))
    attended = from_heads(mixed_heads)
    hidden_in = inputs + jnp.dot(attended, out_weight, preferred_element_type=jnp.float32)
    normed_mlp = norm_rows(hidden_in, gain_mlp.astype(jnp.float32)).astype(jnp.bfloat16)
    gate_pre = jnp.dot(normed_mlp, gate_weight, preferred_element_type=jnp.float32)
    up_pre = jnp.dot(normed_mlp, up_weight, preferred_element_type=jnp.float32)
    activated = gated(gate_pre, up_pre).astype(jnp.bfloat16)
    output = hidden_in + jnp.dot(activated, down_weight, preferred_element_type=jnp.float32)
    saved = (
        normed,
        query_heads,
        key_heads,
        value_heads,
        log_total,
        attended,
        hidden_in,
        normed_mlp,
        gate_pre,
        up_pre,
        activated,
    )
    return (output, saved)


def body_general(
    plots,
    plot_grid,
    query_weight,
    key_weight,
    value_weight,
    out_weight,
    gate_weight,
    up_weight,
    down_weight,
    gain_attn,
    gain_mlp,
    cotangent,
):
    shards = (
        query_weight,
        key_weight,
        value_weight,
        out_weight,
        gate_weight,
        up_weight,
        down_weight,
        gain_attn,
        gain_mlp,
    )
    inputs = plots.astype(jnp.float32)
    counts = plot_grid[:, 0] * plot_grid[:, 1]
    length = plots.shape[1] * lax.axis_size("narrow")
    valid = jnp.arange(length)[None, :] < counts[:, None]
    weights = (
        lax.all_gather(shards[0], "wide", axis=0, tiled=True),
        lax.all_gather(shards[1], "wide", axis=0, tiled=True),
        lax.all_gather(shards[2], "wide", axis=0, tiled=True),
        lax.all_gather(shards[3], "wide", axis=0, tiled=True),
        lax.all_gather(shards[4], "wide", axis=0, tiled=True),
        lax.all_gather(shards[5], "wide", axis=0, tiled=True),
        lax.all_gather(shards[6], "wide", axis=0, tiled=True),
        lax.all_gather(shards[7], "wide", axis=0, tiled=True),
        lax.all_gather(shards[8], "wide", axis=0, tiled=True),
    )
    output, saved = forward_pass(inputs, weights, valid)
    weights = (
        lax.all_gather(shards[0], "wide", axis=0, tiled=True),
        lax.all_gather(shards[1], "wide", axis=0, tiled=True),
        lax.all_gather(shards[2], "wide", axis=0, tiled=True),
        lax.all_gather(shards[3], "wide", axis=0, tiled=True),
        lax.all_gather(shards[4], "wide", axis=0, tiled=True),
        lax.all_gather(shards[5], "wide", axis=0, tiled=True),
        lax.all_gather(shards[6], "wide", axis=0, tiled=True),
        lax.all_gather(shards[7], "wide", axis=0, tiled=True),
        lax.all_gather(shards[8], "wide", axis=0, tiled=True),
    )
    rerun, saved = forward_pass(inputs, weights, valid)
    (
        normed,
        query_heads,
        key_heads,
        value_heads,
        log_total,
        attended,
        hidden_in,
        normed_mlp,
        gate_pre,
        up_pre,
        activated,
    ) = saved
    (
        full_query,
        full_key,
        full_value,
        full_out,
        full_gate,
        full_up,
        full_down,
        full_gain_attn,
        full_gain_mlp,
    ) = weights
    grad_output = cotangent.astype(jnp.float32)
    grad_branch = grad_output.astype(jnp.bfloat16)
    grad_down = weight_grad(activated, grad_branch)
    grad_act = back_product(grad_branch, full_down)
    gate_value, gate_pull = jax.vjp(gated, gate_pre, up_pre)
    grad_gate_pre, grad_up_pre = gate_pull(grad_act)
    grad_gate_low = grad_gate_pre.astype(jnp.bfloat16)
    grad_up_low = grad_up_pre.astype(jnp.bfloat16)
    grad_gate = weight_grad(normed_mlp, grad_gate_low)
    grad_up = weight_grad(normed_mlp, grad_up_low)
    grad_normed_mlp = back_product(grad_gate_low, full_gate) + back_product(grad_up_low, full_up)
    norm_value, norm_pull = jax.vjp(norm_rows, hidden_in, full_gain_mlp.astype(jnp.float32))
    grad_hidden_norm, grad_gain_mlp = norm_pull(grad_normed_mlp)
    grad_hidden = grad_output + grad_hidden_norm
    grad_hidden_low = grad_hidden.astype(jnp.bfloat16)
    grad_out = weight_grad(attended, grad_hidden_low)
    grad_attended = back_product(grad_hidden_low, full_out).astype(jnp.bfloat16)
    grad_heads = to_heads(grad_attended)

    def head_backward(operands):
        query_one, keys_one, values_one, log_one, grad_one = operands
        scores = masked_scores(query_one, keys_one, valid)
        attention = jnp.exp(scores - log_one[..., None])
        grad_soft = jnp.einsum(
            "pqe,pke->pqk", grad_one, values_one, preferred_element_type=jnp.float32
        )
        row_dot = jnp.sum(attention * grad_soft, axis=-1, keepdims=True)
        grad_scores = (attention * (grad_soft - row_dot)).astype(jnp.bfloat16)
        grad_query_one = jnp.einsum(
            "pqk,pke->pqe", grad_scores, keys_one, preferred_element_type=jnp.float32
        )
        grad_keys_one = jnp.einsum(
            "pqk,pqe->pke", grad_scores, query_one, preferred_element_type=jnp.float32
        )
        grad_values_one = jnp.einsum(
            "pqk,pqe->pke",
            attention.astype(jnp.bfloat16),
            grad_one,
            preferred_element_type=jnp.float32,
        )
        return (grad_query_one, grad_keys_one, grad_values_one)

    grad_query_heads, grad_key_heads, grad_value_heads = lax.map(
        head_backward, (query_heads, key_heads, value_heads, log_total, grad_heads)
    )
    grad_key_local, grad_value_local = (
        lax.psum_scatter(
            grad_key_heads.astype(jnp.bfloat16), "narrow", scatter_dimension=2, tiled=True
        ).astype(jnp.float32),
        lax.psum_scatter(
            grad_value_heads.astype(jnp.bfloat16), "narrow", scatter_dimension=2, tiled=True
        ).astype(jnp.float32),
    )
    grad_query_low = from_heads(grad_query_heads).astype(jnp.bfloat16)
    grad_key_low = from_heads(grad_key_local).astype(jnp.bfloat16)
    grad_value_low = from_heads(grad_value_local).astype(jnp.bfloat16)
    grad_query = weight_grad(normed, grad_query_low)
    grad_key = weight_grad(normed, grad_key_low)
    grad_value = weight_grad(normed, grad_value_low)
    grad_normed = (
        back_product(grad_query_low, full_query)
        + back_product(grad_key_low, full_key)
        + back_product(grad_value_low, full_value)
    )
    first_value, first_pull = jax.vjp(norm_rows, inputs, full_gain_attn.astype(jnp.float32))
    grad_input_norm, grad_gain_attn = first_pull(grad_normed)
    grad_plots = (grad_hidden + grad_input_norm).astype(jnp.bfloat16)
    owned = (
        lax.psum_scatter(
            grad_query.astype(jnp.bfloat16), "wide", scatter_dimension=0, tiled=True
        ).astype(jnp.float32),
        lax.psum_scatter(
            grad_key.astype(jnp.bfloat16), "wide", scatter_dimension=0, tiled=True
        ).astype(jnp.float32),
        lax.psum_scatter(
            grad_value.astype(jnp.bfloat16), "wide", scatter_dimension=0, tiled=True
        ).astype(jnp.float32),
        lax.psum_scatter(
            grad_out.astype(jnp.bfloat16), "wide", scatter_dimension=0, tiled=True
        ).astype(jnp.float32),
        lax.psum_scatter(
            grad_gate.astype(jnp.bfloat16), "wide", scatter_dimension=0, tiled=True
        ).astype(jnp.float32),
        lax.psum_scatter(
            grad_up.astype(jnp.bfloat16), "wide", scatter_dimension=0, tiled=True
        ).astype(jnp.float32),
        lax.psum_scatter(
            grad_down.astype(jnp.bfloat16), "wide", scatter_dimension=0, tiled=True
        ).astype(jnp.float32),
        lax.psum_scatter(
            grad_gain_attn.astype(jnp.bfloat16), "wide", scatter_dimension=0, tiled=True
        ).astype(jnp.float32),
        lax.psum_scatter(
            grad_gain_mlp.astype(jnp.bfloat16), "wide", scatter_dimension=0, tiled=True
        ).astype(jnp.float32),
    )
    summed = (
        lax.psum(owned[0].astype(jnp.bfloat16), "narrow").astype(jnp.float32),
        lax.psum(owned[1].astype(jnp.bfloat16), "narrow").astype(jnp.float32),
        lax.psum(owned[2].astype(jnp.bfloat16), "narrow").astype(jnp.float32),
        lax.psum(owned[3].astype(jnp.bfloat16), "narrow").astype(jnp.float32),
        lax.psum(owned[4].astype(jnp.bfloat16), "narrow").astype(jnp.float32),
        lax.psum(owned[5].astype(jnp.bfloat16), "narrow").astype(jnp.float32),
        lax.psum(owned[6].astype(jnp.bfloat16), "narrow").astype(jnp.float32),
        lax.psum(owned[7].astype(jnp.bfloat16), "narrow").astype(jnp.float32),
        lax.psum(owned[8].astype(jnp.bfloat16), "narrow").astype(jnp.float32),
    )
    return (
        output.astype(jnp.bfloat16),
        grad_plots,
        summed[0],
        summed[1],
        summed[2],
        summed[3],
        summed[4],
        summed[5],
        summed[6],
        summed[7],
        summed[8],
    )


F32, BF16 = jnp.float32, jnp.bfloat16
ROOT = 0.7978845608028654
CUBE = 0.044715
VMEM_BYTES = 62 << 20


def nn(left, right):
    return lax.dot_general(left, right, (((1,), (0,)), ((), ())), preferred_element_type=F32)


def nt(left, right):
    return lax.dot_general(left, right, (((1,), (1,)), ((), ())), preferred_element_type=F32)


def lanes_of(rows, width=128):
    return lax.broadcasted_iota(jnp.int32, (rows, width), 1)


def row_block(index, size):
    return pl.ds(pl.multiple_of(index * size, size), size)


def head_masks(pair, lane, flag):
    first = jnp.where(lane < 64, pair, jnp.where(lane == 64, flag, 0.0))
    second = jnp.where(lane >= 64, pair, jnp.where(lane == 0, flag, 0.0))
    return first.astype(BF16), second.astype(BF16)


MESH_ID = pl.DeviceIdType.MESH


class Place:
    def __init__(self):
        wide, self.y = lax.axis_index("wide"), lax.axis_index("narrow")
        self.z, self.x, self.c = wide // 4, (wide // 2) % 2, wide % 2
        self.wide = wide

    def block(self, z, x, c):
        return (z * 2 + x) * 2 + c

    def other_z(self, j):
        z = self.z
        return (z + 1 - 2 * (z % 2), (z + 2) % 4, 3 - z)[j]

    def to_z(self, j):
        return (self.block(self.other_z(j), self.x, self.c), self.y)

    def at_z(self, z):
        return (self.block(z, self.x, self.c), self.y)

    def to_x(self):
        return (self.block(self.z, 1 - self.x, self.c), self.y)

    def to_core(self):
        return (self.block(self.z, self.x, 1 - self.c), self.y)

    def to_y(self):
        return (self.wide, 1 - self.y)

    def greet(self):
        barrier = pltpu.get_barrier_semaphore()
        partners = [self.to_z(0), self.to_z(1), self.to_z(2), self.to_x(), self.to_core(), self.to_y()]
        for partner in partners:
            pl.semaphore_signal(barrier, inc=1, device_id=partner, device_id_type=MESH_ID)
        pl.semaphore_wait(barrier, len(partners))


class Gather:
    def __init__(self, place, full, send, recv, halves):
        self.place, self.full, self.sends, self.recvs, self.halves = place, full, send, recv, halves
        self.width = full.shape[4] // 2
        self.pending = {}
        self.settled = set()

    def view(self, spot, half):
        if self.halves:
            return self.full.at[(*spot, slice(None), row_block(half, self.width))]
        return self.full.at[spot]

    def copy(self, spot, half, target, slot):
        view = self.view(spot, half)
        block = self.place.block(*spot)
        return pltpu.make_async_remote_copy(
            src_ref=view, dst_ref=view, send_sem=self.sends.at[slot], recv_sem=self.recvs.at[block * 2 + half],
            device_id=target, device_id_type=MESH_ID)

    def send(self, name, spot, half, target, when=None):
        slot = self.pending.setdefault(name, (len(self.pending), when))[0]
        if when is None:
            self.copy(spot, half, target, slot).start()
        else:
            pl.when(when())(lambda: self.copy(spot, half, target, slot).start())

    def wait(self, spot, half):
        self.copy(spot, half, self.place.to_core(), 0).wait_recv()

    def first(self):
        return self.place.y if self.halves else 0

    def start(self):
        p = self.place
        own = (p.z, p.x, p.c)
        self.send("up", own, self.first(), p.at_z(p.z + 1), lambda: p.z < 3)
        self.send("down", own, self.first(), p.at_z(p.z - 1), lambda: p.z > 0)
        self.send("x", own, self.first(), p.to_x())
        for half in range(2 if self.halves else 1):
            self.send(("core", half), own, half, p.to_core())

    def pass_z(self, hops):
        p = self.place
        z = p.z + hops
        onward = p.z + (1 if hops < 0 else -1)
        block = (z, p.x, p.c)

        def there():
            return (p.z >= -hops) if hops < 0 else (p.z <= 3 - hops)

        def inside():
            return jnp.logical_and(there(), (p.z < 3) if hops < 0 else (p.z > 0))

        pl.when(there())(lambda: self.wait(block, self.first()))
        self.send(("z", hops), block, self.first(), p.at_z(onward), inside)
        self.send(("zx", hops), block, self.first(), p.to_x(), there)
        if self.halves:
            self.send(("zy", hops), block, self.first(), p.to_y(), there)
        self.send(("zc", hops), block, self.first(), p.to_core(), there)

    def pass_x(self, hops):
        p = self.place
        block = ((p.z + hops) % 4, 1 - p.x, p.c)
        self.wait(block, self.first())
        if self.halves:
            self.send(("xy", hops), block, self.first(), p.to_y())
        self.send(("xc", hops), block, self.first(), p.to_core())

    def pass_y(self, hops, across):
        p = self.place
        block = ((p.z + hops) % 4, 1 - p.x if across else p.x, p.c)
        self.wait(block, 1 - p.y)
        self.send(("yc", hops, across), block, 1 - p.y, p.to_core())

    def end(self, half=0):
        p = self.place
        for z in range(4):
            for x in range(2):
                self.wait((z, x, 1 - p.c), half)

    def sent(self):
        for name, (slot, when) in self.pending.items():
            if name in self.settled:
                continue
            self.settled.add(name)
            wait = lambda slot=slot: self.copy((0, 0, 0), 0, self.place.to_core(), slot).wait_send()
            if when is None:
                wait()
            else:
                pl.when(when())(wait)

    def pass_both(self, hops):
        self.pass_z(-hops)
        self.pass_z(hops)

    def relay_z(self):
        for hops in (1, 2, 3):
            self.pass_both(hops)

    def relay_x(self):
        for hops in (0, 1, 3, 2):
            self.pass_x(hops)

    def relay_y(self):
        if self.halves:
            for hops in (1, 3, 2):
                self.pass_y(hops, False)
            for hops in (0, 1, 3, 2):
                self.pass_y(hops, True)


def relay_order(gathers, ahead):
    order = [gather.start for gather in gathers[:ahead]]
    for i in range(len(gathers) + 1):
        along_z, along_x = [], []
        if i < len(gathers):
            for hops in (1, 2, 3):
                along_z.append(functools.partial(gathers[i].pass_both, hops))
        if i > 0:
            for hops in (0, 1, 3, 2):
                along_x.append(functools.partial(gathers[i - 1].pass_x, hops))
        if i + ahead < len(gathers):
            along_z.insert(1, gathers[i + ahead].start)
        while along_z or along_x:
            if along_z:
                order.append(along_z.pop(0))
            if along_x:
                order.append(along_x.pop(0))
    return order


class Scatter:
    def __init__(self, place, grad, start, width, stages, at, out, send, recv):
        self.place, self.grad, self.cols, self.at = place, grad, pl.ds(start, width), pl.ds(at, width)
        self.recv_c, self.recv_x, self.recv_z, self.recv_y = stages
        self.out, self.sends, self.recvs = out, send, recv

    def copy(self, stage, source, target, device):
        return pltpu.make_async_remote_copy(
            src_ref=source, dst_ref=target, send_sem=self.sends.at[stage], recv_sem=self.recvs.at[stage],
            device_id=device, device_id_type=MESH_ID)

    def core_copy(self):
        p = self.place
        return self.copy(0, self.grad.at[:, :, 1 - p.c, :, self.cols], self.recv_c.at[:, :, :, self.at], p.to_core())

    def x_copy(self):
        p = self.place
        return self.copy(1, self.grad.at[:, 1 - p.x, p.c, :, self.cols], self.recv_x.at[:, :, self.at], p.to_x())

    def z_copy(self, j):
        p = self.place
        return self.copy(2 + j, self.grad.at[p.other_z(j), p.x, p.c, :, self.cols], self.recv_z.at[j, :, self.at], p.to_z(j))

    def y_copy(self):
        p = self.place
        return self.copy(5, self.grad.at[p.z, p.x, p.c, :, self.cols], self.recv_y.at[:, self.at], p.to_y())

    def start(self):
        self.core_copy().start()

    def add_core(self):
        self.core_copy().wait_recv()
        c = self.place.c

        def step(i, carry):
            z, x = i // 2, i % 2
            self.grad[z, x, c, :, self.cols] = self.grad[z, x, c, :, self.cols] + self.recv_c[z, x, :, self.at]
            return carry

        lax.fori_loop(0, 8, step, 0)

    def send_x(self):
        self.x_copy().start()

    def add_x(self):
        self.x_copy().wait_recv()
        x, c = self.place.x, self.place.c

        def step(z, carry):
            self.grad[z, x, c, :, self.cols] = self.grad[z, x, c, :, self.cols] + self.recv_x[z, :, self.at]
            return carry

        lax.fori_loop(0, 4, step, 0)
        for j in (2, 1, 0):
            self.z_copy(j).start()

    def add_z(self):
        for j in range(3):
            self.z_copy(j).wait_recv()
        z, x, c = self.place.z, self.place.x, self.place.c
        total = self.grad[z, x, c, :, self.cols].astype(F32)
        for j in range(3):
            total = total + self.recv_z[j, :, self.at].astype(F32)
        self.grad[z, x, c, :, self.cols] = total.astype(self.grad.dtype)
        self.y_copy().start()

    def add_y(self):
        self.y_copy().wait_recv()
        z, x, c = self.place.z, self.place.x, self.place.c
        self.out[:, self.cols] = self.grad[z, x, c, :, self.cols].astype(F32) + self.recv_y[:, self.at].astype(F32)

    def sent(self):
        self.core_copy().wait_send()
        self.x_copy().wait_send()
        for j in range(3):
            self.z_copy(j).wait_send()
        self.y_copy().wait_send()


CHUNKS = 4


def layer(count_ref, plots_hbm, cot_hbm, gain_a_ref, gain_m_ref, own_q, own_k, own_v, own_o, own_g, own_u, own_d,
          block_out, gplots_out, sum_q, sum_k, sum_v, sum_o, sum_g, sum_u, sum_d, sum_gain, park_q, park_k, park_v, park_h,
          wq, wk, wv, wo, wg, wu, wd, x_s, q_s, k_s, v_s, mixed_s, cot_s, acc, dn_s, low_s, turned, block_s, actt,
          dsum, lse_ref, gains_ref, ggain, gmlp, qh, kh, vh, dh, kt, dqt, own_gain, wgain,
          c_g, c_u, c_d, c_o, c_n, x_g, x_u, x_d, x_q, x_k, x_v, x_o, x_n,
          z_g, z_u, z_d, z_q, z_k, z_v, z_o, z_n, y_g, y_u, y_d, y_q, y_k, y_v, y_o, y_n,
          sends_w, recvs_w, half_sems, park_sems, sends, recvs, load_sems, out_sems):
    half = plots_hbm.shape[1]
    slots = 2 * half
    d = plots_hbm.shape[2]
    tile_f = 512
    tiles_f = slots // tile_f
    pairs_f = HEADS // 2
    tile = 256
    tiles = slots // tile
    ff = wg.shape[4]
    place = Place()
    mine = pl.ds(pl.multiple_of(place.y * half, half), half)

    def half_copies(source, target, i):
        far = pltpu.make_async_remote_copy(
            src_ref=source.at[1 - place.y], dst_ref=target.at[mine], send_sem=half_sems.at[3 * i],
            recv_sem=half_sems.at[3 * i + 1], device_id=place.to_y(), device_id_type=MESH_ID)
        near = pltpu.make_async_copy(source.at[place.y], target.at[mine], half_sems.at[3 * i + 2])
        return far, near

    x_far, x_near = half_copies(plots_hbm, x_s, 0)
    cot_far, cot_near = half_copies(cot_hbm, cot_s, 1)
    x_near.start()
    cot_near.start()
    fulls = (wgain, wq, wk, wv, wo, wd, wg, wu)
    here = (place.z, place.x, place.c)
    for full, own in zip(fulls[1:], (own_q, own_k, own_v, own_o, own_d, own_g, own_u)):
        full[here] = own[...]
    rows_own = own_q.shape[0]
    wgain[(*here, slice(0, 1), slice(0, rows_own))] = gain_a_ref[...].astype(F32)
    wgain[(*here, slice(1, 2), slice(0, rows_own))] = gain_m_ref[...].astype(F32)
    gathers = [Gather(place, full, sends_w.at[i], recvs_w.at[i], full is wg or full is wu) for i, full in enumerate(fulls)]
    g_gain, g_q, g_k, g_v, g_o, g_d, g_g, g_u = gathers
    copies = []

    def put(source, target):
        copy = pltpu.make_async_copy(source, target, park_sems.at[len(copies)])
        copy.start()
        copies.append(copy)

    place.greet()
    x_far.start()
    g_gain.start()
    order = relay_order(gathers[1:], 2)

    def relay(events):
        for event in events:
            event()

    def find(gather, kind, hops):
        for i, event in enumerate(order):
            if getattr(event, "func", None) == kind and event.args == (hops,):
                return i + 1
        raise ValueError(hops)

    done_q = find(g_q, g_q.pass_x, 2)
    done_k = find(g_k, g_k.pass_x, 2)
    done_v = find(g_v, g_v.pass_x, 2)
    relay(order[:done_q])
    g_gain.relay_z()
    g_gain.relay_x()
    g_gain.end()
    for w in range(16):
        for i in range(2):
            gains_ref[i:i + 1, w * rows_own:(w + 1) * rows_own] = wgain[w // 4, (w // 2) % 2, w % 2, i:i + 1, 0:rows_own]
    relay(order[done_q:done_k])
    x_far.wait_recv()
    x_near.wait()
    cot_far.start()

    def normalise(t, carry):
        rows = row_block(t, 256)
        x = x_s[rows, :].astype(F32)
        r = lax.rsqrt(jnp.mean(x * x, axis=-1, keepdims=True) + epsilon)
        low_s[rows, :] = (x * r * gains_ref[0:1, :]).astype(BF16)
        return carry

    lax.fori_loop(0, slots // 256, normalise, 0)

    def project(target, full, out):
        def step(t, carry):
            rows = row_block(t, 512)
            target[rows, :] = nn(low_s[rows, :], full[...].reshape(d, d)).astype(BF16)
            return carry

        lax.fori_loop(0, slots // 512, step, 0)
        put(target, out)

    g_q.end()
    project(q_s, wq, park_q)
    relay(order[done_k:done_v])
    g_k.end()
    project(k_s, wk, park_k)
    g_v.end()
    project(v_s, wv, park_v)

    count = count_ref[0]
    lane = lanes_of(slots)
    slot = lax.broadcasted_iota(jnp.int32, (slots, 128), 0)
    bias = jnp.where(slot < count, 0.0, -1e30)
    lse_cols = pl.ds(0, 128)
    dn_s[:, lse_cols] = jnp.zeros((slots, 128), F32)
    values = [pl.ds(256 * h, 128) for h in range(2)]
    values_ones = [pl.ds(256 * h, 256) for h in range(2)]
    for h in range(2):
        block_s[:, 256 * h + 128:256 * h + 256] = jnp.ones((slots, 128), BF16)
    steps = pairs_f * tiles_f
    late = order[done_v:]
    first, per = 4, 1.7
    cuts = [min(len(late), int(first + per * s)) for s in range(steps)]
    hooks = [late[:cuts[0]]] + [late[cuts[s - 1]:cuts[s]] for s in range(1, steps)]

    def forward_step(s, carry):
        p, t = s // tiles_f, s % tiles_f
        cols = row_block(p, 128)
        for when, events in enumerate(hooks):
            pl.when(s == when)(functools.partial(relay, events))

        @pl.when(t == 0)
        def _():
            kh[0], kh[1] = head_masks(k_s[:, cols].astype(F32), lane, bias)
            qp = q_s[:, cols].astype(F32)
            qh[0] = jnp.where(lane == 64, 1.0, qp).astype(BF16)
            qh[1] = jnp.where(lane == 0, 1.0, qp).astype(BF16)
            block_s[:, values[0]], block_s[:, values[1]] = head_masks(v_s[:, cols].astype(F32), lane, 0.0)

        rows = row_block(t, tile_f)
        total = None
        cols_out = dn_s[rows, lse_cols]
        scores = [nt(qh[h, rows, :], kh[h]) for h in range(2)]
        for h in range(2):
            top = jnp.max(scores[h], axis=1, keepdims=True)
            weight = jnp.exp(scores[h] - top).astype(BF16)
            out = nn(weight, block_s[:, values_ones[h]])
            part = out[:, :128] / out[:, 128:]
            total = part if total is None else total + part
            cols_out = jnp.where(lanes_of(tile_f) == 2 * p + h, top + jnp.log(out[:, 128:]), cols_out)
        mixed_s[rows, cols] = total.astype(BF16)
        dn_s[rows, lse_cols] = cols_out
        return carry

    lax.fori_loop(0, steps, forward_step, 0)
    g_o.end()

    def project_out(t, carry):
        rows = row_block(t, tile)
        hidden = x_s[rows, :].astype(F32) + nn(mixed_s[rows, :], wo[...].reshape(d, d))
        acc[rows, :] = hidden
        lse_ref[:, rows] = jnp.transpose(dn_s[rows, lse_cols])
        r = lax.rsqrt(jnp.mean(hidden * hidden, axis=-1, keepdims=True) + epsilon)
        low = (hidden * r * gains_ref[1:2, :]).astype(BF16)
        low_s[rows, :] = low
        turned[:, rows] = jnp.transpose(low)
        dn_s[rows, :] = jnp.zeros_like(hidden)
        return carry

    lax.fori_loop(0, tiles, project_out, 0)
    put(acc, park_h)
    relay(late[cuts[-1]:])
    cot_far.wait_recv()
    cot_near.wait()
    g_d.end()
    g_g.end(place.y)
    g_u.end(place.y)
    for g in (g_gain, g_q, g_k, g_v, g_o, g_d):
        g.sent()
    for copy in copies:
        copy.wait()

    def load(source, target, i):
        copy = pltpu.make_async_copy(source, target, load_sems.at[i])
        copy.start()
        return copy

    scatters = []

    def scatter(grad, start, width, stages, at, out, i=None):
        i = len(scatters) if i is None else i
        scatters.append(Scatter(place, grad, start, width, stages, at, out, sends.at[i], recvs.at[i]))
        return scatters[-1]

    width = ff // CHUNKS
    s_gu = []
    chunks = [(f + 2 * place.y) % CHUNKS for f in range(CHUNKS)]
    starts = [pl.multiple_of(f * width, width) for f in chunks]
    for f, start in zip(chunks, starts):
        s_gu.append([scatter(wg, start, width, (c_g, x_g, z_g, y_g), start, sum_g, 2 * f),
                     scatter(wu, start, width, (c_u, x_u, z_u, y_u), start, sum_u, 2 * f + 1)])
    s_d = scatter(wd, 0, d, (c_d, x_d, z_d, y_d), 0, sum_d)
    s_o = scatter(wo, 0, d, (c_o, x_o, z_o, y_o), 0, sum_o)
    pair_groups = ((0, 3), (3, 5), (5, 6))
    s_qkv = []
    for low, high in pair_groups:
        at, wide = 128 * low, 128 * (high - low)
        s_qkv.append([scatter(wq, at, wide, (c_g.at[:, :, :, pl.ds(0, d)], x_q, z_q, y_q), at, sum_q),
                      scatter(wk, at, wide, (c_g.at[:, :, :, pl.ds(d, d)], x_k, z_k, y_k), at, sum_k),
                      scatter(wv, at, wide, (c_u.at[:, :, :, pl.ds(0, d)], x_v, z_v, y_v), at, sum_v)])
    s_n = scatter(own_gain, 0, 128, (c_n, x_n, z_n, y_n), 0, sum_gain)
    other = pl.ds(pl.multiple_of((1 - place.y) * half, half), half)

    def half_out(source, target, i):
        far = pltpu.make_async_remote_copy(
            src_ref=source.at[other], dst_ref=target.at[place.y], send_sem=out_sems.at[3 * i],
            recv_sem=out_sems.at[3 * i + 1], device_id=place.to_y(), device_id_type=MESH_ID)
        near = pltpu.make_async_copy(source.at[mine], target.at[place.y], out_sems.at[3 * i + 2])
        return far, near

    chunk = pl.ds(0, width)

    def flat(ref, start):
        return ref[:, :, :, :, pl.ds(start, width)].reshape(d, width)

    def run(events):
        for event in events:
            event()

    def each(kind, group):
        return [functools.partial(kind, s) for s in group]

    C, AC, SX, AX, AZ, AY = Scatter.start, Scatter.add_core, Scatter.send_x, Scatter.add_x, Scatter.add_z, Scatter.add_y
    for f, (spot, start) in enumerate(zip(chunks, starts)):
        if f == 2:
            g_u.relay_y()
            g_g.end(1 - place.y)
            g_u.end(1 - place.y)

        def elem(t, carry):
            rows = row_block(t, 512)
            gate_pre = nn(low_s[rows, :], flat(wg, start))
            up_pre = nn(low_s[rows, :], flat(wu, start))
            d_act = nt(cot_s[rows, :], wd[spot].reshape(width, d))
            square = gate_pre * gate_pre
            th = jnp.tanh(gate_pre * (ROOT + (ROOT * CUBE) * square))
            part = 0.5 + 0.5 * th
            gelu = gate_pre * part
            slope = part + gelu * (1.0 - th) * (ROOT + (3.0 * CUBE * ROOT) * square)
            act = (gelu * up_pre).astype(BF16)
            q_s[rows, chunk] = act
            actt[:, rows] = jnp.transpose(act)
            k_s[rows, chunk] = (d_act * up_pre * slope).astype(BF16)
            v_s[rows, chunk] = (d_act * gelu).astype(BF16)
            return carry

        lax.fori_loop(0, slots // 512, elem, 0)
        if f == 0:
            g_g.relay_y()
        if f >= 2:
            run(each(AX, s_gu[f - 2]))
        if f >= 1:
            for s in s_gu[f - 1]:
                s.add_core()
                s.send_x()

        def add_up(t, carry):
            rows = row_block(t, 512)
            acc[rows, :] += nn(q_s[rows, chunk], wd[spot].reshape(width, d))
            dn_s[rows, :] += nt(k_s[rows, chunk], flat(wg, start)) + nt(v_s[rows, chunk], flat(wu, start))
            return carry

        lax.fori_loop(0, slots // 512, add_up, 0)
        if f >= 3:
            run(each(AZ, s_gu[f - 3]))
        if f in (0, 2):
            g_g.sent()
        wg[:, :, :, :, pl.ds(start, width)] = nn(turned[...], k_s[:, chunk]).astype(BF16).reshape(wg.shape[:4] + (width,))
        s_gu[f][0].start()
        if f in (0, 2):
            g_u.sent()
        wu[:, :, :, :, pl.ds(start, width)] = nn(turned[...], v_s[:, chunk]).astype(BF16).reshape(wg.shape[:4] + (width,))
        s_gu[f][1].start()
        wd[spot] = nn(actt[...], cot_s[...]).astype(BF16).reshape(wd.shape[1:])
    get_last = [load(park_q, q_s, 0), load(park_k, k_s, 1), load(park_v, v_s, 2)]
    s_d.start()

    def block_step(t, carry):
        rows = row_block(t, tile)
        block_s[rows, :] = acc[rows, :].astype(BF16)
        return carry

    lax.fori_loop(0, tiles, block_step, 0)
    get_hidden = load(park_h, acc, 3)
    block_far, block_near = half_out(block_s, block_out, 0)
    block_far.start()
    block_near.start()
    run(each(AX, s_gu[2]))
    for s in s_gu[3]:
        s.add_core()
        s.send_x()
    head_row = lax.broadcasted_iota(jnp.int32, (128, d), 0)
    head_col = lax.broadcasted_iota(jnp.int32, (128, d), 1)
    pick = jnp.where(head_col // HEAD_DIM == head_row, 1.0, 0.0).astype(BF16)
    gmlp[...] = jnp.zeros_like(gmlp)
    run(each(AZ, s_gu[1]))
    s_d.add_core()
    get_hidden.wait()

    def first(t, carry):
        rows = row_block(t, tile)
        hidden = acc[rows, :]
        dn = dn_s[rows, :]
        r = lax.rsqrt(jnp.mean(hidden * hidden, axis=-1, keepdims=True) + epsilon)
        scaled = dn * gains_ref[1:2, :]
        mean = jnp.mean(scaled * hidden, axis=-1, keepdims=True)
        dhid = cot_s[rows, :].astype(F32) + r * scaled - hidden * (r * r * r * mean)
        gmlp[...] += jnp.sum(dn * hidden * r, axis=0, keepdims=True)
        dn_s[rows, :] = dhid
        acc[rows, :] = jnp.zeros_like(dhid)
        low = dhid.astype(BF16)
        low_s[rows, :] = low
        grad = nt(low, wo[...].reshape(d, d)).astype(BF16)
        cot_s[rows, :] = grad
        mixed = mixed_s[rows, :]
        prod = grad.astype(F32) * mixed.astype(F32)
        high = prod.astype(BF16)
        rest = (prod - high.astype(F32)).astype(BF16)
        dsum[:, rows] = nt(pick, high) + nt(pick, rest)
        turned[:, rows] = jnp.transpose(mixed)
        return carry

    lax.fori_loop(0, tiles, first, 0)
    dmix = cot_s

    def weight_grads(target, right, start, wide):
        cols = pl.ds(start, wide)
        target[:, :, :, :, cols] = nn(turned[...], right[:, cols]).astype(BF16).reshape(4, 2, 2, rows_own, wide)

    for i in range(3):
        weight_grads(wo, low_s, i * (d // 3), d // 3)
    s_o.start()

    def norm_again(t, carry):
        rows = row_block(t, tile)
        x = x_s[rows, :].astype(F32)
        r = lax.rsqrt(jnp.mean(x * x, axis=-1, keepdims=True) + epsilon)
        turned[:, rows] = jnp.transpose((x * r * gains_ref[0:1, :]).astype(BF16))
        return carry

    lax.fori_loop(0, tiles, norm_again, 0)
    for copy in get_last:
        copy.wait()
    s_o.add_core()
    hooks = {
        3: each(AX, s_gu[3]) + each(SX, [s_d]), 4: each(AZ, s_gu[2]), 10: each(AZ, s_gu[3]), 11: each(AY, s_gu[2]),
        13: each(AX, [s_d]) + each(SX, [s_o]), 14: each(AC, s_qkv[0]), 15: each(AY, s_gu[3]) + each(AY, s_gu[0]), 16: each(AY, s_gu[1]),
        17: each(AX, [s_o]) + each(SX, s_qkv[0]), 21: each(AZ, [s_o]) + each(AC, s_qkv[1]),
        22: each(AX, s_qkv[0]) + each(SX, s_qkv[1]), 23: each(AZ, [s_d]) + each(AY, [s_o]),
    }

    def pair_step(s, carry, low, high):
        p, t = s // tiles, s % tiles
        cols = row_block(p, 128)
        for when, events in hooks.items():
            if low * tiles <= when < high * tiles:
                pl.when(s == when)(functools.partial(run, events))

        @pl.when(t == 0)
        def _():
            kp = k_s[:, cols].astype(F32)
            kh[0], kh[1] = head_masks(kp, lane, bias)
            for h in range(2):
                own = (lane < 64) if h == 0 else (lane >= 64)
                kt[h] = jnp.transpose(jnp.where(own, kp, 0.0)).astype(BF16)
            qp = q_s[:, cols].astype(F32)
            qh[0] = jnp.where(lane == 64, 1.0, qp).astype(BF16)
            qh[1] = jnp.where(lane == 0, 1.0, qp).astype(BF16)
            qh[2], qh[3] = head_masks(qp, lane, 0.0)
            vh[0], vh[1] = head_masks(v_s[:, cols].astype(F32), lane, 0.0)
            dh[0], dh[1] = head_masks(dmix[:, cols].astype(F32), lane, 0.0)
            dqt[...] = jnp.zeros_like(dqt)

        rows = row_block(t, tile)
        d_k = d_v = d_q = None
        scores = [nt(kh[h, rows, :], qh[h]) for h in range(2)]
        d_atts = [nt(vh[h, rows, :], dmix[:, cols]) for h in range(2)]
        for h in range(2):
            weight = jnp.exp(scores[h] - lse_ref[pl.ds(2 * p + h, 1), :])
            d_score = (weight * (d_atts[h] - dsum[pl.ds(2 * p + h, 1), :])).astype(BF16)
            part_v = nn(weight.astype(BF16), dh[h])
            part_k = nn(d_score, qh[2 + h])
            part_q = nn(kt[h, :, rows], d_score)
            d_v = part_v if d_v is None else d_v + part_v
            d_k = part_k if d_k is None else d_k + part_k
            d_q = part_q if d_q is None else d_q + part_q
        dqt[...] += d_q
        k_s[rows, cols] = d_k.astype(BF16)
        v_s[rows, cols] = d_v.astype(BF16)

        @pl.when(t == tiles - 1)
        def _():
            q_s[:, cols] = jnp.transpose(dqt[...]).astype(BF16)

        return carry

    ggain[...] = jnp.zeros_like(ggain)
    gplots = low_s
    def finish_group(group):
        for target, right, out in zip((wq, wk, wv), (q_s, k_s, v_s), s_qkv[group]):
            low, high = pair_groups[group]
            weight_grads(target, right, 128 * low, 128 * (high - low))
            out.start()

    for group, (low, high) in enumerate(pair_groups):
        lax.fori_loop(low * tiles, high * tiles, functools.partial(pair_step, low=low, high=high), 0)
        wide = 128 * (high - low)
        cols = pl.ds(128 * low, wide)

        def flat_group(ref):
            return ref[:, :, :, :, cols].reshape(d, wide)

        def group_part(rows):
            return (nt(q_s[rows, cols], flat_group(wq)) + nt(k_s[rows, cols], flat_group(wk))
                    + nt(v_s[rows, cols], flat_group(wv)))

        def add_group(t, carry):
            rows = row_block(t, tile)
            acc[rows, :] += group_part(rows)
            return carry

        if high < HEADS // 2:
            lax.fori_loop(0, tiles, add_group, 0)
            finish_group(group)

    def last(i, carry):
        t = (i + (tiles // 2) * (1 - place.y)) % tiles
        rows = row_block(t, tile)
        x = x_s[rows, :].astype(F32)
        dn = acc[rows, :] + group_part(rows)
        r = lax.rsqrt(jnp.mean(x * x, axis=-1, keepdims=True) + epsilon)
        scaled = dn * gains_ref[0:1, :]
        mean = jnp.mean(scaled * x, axis=-1, keepdims=True)
        gplots[rows, :] = (dn_s[rows, :] + r * scaled - x * (r * r * r * mean)).astype(BF16)
        ggain[...] += jnp.sum(dn * x * r, axis=0, keepdims=True)
        return carry

    gplots_far, gplots_near = half_out(gplots, gplots_out, 1)
    lax.fori_loop(0, tiles // 2, last, 0)
    gplots_far.start()
    lax.fori_loop(tiles // 2, tiles, last, 0)
    finish_group(2)
    run(each(AX, s_qkv[1]))
    for s in s_qkv[2]:
        s.add_core()
        s.send_x()
    gplots_near.start()
    for w in range(16):
        z, x, c = w // 4, (w // 2) % 2, w % 2
        cols = slice(w * rows_own, (w + 1) * rows_own)
        own_gain[z, x, c, 0:1, 0:rows_own] = ggain[0:1, cols]
        own_gain[z, x, c, 1:2, 0:rows_own] = gmlp[0:1, cols]
    s_n.start()
    run(each(AZ, s_qkv[0]) + each(AY, [s_d]))
    s_n.add_core()
    s_n.send_x()
    for s in s_qkv[2] + [s_n]:
        s.add_x()
    run(each(AZ, s_qkv[1]) + each(AY, s_qkv[0]))
    for s in s_qkv[2] + [s_n]:
        s.add_z()
    for s in s_qkv[1] + s_qkv[2] + [s_n]:
        s.add_y()
    for s in scatters + gathers:
        s.sent()
    x_far.wait_send()
    cot_far.wait_send()
    block_far.wait()
    block_near.wait()
    gplots_far.wait()
    gplots_near.wait()


def body_plot(plots, plot_grid, query_weight, key_weight, value_weight, out_weight, gate_weight, up_weight, down_weight,
              gain_attn, gain_mlp, cotangent):
    rows, d = query_weight.shape
    ff = gate_weight.shape[1]
    rows_down = down_weight.shape[0]
    half = plots.shape[1]
    slots = 2 * half
    counts = plot_grid[:, 0] * plot_grid[:, 1]
    count = lax.dynamic_slice(counts, (lax.axis_index("narrow"),), (1,))
    vm = lambda shape, dtype=BF16: pltpu.VMEM(shape, dtype)
    weights = [(4, 2, 2) + w.shape for w in (query_weight, key_weight, value_weight, out_weight, gate_weight, up_weight,
                                             down_weight)]
    sums = [(rows, d)] * 4 + [(rows, ff)] * 2 + [(rows_down, d), (8, 128)]
    any_spec, vmem_spec = pl.BlockSpec(memory_space=pl.ANY), pl.BlockSpec(memory_space=pltpu.VMEM)
    big = lambda dtype=BF16: pltpu.VMEM((slots, d), dtype)
    stage = {"g": (rows, ff), "u": (rows, ff), "d": (rows_down, d), "q": (rows, d), "k": (rows, d), "v": (rows, d),
             "o": (rows, d), "n": (8, 128)}
    stages = lambda names, lead: [vm(lead + stage[n], F32 if n == "n" else BF16) for n in names]
    dma = pltpu.SemaphoreType.DMA
    groups = 2 * CHUNKS + 2 + 9 + 1
    results = pl.pallas_call(
        layer,
        out_shape=[jax.ShapeDtypeStruct(plots.shape, BF16)] * 2 + [jax.ShapeDtypeStruct(shape, F32) for shape in sums]
        + [jax.ShapeDtypeStruct((slots, d), BF16)] * 3 + [jax.ShapeDtypeStruct((slots, d), F32)],
        in_specs=[pl.BlockSpec(memory_space=pltpu.SMEM)] + [any_spec] * 2 + [vmem_spec] * 9,
        out_specs=[any_spec] * 2 + [vmem_spec] * 8 + [any_spec] * 4,
        scratch_shapes=[vm(shape) for shape in weights]
        + [big() for _ in range(6)] + [big(F32), big(F32), big(), vm((d, slots)), big(), vm((ff // CHUNKS, slots))]
        + [vm((128, slots), F32), vm((128, slots), F32), vm((2, d), F32), vm((1, d), F32), vm((1, d), F32)]
        + [vm((4, slots, 128)), vm((2, slots, 128)), vm((2, slots, 128)), vm((2, slots, 128)), vm((2, 128, slots)),
           vm((128, slots), F32), vm((4, 2, 2, 8, 128), F32), vm((4, 2, 2, 8, 128), F32)]
        + stages("gudon", (4, 2)) + stages("gudqkvon", (4,)) + stages("gudqkvon", (3,)) + stages("gudqkvon", ())
        + [dma((8, 48)), dma((8, 32)), dma((6,)), dma((4,)), dma((groups, 6)), dma((groups, 6)), dma((4,)), dma((6,))],
        compiler_params=pltpu.CompilerParams(vmem_limit_bytes=VMEM_BYTES, collective_id=1, has_side_effects=True),
    )(count, plots, cotangent, gain_attn.reshape(1, -1), gain_mlp.reshape(1, -1), query_weight, key_weight, value_weight,
      out_weight, gate_weight, up_weight, down_weight)
    return (*results[:9], results[9][0, :rows], results[9][1, :rows])


def body_for(mesh):
    plots_fit = mesh.shape["narrow"] == 2 and mesh.shape["wide"] == 16

    def body(plots, *rest):
        if plots_fit and plots.shape == (2, 512, HEADS * HEAD_DIM):
            return body_plot(plots, *rest)
        return body_general(plots, *rest)

    return body


def solution(mesh):
    return jax.shard_map(
        body_for(mesh),
        mesh=mesh,
        in_specs=(
            P("wide", "narrow", None),
            P("wide", None),
            P("wide", None),
            P("wide", None),
            P("wide", None),
            P("wide", None),
            P("wide", None),
            P("wide", None),
            P("wide", None),
            P("wide"),
            P("wide"),
            P("wide", "narrow", None),
        ),
        out_specs=(
            P("wide", "narrow", None),
            P("wide", "narrow", None),
            P("wide", None),
            P("wide", None),
            P("wide", None),
            P("wide", None),
            P("wide", None),
            P("wide", None),
            P("wide", None),
            P("wide"),
            P("wide"),
        ),
        check_vma=False,
    )
```
